128 devices in a mesh: row: 4 (over z), col: 16 (over x, y), gz: 2 (over core).
Axes of the slice: x: 4, y: 4, z: 4, core: 2. Of those that a mesh axis runs over, the one named last changes fastest.
Arguments:
- rhs_half: float32 [2, 3, 64, 4096], P('gz', None, None, ('row', 'col')), may hold values from -6 to 6
- rhs_root: float32 [64, 4096], P(None, ('row', 'col')), may hold values from -6 to 6
- lower_coupling: bfloat16 [2, 5, 4096, 4096], P('gz', None, 'col', 'row'), may hold values from -0.046875 to 0.046875
- lower_pattern: int32 [2, 5, 32, 32], P('gz', None, 'col', 'row'), may hold values 0 or 1
- upper_coupling: bfloat16 [2, 5, 4096, 4096], P('gz', None, 'col', 'row'), may hold values from -0.046875 to 0.046875
- upper_pattern: int32 [2, 5, 32, 32], P('gz', None, 'col', 'row'), may hold values 0 or 1
- lower_inverse: bfloat16 [2, 3, 4096, 4096], P('gz', None, 'col', 'row'), may hold values from -0.09375 to 0.09375
- upper_inverse: bfloat16 [2, 3, 4096, 4096], P('gz', None, 'col', 'row'), may hold values from -0.09375 to 0.09375
- root_lower_inverse: bfloat16 [4096, 4096], P('col', 'row'), may hold values from -0.09375 to 0.09375
- root_upper_inverse: bfloat16 [4096, 4096], P('col', 'row'), may hold values from -0.09375 to 0.09375
Outputs:
- sol_half: float32 [2, 3, 64, 4096], P('gz', None, None, ('row', 'col'))
- sol_root: float32 [64, 4096], P(None, ('row', 'col'))
The draws below stay inside these ranges and needn't reach their ends.
All inputs are finite; a program needn't handle non-finite values. No bound on the sum of `lower_pattern` or of `upper_pattern` on one device may be relied on, other than what follows from the above.
Results may differ from the reference program's by a relative error of at most 0.007.
Values may be sent and summed in bfloat16 or wider, within the bound.
A program may use at most 64 MiB of HBM per device.

```python
import jax
import jax.numpy as jnp

NRHS = 64
BLK = 128
SEPW = 4096
BLOCKS = 32


def place_ends(values, stream_key, low, top_value):
    dims = values.shape
    place = [jax.random.randint(jax.random.fold_in(stream_key, axis), (), 0, dims[axis]) for axis in range(len(dims))]
    values = values.at[tuple(place)].set(low)
    longest = dims.index(max(dims))
    place[longest] = (place[longest] + 1) % dims[longest]
    return values.at[tuple(place)].set(top_value)


def block_scale(own_key, dims, cuts, low, largest):
    loudness = 1.0
    for dim, shards_of in cuts:
        draws = jax.random.uniform(jax.random.fold_in(jax.random.fold_in(own_key, 6), dim), (shards_of,), jnp.float32, low / len(cuts), largest / len(cuts))
        loudness = loudness * jnp.repeat(jnp.exp(draws), dims[dim] // shards_of).reshape((-1,) + (1,) * (len(dims) - 1 - dim))
    return loudness


def bell_draw(rng, dims, spread, most, shards=(), held_as=jnp.bfloat16):
    gain = block_scale(rng, dims, shards, -0.22, 0.18) if shards else 1.0
    entries = jax.random.normal(rng, dims, jnp.float32) * spread * gain
    return jnp.minimum(jnp.maximum(entries, -most), most).astype(held_as)


def setup_inputs(seed: int = 0) -> dict:
    keys = jax.random.split(jax.random.key(seed), 11)
    rhs_half = bell_draw(keys[0], (2, 3, NRHS, SEPW), 1.0, 6.0, ((0, 2), (3, 64)), jnp.float32)
    rhs_root = bell_draw(keys[1], (NRHS, SEPW), 1.0, 6.0, ((1, 64),), jnp.float32)
    lower_coupling = bell_draw(keys[2], (2, 5, SEPW, SEPW), (4 * SEPW) ** -0.5, 0.046875, ((0, 2), (2, 16), (3, 4)))
    lower_pattern = place_ends((jax.random.randint(keys[3], (2, 5, BLOCKS, BLOCKS), 0, 2) < 1).astype(jnp.int32), jax.random.fold_in(keys[3], 1), 0, 1)
    upper_coupling = bell_draw(keys[4], (2, 5, SEPW, SEPW), (4 * SEPW) ** -0.5, 0.046875, ((0, 2), (2, 16), (3, 4)))
    upper_pattern = place_ends((jax.random.randint(keys[5], (2, 5, BLOCKS, BLOCKS), 0, 2) < 1).astype(jnp.int32), jax.random.fold_in(keys[5], 1), 0, 1)
    lower_inverse = bell_draw(keys[6], (2, 3, SEPW, SEPW), SEPW ** -0.5, 0.09375, ((0, 2), (2, 16), (3, 4)))
    upper_inverse = bell_draw(keys[7], (2, 3, SEPW, SEPW), SEPW ** -0.5, 0.09375, ((0, 2), (2, 16), (3, 4)))
    root_lower_inverse = bell_draw(keys[8], (SEPW, SEPW), SEPW ** -0.5, 0.09375, ((0, 16), (1, 4)))
    root_upper_inverse = bell_draw(keys[9], (SEPW, SEPW), SEPW ** -0.5, 0.09375, ((0, 16), (1, 4)))
    return {"rhs_half": rhs_half, "rhs_root": rhs_root, "lower_coupling": lower_coupling, "lower_pattern": lower_pattern, "upper_coupling": upper_coupling, "upper_pattern": upper_pattern, "lower_inverse": lower_inverse, "upper_inverse": upper_inverse, "root_lower_inverse": root_lower_inverse, "root_upper_inverse": root_upper_inverse}


couplings = ((0, 1), (0, 2), (-1, 0), (-1, 1), (-1, 2))


def masked(coupling, pattern):
    tiles = coupling.reshape(pattern.shape[0], BLK, pattern.shape[1], BLK)
    tiles = tiles * pattern[:, None, :, None].astype(jnp.bfloat16)
    return tiles.reshape(coupling.shape)


def product(vector, matrix):
    return jnp.dot(vector.astype(jnp.bfloat16), matrix, preferred_element_type=jnp.float32)


def reference(rhs_half, rhs_root, lower_coupling, lower_pattern, upper_coupling, upper_pattern,
              lower_inverse, upper_inverse, root_lower_inverse, root_upper_inverse):
    forward = []
    root_update = jnp.zeros((NRHS, SEPW), jnp.float32)
    for halfside in range(2):
        solved = {}
        for target in (1, 2):
            solved[target] = product(rhs_half[halfside, target], lower_inverse[halfside, target])
        update = jnp.zeros((NRHS, SEPW), jnp.float32)
        for number, pair in enumerate(couplings):
            if pair[0] == 0:
                update = update + product(solved[pair[1]], masked(lower_coupling[halfside, number], lower_pattern[halfside, number]))
        solved[0] = product(rhs_half[halfside, 0] - update, lower_inverse[halfside, 0])
        for number, pair in enumerate(couplings):
            if pair[0] < 0:
                root_update = root_update + product(solved[pair[1]], masked(lower_coupling[halfside, number], lower_pattern[halfside, number]))
        forward.append(solved)
    root_forward = product(rhs_root - root_update, root_lower_inverse)
    sol_root = product(root_forward, root_upper_inverse)
    results = []
    for halfside in range(2):
        backward = {-1: sol_root}
        for target in range(3):
            update = jnp.zeros((NRHS, SEPW), jnp.float32)
            for number, pair in enumerate(couplings):
                if pair[1] == target:
                    update = update + product(backward[pair[0]], masked(upper_coupling[halfside, number], upper_pattern[halfside, number]))
            backward[target] = product(forward[halfside][target] - update, upper_inverse[halfside, target])
        results.append(jnp.stack([backward[target] for target in range(3)]))
    return jnp.stack(results), sol_root
```

```python
import jax
import jax.numpy as jnp
from jax import lax
from jax.experimental import pallas as pl
from jax.experimental.pallas import tpu as pltpu
from jax.sharding import PartitionSpec as P

MESH = pl.DeviceIdType.MESH
F32 = jnp.float32
BF16 = jnp.bfloat16

NEAR = sorted(
    ((dx, dy) for dx in range(4) for dy in range(4) if dx or dy),
    key=lambda d: -(min(d[0], 4 - d[0]) + min(d[1], 4 - d[1])),
)


def dot(vector, tiles):
    return jnp.dot(vector, tiles, preferred_element_type=F32)


def add_up(ref, count):
    total = ref[0].astype(F32)
    for i in range(1, count):
        total = total + ref[i].astype(F32)
    return total


def kernel(
    rhs_half,
    rhs_root,
    lower_pattern,
    upper_pattern,
    lower_hbm,
    upper_hbm,
    lower_inverse_hbm,
    upper_inverse_hbm,
    root_lower_hbm,
    root_upper_hbm,
    sol_half,
    sol_root,
    lower,
    upper,
    lower_inverse,
    upper_inverse,
    root_lower,
    root_upper,
    leaf_pack,
    leaf_recv,
    bias_pack,
    bias_recv,
    send1,
    send2,
    send3,
    send4,
    send5,
    send6,
    send7,
    send8,
    send9,
    send10,
    recv1,
    recv2,
    recv3,
    recv4,
    recv5,
    recv6,
    recv7,
    recv8,
    recv9,
    recv10,
    part1,
    part2,
    part3,
    part4,
    part5,
    part6,
    part7,
    part8,
    part9,
    vec1,
    vec2,
    vec3,
    vec4,
    vec5,
    vec6,
    vec7,
    vec8,
    vec9,
    leaf_value,
    top_value,
    root_early,
    second_early,
    root_out,
    root_out_recv,
    first_out,
    first_out_recv,
    weight_sem,
    scatter_send,
    scatter_recv,
    spread_send,
    spread_recv,
    spread_self,
    misc_send,
    misc_recv,
    misc_self,
):
    z = lax.axis_index("row")
    col = lax.axis_index("col")
    core = lax.axis_index("gz")
    x = col // 4
    y = col % 4
    other = 1 - core

    def start_local(src, dst, sem):
        pltpu.make_async_copy(src, dst, sem).start()

    def wait_for(ref, sem):
        pltpu.make_async_copy(ref, ref, sem).wait()

    def send(src, dst, send_sem, recv_sem, device):
        pltpu.make_async_remote_copy(
            src_ref=src,
            dst_ref=dst,
            send_sem=send_sem,
            recv_sem=recv_sem,
            device_id=device,
            device_id_type=MESH,
        ).start()

    def send_or_keep(here, src, dst, send_sem, recv_sem, device):
        @pl.when(jnp.logical_not(here))
        def _():
            send(src, dst, send_sem, recv_sem, device)

        @pl.when(here)
        def _():
            start_local(src, dst, recv_sem)

    def wait_sent_unless(here, ref, sem):
        @pl.when(jnp.logical_not(here))
        def _():
            wait_for(ref, sem)

    start_local(lower_inverse_hbm, lower_inverse, weight_sem.at[0])
    start_local(lower_hbm, lower, weight_sem.at[1])
    for j in range(4):
        columns = pl.ds(pl.multiple_of(256 * j + 128 * core, 128), 128)
        start_local(
            root_lower_hbm.at[:, columns], root_lower.at[:, pl.ds(128 * j, 128)], weight_sem.at[2]
        )
    for j in range(4):
        columns = pl.ds(pl.multiple_of(256 * j + 128 * core, 128), 128)
        start_local(
            root_upper_hbm.at[:, columns], root_upper.at[:, pl.ds(128 * j, 128)], weight_sem.at[3]
        )
    start_local(upper_hbm, upper, weight_sem.at[4])
    start_local(upper_inverse_hbm, upper_inverse, weight_sem.at[5])

    barrier = pltpu.get_barrier_semaphore()

    def greet(px, py, pz, pcore):
        pl.semaphore_signal(
            barrier, inc=1, device_id=(pz, 4 * px + py, pcore), device_id_type=MESH
        )

    @pl.when(x != z)
    def _():
        for u in range(4):
            greet(y, u, x, core)
            greet(u, y, x, core)
            greet(u, y, x, other)

    for dx, dy in NEAR:
        greet((x + dx) % 4, (y + dy) % 4, z, core)
        greet((x + dx) % 4, (y + dy) % 4, z, other)
    greet(x, y, z, other)

    leaf_pack[...] = jnp.concatenate([rhs_half[1], rhs_half[2]], axis=1).astype(BF16)
    bias_pack[...] = jnp.concatenate([rhs_half[0], rhs_root[...]], axis=1)
    pl.semaphore_wait(barrier, 31 + 9)

    leaf_here = jnp.logical_and(x == z, x == y)
    for dz in (2, 1, 3):
        send(
            leaf_pack,
            leaf_recv.at[y],
            misc_send.at[0],
            misc_recv.at[0],
            ((z + dz) % 4, 4 * z + x, core),
        )
    send_or_keep(
        leaf_here, leaf_pack, leaf_recv.at[y], misc_self.at[0], misc_recv.at[0], (z, 4 * z + x, core)
    )
    bias_here = x == y
    for dq in (2, 1, 3):
        q = (x + dq) % 4
        send(
            bias_pack.at[pl.ds(pl.multiple_of(16 * q, 16), 16)],
            bias_recv.at[y],
            misc_send.at[1],
            misc_recv.at[1],
            (z, 4 * q + x, core),
        )
    own_rows = pl.ds(pl.multiple_of(16 * x, 16), 16)
    send_or_keep(
        bias_here,
        bias_pack.at[own_rows],
        bias_recv.at[y],
        misc_self.at[1],
        misc_recv.at[1],
        (z, 4 * x + x, core),
    )

    def scatter(src, dst, stage):
        for dx, dy in NEAR:
            peer = 4 * ((x + dx) % 4) + (y + dy) % 4
            send(
                src.at[peer],
                dst.at[col],
                scatter_send.at[stage],
                scatter_recv.at[stage],
                (z, peer, core),
            )
        start_local(src.at[col], dst.at[col], scatter_recv.at[stage])

    def spread(src, dst, stage):
        for dz in (2, 1, 3):
            send(
                src,
                dst.at[x],
                spread_send.at[stage],
                spread_recv.at[stage],
                ((z + dz) % 4, 4 * z + y, core),
            )
        send_or_keep(
            x == z,
            src,
            dst.at[x],
            spread_self.at[stage],
            spread_recv.at[stage],
            (z, 4 * z + y, core),
        )

    def spread_both(src, dst, stage):
        for dz in (2, 1, 3):
            for to in (other, core):
                send(
                    src,
                    dst.at[core, x],
                    spread_send.at[stage],
                    spread_recv.at[stage],
                    ((z + dz) % 4, 4 * z + y, to),
                )
        send(
            src,
            dst.at[core, x],
            spread_send.at[stage],
            spread_recv.at[stage],
            (z, 4 * z + y, other),
        )
        send_or_keep(
            x == z,
            src,
            dst.at[core, x],
            spread_self.at[stage],
            spread_recv.at[stage],
            (z, 4 * z + y, core),
        )

    def mask(tiles, pattern):
        @pl.loop(0, 5)
        def _(p):
            for a in range(2):
                for b in range(8):
                    here = (p, pl.ds(128 * a, 128), pl.ds(128 * b, 128))
                    keep = jnp.full((128, 128), pattern[p, a, b].astype(F32), F32)
                    tiles[here] = tiles[here] * keep.astype(BF16)

    def block(ref, j):
        return ref[:, 256 * j : 256 * j + 256]

    def chunks(ref, j, value):
        for q in range(4):
            ref[4 * q + j] = value[16 * q : 16 * q + 16].astype(BF16)

    wait_for(lower, weight_sem.at[1])
    mask(lower, lower_pattern)

    wait_for(leaf_recv, misc_recv.at[0])
    wait_for(lower_inverse, weight_sem.at[0])
    pieces = [leaf_recv[u].astype(F32) for u in range(4)]
    for s in range(2):
        leaf = jnp.concatenate([p[:, 64 * s : 64 * s + 64] for p in pieces], axis=1).astype(BF16)
        for j in range(4):
            value = dot(leaf, block(lower_inverse.at[1 + s], j))
            for q in range(4):
                send1[4 * q + j, s] = value[16 * q : 16 * q + 16].astype(BF16)
    scatter(send1, recv1, 0)
    wait_for(recv1, scatter_recv.at[0])
    leaf_value[...] = add_up(recv1, 16)
    part1[...] = leaf_value[...].astype(BF16)
    spread(part1, vec1, 0)

    wait_for(vec1, spread_recv.at[0])
    leaf1 = vec1[:, 0].reshape(64, 256)
    leaf2 = vec1[:, 1].reshape(64, 256)
    for j in range(4):
        chunks(send2, j, dot(leaf1, block(lower.at[0], j)) + dot(leaf2, block(lower.at[1], j)))
    scatter(send2, recv2, 1)
    for j in range(4):
        root_early[:, 256 * j : 256 * j + 256] = dot(leaf1, block(lower.at[3], j)) + dot(
            leaf2, block(lower.at[4], j)
        )
    wait_for(bias_recv, misc_recv.at[1])
    top_bias = jnp.concatenate([bias_recv[u][:, 0:64] for u in range(4)], axis=1)
    wait_for(recv2, scatter_recv.at[1])
    part2[...] = (top_bias - add_up(recv2, 16)).astype(BF16)
    spread(part2, vec2, 1)

    wait_for(vec2, spread_recv.at[1])
    vector = vec2[...].reshape(64, 256)
    for j in range(4):
        chunks(send3, j, dot(vector, block(lower_inverse.at[0], j)))
    scatter(send3, recv3, 2)
    wait_for(recv3, scatter_recv.at[2])
    top_value[...] = add_up(recv3, 16)
    part3[...] = top_value[...].astype(BF16)
    spread(part3, vec3, 2)

    wait_for(vec3, spread_recv.at[2])
    vector = vec3[...].reshape(64, 256)
    for j in range(4):
        value = root_early[:, 256 * j : 256 * j + 256] + dot(vector, block(lower.at[2], j))
        for half in range(2):
            for q in range(4):
                send4[half, 4 * q + j] = value[
                    16 * q : 16 * q + 16, 128 * half : 128 * half + 128
                ].astype(BF16)
    for dx, dy in NEAR:
        peer = 4 * ((x + dx) % 4) + (y + dy) % 4
        for to in (other, core):
            send(
                send4.at[to, peer],
                recv4.at[core, col],
                scatter_send.at[3],
                scatter_recv.at[3],
                (z, peer, to),
            )
    send(
        send4.at[other, col],
        recv4.at[core, col],
        scatter_send.at[3],
        scatter_recv.at[3],
        (z, col, other),
    )
    start_local(send4.at[core, col], recv4.at[core, col], scatter_recv.at[3])
    root_bias = jnp.concatenate(
        [bias_recv[2 * core][:, 64:128], bias_recv[2 * core + 1][:, 64:128]], axis=1
    )
    wait_for(upper, weight_sem.at[4])
    mask(upper, upper_pattern)
    wait_for(recv4, scatter_recv.at[3])
    part4[...] = (root_bias - add_up(recv4.at[0], 16) - add_up(recv4.at[1], 16)).astype(BF16)
    spread_both(part4, vec4, 3)

    def whole(ref):
        return jnp.concatenate([ref[0].reshape(64, 128), ref[1].reshape(64, 128)], axis=1)

    def halves(ref, vector, tiles):
        for pair in range(2):
            value = dot(vector, tiles[:, 256 * pair : 256 * pair + 256])
            for k in range(2):
                for q in range(4):
                    ref[4 * q + 2 * pair + k] = value[
                        16 * q : 16 * q + 16, 128 * k : 128 * k + 128
                    ].astype(BF16)

    wait_for(root_lower, weight_sem.at[2])
    wait_for(vec4, spread_recv.at[3])
    halves(send5, whole(vec4), root_lower)
    scatter(send5, recv5, 4)
    wait_for(recv5, scatter_recv.at[4])
    part5[...] = add_up(recv5, 16).astype(BF16)
    spread_both(part5, vec5, 4)
    wait_for(root_upper, weight_sem.at[3])
    wait_for(vec5, spread_recv.at[4])
    halves(send6, whole(vec5), root_upper)
    scatter(send6, recv6, 5)
    wait_for(recv6, scatter_recv.at[5])
    root_out[...] = add_up(recv6, 16)
    part6[...] = root_out[...].astype(BF16)
    spread_both(part6, vec6, 5)

    def out_here(k, to):
        return jnp.logical_and(jnp.logical_and(x == y, 2 * core + k == y), to == core)

    for k in range(2):
        owner = 4 * y + 2 * core + k
        send(root_out, root_out_recv.at[x], misc_send.at[2], misc_recv.at[2], (z, owner, other))
        send_or_keep(
            out_here(k, core),
            root_out,
            root_out_recv.at[x],
            misc_self.at[2 + k],
            misc_recv.at[2],
            (z, owner, core),
        )

    wait_for(vec6, spread_recv.at[5])
    vector = whole(vec6)
    for j in range(4):
        chunks(send7, j, dot(vector, block(upper.at[2], j)))
    scatter(send7, recv7, 6)
    for s in range(2):
        for j in range(4):
            second_early[s, :, 256 * j : 256 * j + 256] = dot(vector, block(upper.at[3 + s], j))
    wait_for(recv7, scatter_recv.at[6])
    part7[...] = (top_value[...] - add_up(recv7, 16)).astype(BF16)
    spread(part7, vec7, 6)

    wait_for(upper_inverse, weight_sem.at[5])
    wait_for(vec7, spread_recv.at[6])
    vector = vec7[...].reshape(64, 256)
    for j in range(4):
        chunks(send8, j, dot(vector, block(upper_inverse.at[0], j)))
    scatter(send8, recv8, 7)
    wait_for(recv8, scatter_recv.at[7])
    first = add_up(recv8, 16)
    part8[...] = first.astype(BF16)
    spread(part8, vec8, 7)
    first_out[0] = first[:, 0:128]
    first_out[1] = first[:, 128:256]
    first_here = x == y
    for du in (2, 1, 3):
        u = (y + du) % 4
        send(
            first_out.at[u // 2],
            first_out_recv.at[x],
            misc_send.at[3],
            misc_recv.at[3],
            (z, 4 * y + u, core),
        )
    send_or_keep(
        first_here,
        first_out.at[y // 2],
        first_out_recv.at[x],
        misc_self.at[4],
        misc_recv.at[3],
        (z, 4 * y + y, core),
    )

    wait_for(vec8, spread_recv.at[7])
    vector = vec8[...].reshape(64, 256)
    for s in range(2):
        for j in range(4):
            value = second_early[s, :, 256 * j : 256 * j + 256] + dot(
                vector, block(upper.at[s], j)
            )
            for q in range(4):
                send9[4 * q + j, s] = value[16 * q : 16 * q + 16].astype(BF16)
    scatter(send9, recv9, 8)

    odd = y % 2 == 1
    wait_for(root_out_recv, misc_recv.at[2])
    value = root_out_recv[...].reshape(64, 128)
    sol_root[...] = jnp.where(odd, value[:, 64:128], value[:, 0:64])
    wait_for(first_out_recv, misc_recv.at[3])
    value = first_out_recv[...].reshape(64, 128)
    sol_half[0] = jnp.where(odd, value[:, 64:128], value[:, 0:64])

    wait_for(recv9, scatter_recv.at[8])
    part9[...] = (leaf_value[...] - add_up(recv9, 16)).astype(BF16)
    spread(part9, vec9, 8)

    wait_for(vec9, spread_recv.at[8])
    second1 = vec9[:, 0].reshape(64, 256)
    second2 = vec9[:, 1].reshape(64, 256)
    for j in range(4):
        value1 = dot(second1, block(upper_inverse.at[1], j))
        value2 = dot(second2, block(upper_inverse.at[2], j))
        for u in range(4):
            span = slice(64 * u, 64 * u + 64)
            send10[4 * j + u] = jnp.concatenate([value1[:, span], value2[:, span]], axis=1).astype(
                BF16
            )
    scatter(send10, recv10, 9)
    wait_for(recv10, scatter_recv.at[9])
    total = add_up(recv10, 16)
    sol_half[1] = total[:, 0:64]
    sol_half[2] = total[:, 64:128]

    sends = (send1, send2, send3, None, send5, send6, send7, send8, send9, send10)
    for stage, ref in enumerate(sends):
        if ref is not None:
            wait_for(ref.at[pl.ds(0, 15)], scatter_send.at[stage])
    wait_for(recv4.at[0], scatter_send.at[3])
    wait_for(recv4.at[1, pl.ds(0, 15)], scatter_send.at[3])
    for stage, ref in enumerate((vec1, vec2, vec3, None, None, None, vec7, vec8, vec9)):
        if ref is not None:
            wait_for(ref.at[pl.ds(0, 3)], spread_send.at[stage])
            wait_sent_unless(x == z, ref.at[0], spread_self.at[stage])
    for stage, ref in ((3, vec4), (4, vec5), (5, vec6)):
        wait_for(ref.at[0], spread_send.at[stage])
        wait_for(ref.at[1, pl.ds(0, 3)], spread_send.at[stage])
        wait_sent_unless(x == z, ref.at[0, 0], spread_self.at[stage])
    wait_for(leaf_recv.at[pl.ds(0, 3)], misc_send.at[0])
    wait_sent_unless(leaf_here, leaf_recv.at[0], misc_self.at[0])
    wait_for(bias_recv.at[pl.ds(0, 3)], misc_send.at[1])
    wait_sent_unless(bias_here, bias_recv.at[0], misc_self.at[1])
    wait_for(root_out_recv.at[pl.ds(0, 2)], misc_send.at[2])
    for k in range(2):
        wait_sent_unless(out_here(k, core), root_out_recv.at[0], misc_self.at[2 + k])
    wait_for(first_out_recv.at[pl.ds(0, 3)], misc_send.at[3])
    wait_sent_unless(first_here, first_out_recv.at[0], misc_self.at[4])


def per_device(
    rhs_half,
    rhs_root,
    lower_coupling,
    lower_pattern,
    upper_coupling,
    upper_pattern,
    lower_inverse,
    upper_inverse,
    root_lower_inverse,
    root_upper_inverse,
):
    vmem = pl.BlockSpec(memory_space=pltpu.VMEM)
    smem = pl.BlockSpec(memory_space=pltpu.SMEM)
    hbm = pl.BlockSpec(memory_space=pl.ANY)
    one = (16, 256)
    two = (2, 16, 256)
    half = (16, 128)
    stage_chunks = [two, one, one, None, half, half, one, one, two, (64, 128)]
    exchange = [
        pltpu.VMEM((2, 16) + half if chunk is None else (16,) + chunk, BF16)
        for chunk in stage_chunks
    ]
    part_chunks = [two, one, one, half, half, half, one, one, two]
    parts = [pltpu.VMEM(chunk, BF16) for chunk in part_chunks]
    vectors = [
        pltpu.VMEM((2, 4) + chunk if chunk == half else (4,) + chunk, BF16)
        for chunk in part_chunks
    ]
    scratch = [
        pltpu.VMEM((5, 256, 1024), BF16),
        pltpu.VMEM((5, 256, 1024), BF16),
        pltpu.VMEM((3, 256, 1024), BF16),
        pltpu.VMEM((3, 256, 1024), BF16),
        pltpu.VMEM((256, 512), BF16),
        pltpu.VMEM((256, 512), BF16),
        pltpu.VMEM((64, 128), BF16),
        pltpu.VMEM((4, 64, 128), BF16),
        pltpu.VMEM((64, 128), F32),
        pltpu.VMEM((4, 16, 128), F32),
        *exchange,
        *exchange,
        *parts,
        *vectors,
        pltpu.VMEM(two, F32),
        pltpu.VMEM(one, F32),
        pltpu.VMEM((64, 1024), F32),
        pltpu.VMEM((2, 64, 1024), F32),
        pltpu.VMEM(half, F32),
        pltpu.VMEM((4,) + half, F32),
        pltpu.VMEM((2,) + half, F32),
        pltpu.VMEM((4,) + half, F32),
        pltpu.SemaphoreType.DMA((6,)),
        pltpu.SemaphoreType.DMA((10,)),
        pltpu.SemaphoreType.DMA((10,)),
        pltpu.SemaphoreType.DMA((9,)),
        pltpu.SemaphoreType.DMA((9,)),
        pltpu.SemaphoreType.DMA((9,)),
        pltpu.SemaphoreType.DMA((4,)),
        pltpu.SemaphoreType.DMA((4,)),
        pltpu.SemaphoreType.DMA((5,)),
    ]
    sol_half, sol_root = pl.pallas_call(
        kernel,
        name="tree_solve",
        out_shape=(
            jax.ShapeDtypeStruct((3, 64, 64), F32),
            jax.ShapeDtypeStruct((64, 64), F32),
        ),
        in_specs=[vmem, vmem, smem, smem] + [hbm] * 6,
        out_specs=(vmem, vmem),
        scratch_shapes=scratch,
        compiler_params=pltpu.CompilerParams(collective_id=0, has_side_effects=True),
    )(
        rhs_half[0],
        rhs_root,
        lower_pattern[0],
        upper_pattern[0],
        lower_coupling[0],
        upper_coupling[0],
        lower_inverse[0],
        upper_inverse[0],
        root_lower_inverse,
        root_upper_inverse,
    )
    return (sol_half[None], sol_root)


def solution(mesh):
    in_specs = (
        P("gz", None, None, ("row", "col")),
        P(None, ("row", "col")),
        P("gz", None, "col", "row"),
        P("gz", None, "col", "row"),
        P("gz", None, "col", "row"),
        P("gz", None, "col", "row"),
        P("gz", None, "col", "row"),
        P("gz", None, "col", "row"),
        P("col", "row"),
        P("col", "row"),
    )
    out_specs = (P("gz", None, None, ("row", "col")), P(None, ("row", "col")))
    return jax.shard_map(
        per_device, mesh=mesh, in_specs=in_specs, out_specs=out_specs, check_vma=False
    )
```

```python
import jax
import jax.numpy as jnp
from jax import lax
from jax.experimental import pallas as pl
from jax.experimental.pallas import tpu as pltpu
from jax.sharding import PartitionSpec as P

MESH = pl.DeviceIdType.MESH
F32 = jnp.float32
BF16 = jnp.bfloat16

NEAR = sorted(
    ((dx, dy) for dx in range(4) for dy in range(4) if dx or dy),
    key=lambda d: -(min(d[0], 4 - d[0]) + min(d[1], 4 - d[1])),
)


def dot(vector, tiles):
    return jnp.dot(vector, tiles, preferred_element_type=F32)


def add_up(ref, count):
    total = ref[0].astype(F32)
    for i in range(1, count):
        total = total + ref[i].astype(F32)
    return total


def kernel(
    rhs_half_hbm,
    rhs_root_hbm,
    lower_pattern_hbm,
    upper_pattern_hbm,
    lower_hbm,
    upper_hbm,
    lower_inverse_hbm,
    upper_inverse_hbm,
    root_lower_hbm,
    root_upper_hbm,
    sol_half,
    sol_root,
    rhs_half,
    rhs_root,
    lower_pattern,
    upper_pattern,
    lower,
    upper,
    lower_inverse,
    upper_inverse,
    root_lower,
    root_upper,
    leaf_pack,
    leaf_recv,
    bias_pack,
    bias_recv,
    send1,
    send2,
    send3,
    send4,
    send5,
    send6,
    send7,
    send8,
    send9,
    send10,
    recv1,
    recv2,
    recv3,
    recv4,
    recv5,
    recv6,
    recv7,
    recv8,
    recv9,
    recv10,
    part1,
    part2,
    part3,
    part4,
    part5,
    part6,
    part7,
    part8,
    part9,
    vec1,
    vec2,
    vec3,
    vec4,
    vec5,
    vec6,
    vec7,
    vec8,
    vec9,
    leaf_value,
    top_value,
    root_early,
    second_early,
    root_out,
    root_out_recv,
    first_out,
    first_out_recv,
    weight_sem,
    scatter_send,
    scatter_recv,
    spread_send,
    spread_recv,
    spread_self,
    misc_send,
    misc_recv,
    misc_self,
):
    z = lax.axis_index("row")
    col = lax.axis_index("col")
    core = lax.axis_index("gz")
    x = col // 4
    y = col % 4
    other = 1 - core

    def start_local(src, dst, sem):
        pltpu.make_async_copy(src, dst, sem).start()

    def wait_for(ref, sem):
        pltpu.make_async_copy(ref, ref, sem).wait()

    def send(src, dst, send_sem, recv_sem, device):
        pltpu.make_async_remote_copy(
            src_ref=src,
            dst_ref=dst,
            send_sem=send_sem,
            recv_sem=recv_sem,
            device_id=device,
            device_id_type=MESH,
        ).start()

    def send_or_keep(here, src, dst, send_sem, recv_sem, device):
        @pl.when(jnp.logical_not(here))
        def _():
            send(src, dst, send_sem, recv_sem, device)

        @pl.when(here)
        def _():
            start_local(src, dst, recv_sem)

    def wait_sent_unless(here, ref, sem):
        @pl.when(jnp.logical_not(here))
        def _():
            wait_for(ref, sem)

    barrier = pltpu.get_barrier_semaphore()

    def greet(px, py, pz, pcore):
        pl.semaphore_signal(
            barrier, inc=1, device_id=(pz, 4 * px + py, pcore), device_id_type=MESH
        )

    @pl.when(x != z)
    def _():
        for u in range(4):
            greet(y, u, x, core)
            greet(u, y, x, core)
            greet(u, y, x, other)

    for dx, dy in NEAR:
        greet((x + dx) % 4, (y + dy) % 4, z, core)
        greet((x + dx) % 4, (y + dy) % 4, z, other)
    greet(x, y, z, other)

    start_local(rhs_half_hbm, rhs_half, weight_sem.at[6])
    start_local(rhs_root_hbm, rhs_root, weight_sem.at[7])
    start_local(lower_pattern_hbm, lower_pattern, weight_sem.at[8])
    start_local(upper_pattern_hbm, upper_pattern, weight_sem.at[9])
    start_local(lower_inverse_hbm, lower_inverse, weight_sem.at[0])
    start_local(lower_hbm, lower, weight_sem.at[1])
    for j in range(4):
        columns = pl.ds(pl.multiple_of(256 * j + 128 * core, 128), 128)
        start_local(
            root_lower_hbm.at[:, columns], root_lower.at[:, pl.ds(128 * j, 128)], weight_sem.at[2]
        )
    for j in range(4):
        columns = pl.ds(pl.multiple_of(256 * j + 128 * core, 128), 128)
        start_local(
            root_upper_hbm.at[:, columns], root_upper.at[:, pl.ds(128 * j, 128)], weight_sem.at[3]
        )
    start_local(upper_hbm, upper, weight_sem.at[4])
    start_local(upper_inverse_hbm, upper_inverse, weight_sem.at[5])

    wait_for(rhs_half, weight_sem.at[6])
    wait_for(rhs_root, weight_sem.at[7])
    leaf_pack[...] = jnp.concatenate([rhs_half[1], rhs_half[2]], axis=1).astype(BF16)
    bias_pack[...] = jnp.concatenate([rhs_half[0], rhs_root[...]], axis=1)
    pl.semaphore_wait(barrier, 31 + 9)

    leaf_here = jnp.logical_and(x == z, x == y)
    for dz in (2, 1, 3):
        send(
            leaf_pack,
            leaf_recv.at[y],
            misc_send.at[0],
            misc_recv.at[0],
            ((z + dz) % 4, 4 * z + x, core),
        )
    send_or_keep(
        leaf_here, leaf_pack, leaf_recv.at[y], misc_self.at[0], misc_recv.at[0], (z, 4 * z + x, core)
    )
    bias_here = x == y
    for dq in (2, 1, 3):
        q = (x + dq) % 4
        send(
            bias_pack.at[pl.ds(pl.multiple_of(16 * q, 16), 16)],
            bias_recv.at[y],
            misc_send.at[1],
            misc_recv.at[1],
            (z, 4 * q + x, core),
        )
    own_rows = pl.ds(pl.multiple_of(16 * x, 16), 16)
    send_or_keep(
        bias_here,
        bias_pack.at[own_rows],
        bias_recv.at[y],
        misc_self.at[1],
        misc_recv.at[1],
        (z, 4 * x + x, core),
    )

    def scatter(src, dst, stage):
        for dx, dy in NEAR:
            peer = 4 * ((x + dx) % 4) + (y + dy) % 4
            send(
                src.at[peer],
                dst.at[col],
                scatter_send.at[stage],
                scatter_recv.at[stage],
                (z, peer, core),
            )
        start_local(src.at[col], dst.at[col], scatter_recv.at[stage])

    def spread(src, dst, stage):
        for dz in (2, 1, 3):
            send(
                src,
                dst.at[x],
                spread_send.at[stage],
                spread_recv.at[stage],
                ((z + dz) % 4, 4 * z + y, core),
            )
        send_or_keep(
            x == z,
            src,
            dst.at[x],
            spread_self.at[stage],
            spread_recv.at[stage],
            (z, 4 * z + y, core),
        )

    def spread_both(src, dst, stage):
        for dz in (2, 1, 3):
            for to in (other, core):
                send(
                    src,
                    dst.at[core, x],
                    spread_send.at[stage],
                    spread_recv.at[stage],
                    ((z + dz) % 4, 4 * z + y, to),
                )
        send(
            src,
            dst.at[core, x],
            spread_send.at[stage],
            spread_recv.at[stage],
            (z, 4 * z + y, other),
        )
        send_or_keep(
            x == z,
            src,
            dst.at[core, x],
            spread_self.at[stage],
            spread_recv.at[stage],
            (z, 4 * z + y, core),
        )

    def mask(tiles, pattern):
        @pl.loop(0, 5)
        def _(p):
            for a in range(2):
                for b in range(8):
                    here = (p, pl.ds(128 * a, 128), pl.ds(128 * b, 128))
                    keep = jnp.full((128, 128), pattern[p, a, b].astype(F32), F32)
                    tiles[here] = tiles[here] * keep.astype(BF16)

    def columns_of(j):
        return pl.ds(pl.multiple_of(256 * j, 256), 256)

    def block(ref, j):
        return ref[:, columns_of(j)]

    def multiply(values_of, src, dst, stage):
        for dy in (2, 1, 3, 0):
            j = (y + dy) % 4
            values = values_of(j)
            for q in range(4):
                rows = [value[16 * q : 16 * q + 16].astype(BF16) for value in values]
                if len(rows) == 1:
                    src[4 * q + j] = rows[0]
                else:
                    for s in range(2):
                        src[4 * q + j, s] = rows[s]
            for dx in (2, 1, 3, 0):
                peer = 4 * ((x + dx) % 4) + j
                if dx or dy:
                    send(
                        src.at[peer],
                        dst.at[col],
                        scatter_send.at[stage],
                        scatter_recv.at[stage],
                        (z, peer, core),
                    )
                else:
                    start_local(src.at[peer], dst.at[col], scatter_recv.at[stage])

    wait_for(lower, weight_sem.at[1])
    wait_for(lower_pattern, weight_sem.at[8])
    mask(lower, lower_pattern)

    wait_for(leaf_recv, misc_recv.at[0])
    wait_for(lower_inverse, weight_sem.at[0])
    pieces = [leaf_recv[u].astype(F32) for u in range(4)]
    leaves = [
        jnp.concatenate([p[:, 64 * s : 64 * s + 64] for p in pieces], axis=1).astype(BF16)
        for s in range(2)
    ]
    multiply(
        lambda j: [dot(leaves[s], block(lower_inverse.at[1 + s], j)) for s in range(2)],
        send1,
        recv1,
        0,
    )
    wait_for(recv1, scatter_recv.at[0])
    leaf_value[...] = add_up(recv1, 16)
    part1[...] = leaf_value[...].astype(BF16)
    spread(part1, vec1, 0)

    wait_for(vec1, spread_recv.at[0])
    leaf1 = vec1[:, 0].reshape(64, 256)
    leaf2 = vec1[:, 1].reshape(64, 256)
    multiply(
        lambda j: [dot(leaf1, block(lower.at[0], j)) + dot(leaf2, block(lower.at[1], j))],
        send2,
        recv2,
        1,
    )
    for j in range(4):
        root_early[:, 256 * j : 256 * j + 256] = dot(leaf1, block(lower.at[3], j)) + dot(
            leaf2, block(lower.at[4], j)
        )
    wait_for(bias_recv, misc_recv.at[1])
    top_bias = jnp.concatenate([bias_recv[u][:, 0:64] for u in range(4)], axis=1)
    wait_for(recv2, scatter_recv.at[1])
    part2[...] = (top_bias - add_up(recv2, 16)).astype(BF16)
    spread(part2, vec2, 1)

    wait_for(vec2, spread_recv.at[1])
    vector = vec2[...].reshape(64, 256)
    vector3 = vector
    multiply(lambda j: [dot(vector3, block(lower_inverse.at[0], j))], send3, recv3, 2)
    wait_for(recv3, scatter_recv.at[2])
    top_value[...] = add_up(recv3, 16)
    part3[...] = top_value[...].astype(BF16)
    spread(part3, vec3, 2)

    wait_for(vec3, spread_recv.at[2])
    vector = vec3[...].reshape(64, 256)
    for dy in (2, 1, 3, 0):
        j = (y + dy) % 4
        value = root_early[:, columns_of(j)] + dot(vector, block(lower.at[2], j))
        for half in range(2):
            for q in range(4):
                send4[half, 4 * q + j] = value[
                    16 * q : 16 * q + 16, 128 * half : 128 * half + 128
                ].astype(BF16)
        for dx in (2, 1, 3, 0):
            peer = 4 * ((x + dx) % 4) + j
            for to in (other, core):
                if dx or dy or to is other:
                    send(
                        send4.at[to, peer],
                        recv4.at[core, col],
                        scatter_send.at[3],
                        scatter_recv.at[3],
                        (z, peer, to),
                    )
                else:
                    start_local(send4.at[to, peer], recv4.at[core, col], scatter_recv.at[3])
    root_bias = jnp.concatenate(
        [bias_recv[2 * core][:, 64:128], bias_recv[2 * core + 1][:, 64:128]], axis=1
    )
    wait_for(upper, weight_sem.at[4])
    wait_for(upper_pattern, weight_sem.at[9])
    mask(upper, upper_pattern)
    wait_for(recv4, scatter_recv.at[3])
    part4[...] = (root_bias - add_up(recv4.at[0], 16) - add_up(recv4.at[1], 16)).astype(BF16)
    spread_both(part4, vec4, 3)

    def whole(ref):
        return jnp.concatenate([ref[0].reshape(64, 128), ref[1].reshape(64, 128)], axis=1)

    def halves(ref, vector, tiles):
        for pair in range(2):
            value = dot(vector, tiles[:, 256 * pair : 256 * pair + 256])
            for k in range(2):
                for q in range(4):
                    ref[4 * q + 2 * pair + k] = value[
                        16 * q : 16 * q + 16, 128 * k : 128 * k + 128
                    ].astype(BF16)

    wait_for(root_lower, weight_sem.at[2])
    wait_for(vec4, spread_recv.at[3])
    halves(send5, whole(vec4), root_lower)
    scatter(send5, recv5, 4)
    wait_for(recv5, scatter_recv.at[4])
    part5[...] = add_up(recv5, 16).astype(BF16)
    spread_both(part5, vec5, 4)
    wait_for(root_upper, weight_sem.at[3])
    wait_for(vec5, spread_recv.at[4])
    halves(send6, whole(vec5), root_upper)
    scatter(send6, recv6, 5)
    wait_for(recv6, scatter_recv.at[5])
    root_out[...] = add_up(recv6, 16)
    part6[...] = root_out[...].astype(BF16)
    spread_both(part6, vec6, 5)

    def out_here(k, to):
        return jnp.logical_and(jnp.logical_and(x == y, 2 * core + k == y), to == core)

    for k in range(2):
        owner = 4 * y + 2 * core + k
        send(root_out, root_out_recv.at[x], misc_send.at[2], misc_recv.at[2], (z, owner, other))
        send_or_keep(
            out_here(k, core),
            root_out,
            root_out_recv.at[x],
            misc_self.at[2 + k],
            misc_recv.at[2],
            (z, owner, core),
        )

    wait_for(vec6, spread_recv.at[5])
    vector = whole(vec6)
    vector7 = vector
    multiply(lambda j: [dot(vector7, block(upper.at[2], j))], send7, recv7, 6)
    for s in range(2):
        for j in range(4):
            second_early[s, :, 256 * j : 256 * j + 256] = dot(vector, block(upper.at[3 + s], j))
    wait_for(recv7, scatter_recv.at[6])
    part7[...] = (top_value[...] - add_up(recv7, 16)).astype(BF16)
    spread(part7, vec7, 6)

    wait_for(upper_inverse, weight_sem.at[5])
    wait_for(vec7, spread_recv.at[6])
    vector = vec7[...].reshape(64, 256)
    vector8 = vector
    multiply(lambda j: [dot(vector8, block(upper_inverse.at[0], j))], send8, recv8, 7)
    wait_for(recv8, scatter_recv.at[7])
    first = add_up(recv8, 16)
    part8[...] = first.astype(BF16)
    spread(part8, vec8, 7)
    first_out[0] = first[:, 0:128]
    first_out[1] = first[:, 128:256]
    first_here = x == y
    for du in (2, 1, 3):
        u = (y + du) % 4
        send(
            first_out.at[u // 2],
            first_out_recv.at[x],
            misc_send.at[3],
            misc_recv.at[3],
            (z, 4 * y + u, core),
        )
    send_or_keep(
        first_here,
        first_out.at[y // 2],
        first_out_recv.at[x],
        misc_self.at[4],
        misc_recv.at[3],
        (z, 4 * y + y, core),
    )

    wait_for(vec8, spread_recv.at[7])
    vector = vec8[...].reshape(64, 256)
    vector9 = vector
    multiply(
        lambda j: [
            second_early[s, :, columns_of(j)] + dot(vector9, block(upper.at[s], j))
            for s in range(2)
        ],
        send9,
        recv9,
        8,
    )

    odd = y % 2 == 1
    wait_for(root_out_recv, misc_recv.at[2])
    value = root_out_recv[...].reshape(64, 128)
    sol_root[...] = jnp.where(odd, value[:, 64:128], value[:, 0:64])
    wait_for(first_out_recv, misc_recv.at[3])
    value = first_out_recv[...].reshape(64, 128)
    sol_half[0] = jnp.where(odd, value[:, 64:128], value[:, 0:64])

    wait_for(recv9, scatter_recv.at[8])
    part9[...] = (leaf_value[...] - add_up(recv9, 16)).astype(BF16)
    spread(part9, vec9, 8)

    wait_for(vec9, spread_recv.at[8])
    second1 = vec9[:, 0].reshape(64, 256)
    second2 = vec9[:, 1].reshape(64, 256)
    for dx in (2, 1, 3, 0):
        j = (x + dx) % 4
        value1 = dot(second1, block(upper_inverse.at[1], j))
        value2 = dot(second2, block(upper_inverse.at[2], j))
        for u in range(4):
            span = slice(64 * u, 64 * u + 64)
            send10[4 * j + u] = jnp.concatenate([value1[:, span], value2[:, span]], axis=1).astype(
                BF16
            )
        for dy in (2, 1, 3, 0):
            peer = 4 * j + (y + dy) % 4
            if dx or dy:
                send(
                    send10.at[peer],
                    recv10.at[col],
                    scatter_send.at[9],
                    scatter_recv.at[9],
                    (z, peer, core),
                )
            else:
                start_local(send10.at[peer], recv10.at[col], scatter_recv.at[9])
    wait_for(recv10, scatter_recv.at[9])
    total = add_up(recv10, 16)
    sol_half[1] = total[:, 0:64]
    sol_half[2] = total[:, 64:128]

    sends = (send1, send2, send3, None, send5, send6, send7, send8, send9, send10)
    for stage, ref in enumerate(sends):
        if ref is not None:
            wait_for(ref.at[pl.ds(0, 15)], scatter_send.at[stage])
    wait_for(recv4.at[0], scatter_send.at[3])
    wait_for(recv4.at[1, pl.ds(0, 15)], scatter_send.at[3])
    for stage, ref in enumerate((vec1, vec2, vec3, None, None, None, vec7, vec8, vec9)):
        if ref is not None:
            wait_for(ref.at[pl.ds(0, 3)], spread_send.at[stage])
            wait_sent_unless(x == z, ref.at[0], spread_self.at[stage])
    for stage, ref in ((3, vec4), (4, vec5), (5, vec6)):
        wait_for(ref.at[0], spread_send.at[stage])
        wait_for(ref.at[1, pl.ds(0, 3)], spread_send.at[stage])
        wait_sent_unless(x == z, ref.at[0, 0], spread_self.at[stage])
    wait_for(leaf_recv.at[pl.ds(0, 3)], misc_send.at[0])
    wait_sent_unless(leaf_here, leaf_recv.at[0], misc_self.at[0])
    wait_for(bias_recv.at[pl.ds(0, 3)], misc_send.at[1])
    wait_sent_unless(bias_here, bias_recv.at[0], misc_self.at[1])
    wait_for(root_out_recv.at[pl.ds(0, 2)], misc_send.at[2])
    for k in range(2):
        wait_sent_unless(out_here(k, core), root_out_recv.at[0], misc_self.at[2 + k])
    wait_for(first_out_recv.at[pl.ds(0, 3)], misc_send.at[3])
    wait_sent_unless(first_here, first_out_recv.at[0], misc_self.at[4])


def per_device(
    rhs_half,
    rhs_root,
    lower_coupling,
    lower_pattern,
    upper_coupling,
    upper_pattern,
    lower_inverse,
    upper_inverse,
    root_lower_inverse,
    root_upper_inverse,
):
    vmem = pl.BlockSpec(memory_space=pltpu.VMEM)
    hbm = pl.BlockSpec(memory_space=pl.ANY)
    one = (16, 256)
    two = (2, 16, 256)
    half = (16, 128)
    stage_chunks = [two, one, one, None, half, half, one, one, two, (64, 128)]
    exchange = [
        pltpu.VMEM((2, 16) + half if chunk is None else (16,) + chunk, BF16)
        for chunk in stage_chunks
    ]
    part_chunks = [two, one, one, half, half, half, one, one, two]
    parts = [pltpu.VMEM(chunk, BF16) for chunk in part_chunks]
    vectors = [
        pltpu.VMEM((2, 4) + chunk if chunk == half else (4,) + chunk, BF16)
        for chunk in part_chunks
    ]
    scratch = [
        pltpu.VMEM((3, 64, 64), F32),
        pltpu.VMEM((64, 64), F32),
        pltpu.SMEM((5, 2, 8), jnp.int32),
        pltpu.SMEM((5, 2, 8), jnp.int32),
        pltpu.VMEM((5, 256, 1024), BF16),
        pltpu.VMEM((5, 256, 1024), BF16),
        pltpu.VMEM((3, 256, 1024), BF16),
        pltpu.VMEM((3, 256, 1024), BF16),
        pltpu.VMEM((256, 512), BF16),
        pltpu.VMEM((256, 512), BF16),
        pltpu.VMEM((64, 128), BF16),
        pltpu.VMEM((4, 64, 128), BF16),
        pltpu.VMEM((64, 128), F32),
        pltpu.VMEM((4, 16, 128), F32),
        *exchange,
        *exchange,
        *parts,
        *vectors,
        pltpu.VMEM(two, F32),
        pltpu.VMEM(one, F32),
        pltpu.VMEM((64, 1024), F32),
        pltpu.VMEM((2, 64, 1024), F32),
        pltpu.VMEM(half, F32),
        pltpu.VMEM((4,) + half, F32),
        pltpu.VMEM((2,) + half, F32),
        pltpu.VMEM((4,) + half, F32),
        pltpu.SemaphoreType.DMA((10,)),
        pltpu.SemaphoreType.DMA((10,)),
        pltpu.SemaphoreType.DMA((10,)),
        pltpu.SemaphoreType.DMA((9,)),
        pltpu.SemaphoreType.DMA((9,)),
        pltpu.SemaphoreType.DMA((9,)),
        pltpu.SemaphoreType.DMA((4,)),
        pltpu.SemaphoreType.DMA((4,)),
        pltpu.SemaphoreType.DMA((5,)),
    ]
    sol_half, sol_root = pl.pallas_call(
        kernel,
        name="tree_solve",
        out_shape=(pltpu.VMEM((3, 64, 64), F32), pltpu.VMEM((64, 64), F32)),
        in_specs=[hbm] * 10,
        out_specs=(vmem, vmem),
        scratch_shapes=scratch,
        compiler_params=pltpu.CompilerParams(collective_id=0, has_side_effects=True),
    )(
        rhs_half[0],
        rhs_root,
        lower_pattern[0],
        upper_pattern[0],
        lower_coupling[0],
        upper_coupling[0],
        lower_inverse[0],
        upper_inverse[0],
        root_lower_inverse,
        root_upper_inverse,
    )

    def leave(half_ref, root_ref, half_out, root_out, sems):
        first = pltpu.make_async_copy(half_ref, half_out, sems.at[0])
        second = pltpu.make_async_copy(root_ref, root_out, sems.at[1])
        first.start()
        second.start()
        first.wait()
        second.wait()

    sol_half, sol_root = pl.pallas_call(
        leave,
        name="leave",
        out_shape=(
            jax.ShapeDtypeStruct((3, 64, 64), F32),
            jax.ShapeDtypeStruct((64, 64), F32),
        ),
        in_specs=[vmem, vmem],
        out_specs=(hbm, hbm),
        scratch_shapes=[pltpu.SemaphoreType.DMA((2,))],
        compiler_params=pltpu.CompilerParams(vmem_limit_bytes=1 << 20),
    )(sol_half, sol_root)
    return (sol_half[None], sol_root)


def solution(mesh):
    in_specs = (
        P("gz", None, None, ("row", "col")),
        P(None, ("row", "col")),
        P("gz", None, "col", "row"),
        P("gz", None, "col", "row"),
        P("gz", None, "col", "row"),
        P("gz", None, "col", "row"),
        P("gz", None, "col", "row"),
        P("gz", None, "col", "row"),
        P("col", "row"),
        P("col", "row"),
    )
    out_specs = (P("gz", None, None, ("row", "col")), P(None, ("row", "col")))
    return jax.shard_map(
        per_device, mesh=mesh, in_specs=in_specs, out_specs=out_specs, check_vma=False
    )
```

```python
import jax
import jax.numpy as jnp
from jax import lax
from jax.experimental import pallas as pl
from jax.experimental.pallas import tpu as pltpu
from jax.sharding import PartitionSpec as P

MESH = pl.DeviceIdType.MESH
F32 = jnp.float32
BF16 = jnp.bfloat16

NEAR = sorted(
    ((dx, dy) for dx in range(4) for dy in range(4) if dx or dy),
    key=lambda d: -(min(d[0], 4 - d[0]) + min(d[1], 4 - d[1])),
)


def dot(vector, tiles):
    return jnp.dot(vector, tiles, preferred_element_type=F32)


def add_up(ref, count):
    total = ref[0].astype(F32)
    for i in range(1, count):
        total = total + ref[i].astype(F32)
    return total


def kernel(
    rhs_half_hbm,
    rhs_root_hbm,
    lower_pattern_hbm,
    upper_pattern_hbm,
    lower_hbm,
    upper_hbm,
    lower_inverse_hbm,
    upper_inverse_hbm,
    root_lower_hbm,
    root_upper_hbm,
    sol_half,
    sol_root,
    rhs_half,
    rhs_root,
    lower_pattern,
    upper_pattern,
    lower,
    upper,
    lower_inverse,
    upper_inverse,
    root_lower,
    root_upper,
    leaf_pack,
    leaf_recv,
    leaf_relay,
    bias_pack,
    bias_recv,
    send1,
    send2,
    send3,
    send4,
    send5,
    send6,
    send7,
    send8,
    send9,
    send10,
    recv1,
    recv2,
    recv3,
    recv4,
    recv5,
    recv6,
    recv7,
    recv8,
    recv9,
    recv10,
    part1,
    part2,
    part3,
    part4,
    part5,
    part6,
    part7,
    part8,
    part9,
    vec1,
    vec2,
    vec3,
    vec4,
    vec5,
    vec6,
    vec7,
    vec8,
    vec9,
    leaf_value,
    top_value,
    root_early,
    second_early,
    root_out,
    root_out_recv,
    first_out,
    first_out_recv,
    weight_sem,
    scatter_send,
    scatter_recv,
    spread_send,
    spread_recv,
    spread_self,
    misc_send,
    misc_recv,
    misc_self,
    relay_sem,
    ready,
    go,
):
    z = lax.axis_index("row")
    col = lax.axis_index("col")
    core = lax.axis_index("gz")
    x = col // 4
    y = col % 4
    other = 1 - core

    def start_local(src, dst, sem):
        pltpu.make_async_copy(src, dst, sem).start()

    def wait_for(ref, sem):
        pltpu.make_async_copy(ref, ref, sem).wait()

    def send(src, dst, send_sem, recv_sem, device):
        pltpu.make_async_remote_copy(
            src_ref=src,
            dst_ref=dst,
            send_sem=send_sem,
            recv_sem=recv_sem,
            device_id=device,
            device_id_type=MESH,
        ).start()

    def send_or_keep(here, src, dst, send_sem, recv_sem, device):
        @pl.when(jnp.logical_not(here))
        def _():
            send(src, dst, send_sem, recv_sem, device)

        @pl.when(here)
        def _():
            start_local(src, dst, recv_sem)

    def wait_sent_unless(here, ref, sem):
        @pl.when(jnp.logical_not(here))
        def _():
            wait_for(ref, sem)

    barrier = pltpu.get_barrier_semaphore()

    def greet(px, py, pz, pcore):
        pl.semaphore_signal(
            barrier, inc=1, device_id=(pz, 4 * px + py, pcore), device_id_type=MESH
        )

    @pl.when(core == 0)
    def _():
        for u in range(4):
            greet(y, u, x, 1)
        for dz in (2, 1, 3):
            greet(z, y, (z + dz) % 4, 0)

        @pl.when(x != z)
        def _():
            for u in range(4):
                greet(y, u, x, 0)
                greet(u, y, x, 0)

        for dx, dy in NEAR:
            greet((x + dx) % 4, (y + dy) % 4, z, 0)

    @pl.when(core == 1)
    def _():
        greet(x, y, z, 0)

    start_local(rhs_half_hbm, rhs_half, weight_sem.at[6])
    start_local(rhs_root_hbm, rhs_root, weight_sem.at[7])
    start_local(lower_pattern_hbm, lower_pattern, weight_sem.at[8])
    start_local(upper_pattern_hbm, upper_pattern, weight_sem.at[9])
    start_local(lower_inverse_hbm, lower_inverse, weight_sem.at[0])
    start_local(lower_hbm, lower, weight_sem.at[1])
    for j in range(4):
        columns = pl.ds(pl.multiple_of(256 * j + 128 * core, 128), 128)
        start_local(
            root_lower_hbm.at[:, columns], root_lower.at[:, pl.ds(128 * j, 128)], weight_sem.at[2]
        )
    for j in range(4):
        columns = pl.ds(pl.multiple_of(256 * j + 128 * core, 128), 128)
        start_local(
            root_upper_hbm.at[:, columns], root_upper.at[:, pl.ds(128 * j, 128)], weight_sem.at[3]
        )
    start_local(upper_hbm, upper, weight_sem.at[4])
    start_local(upper_inverse_hbm, upper_inverse, weight_sem.at[5])

    wait_for(rhs_half, weight_sem.at[6])
    wait_for(rhs_root, weight_sem.at[7])
    leaf_pack[...] = jnp.concatenate([rhs_half[1], rhs_half[2]], axis=1).astype(BF16)
    bias_pack[...] = jnp.concatenate([rhs_half[0], rhs_root[...]], axis=1)

    def tell(px, py, pz):
        pl.semaphore_signal(ready, inc=1, device_id=(pz, 4 * px + py, 0), device_id_type=MESH)

    @pl.when(core == 0)
    def _():
        @pl.when(x == z)
        def _():
            pl.semaphore_wait(barrier, 15 + 3 + 3 + 1)

        @pl.when(x != z)
        def _():
            pl.semaphore_wait(barrier, 15 + 3 + 3 + 1 + 4)
            for u in range(4):
                tell(u, y, x)

        for dx, dy in NEAR:
            tell((x + dx) % 4, (y + dy) % 4, z)

    @pl.when(core == 1)
    def _():
        pl.semaphore_wait(barrier, 4)

    leaf_here = jnp.logical_and(x == z, x == y)

    @pl.when(core == 0)
    def _():
        for dz in (2, 1, 3):
            send(
                leaf_pack,
                leaf_recv.at[y],
                misc_send.at[0],
                misc_recv.at[0],
                ((z + dz) % 4, 4 * z + x, 0),
            )
        send_or_keep(
            leaf_here,
            leaf_pack,
            leaf_recv.at[y],
            misc_self.at[0],
            misc_recv.at[0],
            (z, 4 * z + x, 0),
        )

    @pl.when(core == 1)
    def _():
        for dz in (2, 1, 3, 0):
            send(
                leaf_pack,
                leaf_relay.at[y],
                misc_send.at[0],
                relay_sem.at[0],
                ((z + dz) % 4, 4 * z + x, 0),
            )

    def scatter(src, dst, stage):
        for dx, dy in NEAR:
            peer = 4 * ((x + dx) % 4) + (y + dy) % 4
            send(
                src.at[peer],
                dst.at[col],
                scatter_send.at[stage],
                scatter_recv.at[stage],
                (z, peer, core),
            )
        start_local(src.at[col], dst.at[col], scatter_recv.at[stage])

    def spread(src, dst, stage):
        for dz in (2, 1, 3):
            send(
                src,
                dst.at[x],
                spread_send.at[stage],
                spread_recv.at[stage],
                ((z + dz) % 4, 4 * z + y, core),
            )
        send_or_keep(
            x == z,
            src,
            dst.at[x],
            spread_self.at[stage],
            spread_recv.at[stage],
            (z, 4 * z + y, core),
        )

    def spread_both(src, dst, stage):
        for dz in (2, 1, 3):
            for to in (other, core):
                send(
                    src,
                    dst.at[core, x],
                    spread_send.at[stage],
                    spread_recv.at[stage],
                    ((z + dz) % 4, 4 * z + y, to),
                )
        send(
            src,
            dst.at[core, x],
            spread_send.at[stage],
            spread_recv.at[stage],
            (z, 4 * z + y, other),
        )
        send_or_keep(
            x == z,
            src,
            dst.at[core, x],
            spread_self.at[stage],
            spread_recv.at[stage],
            (z, 4 * z + y, core),
        )

    def mask(tiles, pattern):
        @pl.loop(0, 5)
        def _(p):
            for a in range(2):
                for b in range(8):
                    here = (p, pl.ds(128 * a, 128), pl.ds(128 * b, 128))
                    keep = jnp.full((128, 128), pattern[p, a, b].astype(F32), F32)
                    tiles[here] = tiles[here] * keep.astype(BF16)

    def columns_of(j):
        return pl.ds(pl.multiple_of(256 * j, 256), 256)

    def block(ref, j):
        return ref[:, columns_of(j)]

    def multiply(values_of, src, dst, stage):
        for dy in (2, 1, 3, 0):
            j = (y + dy) % 4
            values = values_of(j)
            for q in range(4):
                rows = [value[16 * q : 16 * q + 16].astype(BF16) for value in values]
                if len(rows) == 1:
                    src[4 * q + j] = rows[0]
                else:
                    for s in range(2):
                        src[4 * q + j, s] = rows[s]
            for dx in (2, 1, 3, 0):
                peer = 4 * ((x + dx) % 4) + j
                if dx or dy:
                    send(
                        src.at[peer],
                        dst.at[col],
                        scatter_send.at[stage],
                        scatter_recv.at[stage],
                        (z, peer, core),
                    )
                else:
                    start_local(src.at[peer], dst.at[col], scatter_recv.at[stage])

    wait_for(lower, weight_sem.at[1])
    wait_for(lower_pattern, weight_sem.at[8])
    mask(lower, lower_pattern)

    @pl.when(core == 0)
    def _():
        pl.semaphore_wait(ready, 15 + 3)
        pl.semaphore_signal(go, inc=1, device_id=(z, col, 1), device_id_type=MESH)

    @pl.when(core == 1)
    def _():
        pl.semaphore_wait(go, 1)

    bias_here = x == y
    for dq in (2, 1, 3):
        q = (x + dq) % 4
        send(
            bias_pack.at[pl.ds(pl.multiple_of(16 * q, 16), 16)],
            bias_recv.at[y],
            misc_send.at[1],
            misc_recv.at[1],
            (z, 4 * q + x, core),
        )
    own_rows = pl.ds(pl.multiple_of(16 * x, 16), 16)
    send_or_keep(
        bias_here,
        bias_pack.at[own_rows],
        bias_recv.at[y],
        misc_self.at[1],
        misc_recv.at[1],
        (z, 4 * x + x, core),
    )

    @pl.when(core == 0)
    def _():
        wait_for(leaf_relay, relay_sem.at[0])
        send(leaf_relay, leaf_recv, relay_sem.at[1], misc_recv.at[0], (z, col, 1))

    wait_for(leaf_recv, misc_recv.at[0])
    wait_for(lower_inverse, weight_sem.at[0])
    pieces = [leaf_recv[u].astype(F32) for u in range(4)]
    leaves = [
        jnp.concatenate([p[:, 64 * s : 64 * s + 64] for p in pieces], axis=1).astype(BF16)
        for s in range(2)
    ]
    multiply(
        lambda j: [dot(leaves[s], block(lower_inverse.at[1 + s], j)) for s in range(2)],
        send1,
        recv1,
        0,
    )
    wait_for(recv1, scatter_recv.at[0])
    leaf_value[...] = add_up(recv1, 16)
    part1[...] = leaf_value[...].astype(BF16)
    spread(part1, vec1, 0)

    wait_for(vec1, spread_recv.at[0])
    leaf1 = vec1[:, 0].reshape(64, 256)
    leaf2 = vec1[:, 1].reshape(64, 256)
    multiply(
        lambda j: [dot(leaf1, block(lower.at[0], j)) + dot(leaf2, block(lower.at[1], j))],
        send2,
        recv2,
        1,
    )
    for j in range(4):
        root_early[:, 256 * j : 256 * j + 256] = dot(leaf1, block(lower.at[3], j)) + dot(
            leaf2, block(lower.at[4], j)
        )
    wait_for(bias_recv, misc_recv.at[1])
    top_bias = jnp.concatenate([bias_recv[u][:, 0:64] for u in range(4)], axis=1)
    wait_for(recv2, scatter_recv.at[1])
    part2[...] = (top_bias - add_up(recv2, 16)).astype(BF16)
    spread(part2, vec2, 1)

    wait_for(vec2, spread_recv.at[1])
    vector = vec2[...].reshape(64, 256)
    vector3 = vector
    multiply(lambda j: [dot(vector3, block(lower_inverse.at[0], j))], send3, recv3, 2)
    wait_for(recv3, scatter_recv.at[2])
    top_value[...] = add_up(recv3, 16)
    part3[...] = top_value[...].astype(BF16)
    spread(part3, vec3, 2)

    wait_for(vec3, spread_recv.at[2])
    vector = vec3[...].reshape(64, 256)
    for dy in (2, 1, 3, 0):
        j = (y + dy) % 4
        value = root_early[:, columns_of(j)] + dot(vector, block(lower.at[2], j))
        for half in range(2):
            for q in range(4):
                send4[half, 4 * q + j] = value[
                    16 * q : 16 * q + 16, 128 * half : 128 * half + 128
                ].astype(BF16)
        for dx in (2, 1, 3, 0):
            peer = 4 * ((x + dx) % 4) + j
            for to in (other, core):
                if dx or dy or to is other:
                    send(
                        send4.at[to, peer],
                        recv4.at[core, col],
                        scatter_send.at[3],
                        scatter_recv.at[3],
                        (z, peer, to),
                    )
                else:
                    start_local(send4.at[to, peer], recv4.at[core, col], scatter_recv.at[3])
    root_bias = jnp.concatenate(
        [bias_recv[2 * core][:, 64:128], bias_recv[2 * core + 1][:, 64:128]], axis=1
    )
    wait_for(upper, weight_sem.at[4])
    wait_for(upper_pattern, weight_sem.at[9])
    mask(upper, upper_pattern)
    wait_for(recv4, scatter_recv.at[3])
    part4[...] = (root_bias - add_up(recv4.at[0], 16) - add_up(recv4.at[1], 16)).astype(BF16)
    spread_both(part4, vec4, 3)

    def whole(ref):
        return jnp.concatenate([ref[0].reshape(64, 128), ref[1].reshape(64, 128)], axis=1)

    def halves(ref, vector, tiles):
        for pair in range(2):
            value = dot(vector, tiles[:, 256 * pair : 256 * pair + 256])
            for k in range(2):
                for q in range(4):
                    ref[4 * q + 2 * pair + k] = value[
                        16 * q : 16 * q + 16, 128 * k : 128 * k + 128
                    ].astype(BF16)

    wait_for(root_lower, weight_sem.at[2])
    wait_for(vec4, spread_recv.at[3])
    halves(send5, whole(vec4), root_lower)
    scatter(send5, recv5, 4)
    wait_for(recv5, scatter_recv.at[4])
    part5[...] = add_up(recv5, 16).astype(BF16)
    spread_both(part5, vec5, 4)
    wait_for(root_upper, weight_sem.at[3])
    wait_for(vec5, spread_recv.at[4])
    halves(send6, whole(vec5), root_upper)
    scatter(send6, recv6, 5)
    wait_for(recv6, scatter_recv.at[5])
    root_out[...] = add_up(recv6, 16)
    part6[...] = root_out[...].astype(BF16)
    spread_both(part6, vec6, 5)

    def out_here(k, to):
        return jnp.logical_and(jnp.logical_and(x == y, 2 * core + k == y), to == core)

    for k in range(2):
        owner = 4 * y + 2 * core + k
        send(root_out, root_out_recv.at[x], misc_send.at[2], misc_recv.at[2], (z, owner, other))
        send_or_keep(
            out_here(k, core),
            root_out,
            root_out_recv.at[x],
            misc_self.at[2 + k],
            misc_recv.at[2],
            (z, owner, core),
        )

    wait_for(vec6, spread_recv.at[5])
    vector = whole(vec6)
    vector7 = vector
    multiply(lambda j: [dot(vector7, block(upper.at[2], j))], send7, recv7, 6)
    for s in range(2):
        for j in range(4):
            second_early[s, :, 256 * j : 256 * j + 256] = dot(vector, block(upper.at[3 + s], j))
    wait_for(recv7, scatter_recv.at[6])
    part7[...] = (top_value[...] - add_up(recv7, 16)).astype(BF16)
    spread(part7, vec7, 6)

    wait_for(upper_inverse, weight_sem.at[5])
    wait_for(vec7, spread_recv.at[6])
    vector = vec7[...].reshape(64, 256)
    vector8 = vector
    multiply(lambda j: [dot(vector8, block(upper_inverse.at[0], j))], send8, recv8, 7)
    wait_for(recv8, scatter_recv.at[7])
    first = add_up(recv8, 16)
    part8[...] = first.astype(BF16)
    spread(part8, vec8, 7)
    first_out[0] = first[:, 0:128]
    first_out[1] = first[:, 128:256]
    first_here = x == y
    for du in (2, 1, 3):
        u = (y + du) % 4
        send(
            first_out.at[u // 2],
            first_out_recv.at[x],
            misc_send.at[3],
            misc_recv.at[3],
            (z, 4 * y + u, core),
        )
    send_or_keep(
        first_here,
        first_out.at[y // 2],
        first_out_recv.at[x],
        misc_self.at[4],
        misc_recv.at[3],
        (z, 4 * y + y, core),
    )

    wait_for(vec8, spread_recv.at[7])
    vector = vec8[...].reshape(64, 256)
    vector9 = vector
    multiply(
        lambda j: [
            second_early[s, :, columns_of(j)] + dot(vector9, block(upper.at[s], j))
            for s in range(2)
        ],
        send9,
        recv9,
        8,
    )

    odd = y % 2 == 1
    wait_for(root_out_recv, misc_recv.at[2])
    value = root_out_recv[...].reshape(64, 128)
    sol_root[...] = jnp.where(odd, value[:, 64:128], value[:, 0:64])
    wait_for(first_out_recv, misc_recv.at[3])
    value = first_out_recv[...].reshape(64, 128)
    sol_half[0] = jnp.where(odd, value[:, 64:128], value[:, 0:64])

    wait_for(recv9, scatter_recv.at[8])
    part9[...] = (leaf_value[...] - add_up(recv9, 16)).astype(BF16)
    spread(part9, vec9, 8)

    wait_for(vec9, spread_recv.at[8])
    second1 = vec9[:, 0].reshape(64, 256)
    second2 = vec9[:, 1].reshape(64, 256)
    for dx in (2, 1, 3, 0):
        j = (x + dx) % 4
        value1 = dot(second1, block(upper_inverse.at[1], j))
        value2 = dot(second2, block(upper_inverse.at[2], j))
        for u in range(4):
            span = slice(64 * u, 64 * u + 64)
            send10[4 * j + u] = jnp.concatenate([value1[:, span], value2[:, span]], axis=1).astype(
                BF16
            )
        for dy in (2, 1, 3, 0):
            peer = 4 * j + (y + dy) % 4
            if dx or dy:
                send(
                    send10.at[peer],
                    recv10.at[col],
                    scatter_send.at[9],
                    scatter_recv.at[9],
                    (z, peer, core),
                )
            else:
                start_local(send10.at[peer], recv10.at[col], scatter_recv.at[9])
    wait_for(recv10, scatter_recv.at[9])
    total = add_up(recv10, 16)
    sol_half[1] = total[:, 0:64]
    sol_half[2] = total[:, 64:128]

    sends = (send1, send2, send3, None, send5, send6, send7, send8, send9, send10)
    for stage, ref in enumerate(sends):
        if ref is not None:
            wait_for(ref.at[pl.ds(0, 15)], scatter_send.at[stage])
    wait_for(recv4.at[0], scatter_send.at[3])
    wait_for(recv4.at[1, pl.ds(0, 15)], scatter_send.at[3])
    for stage, ref in enumerate((vec1, vec2, vec3, None, None, None, vec7, vec8, vec9)):
        if ref is not None:
            wait_for(ref.at[pl.ds(0, 3)], spread_send.at[stage])
            wait_sent_unless(x == z, ref.at[0], spread_self.at[stage])
    for stage, ref in ((3, vec4), (4, vec5), (5, vec6)):
        wait_for(ref.at[0], spread_send.at[stage])
        wait_for(ref.at[1, pl.ds(0, 3)], spread_send.at[stage])
        wait_sent_unless(x == z, ref.at[0, 0], spread_self.at[stage])
    wait_for(leaf_recv.at[pl.ds(0, 3)], misc_send.at[0])

    @pl.when(core == 0)
    def _():
        wait_for(leaf_recv, relay_sem.at[1])
        wait_sent_unless(leaf_here, leaf_recv.at[0], misc_self.at[0])

    @pl.when(core == 1)
    def _():
        wait_for(leaf_recv.at[0], misc_send.at[0])

    wait_for(bias_recv.at[pl.ds(0, 3)], misc_send.at[1])
    wait_sent_unless(bias_here, bias_recv.at[0], misc_self.at[1])
    wait_for(root_out_recv.at[pl.ds(0, 2)], misc_send.at[2])
    for k in range(2):
        wait_sent_unless(out_here(k, core), root_out_recv.at[0], misc_self.at[2 + k])
    wait_for(first_out_recv.at[pl.ds(0, 3)], misc_send.at[3])
    wait_sent_unless(first_here, first_out_recv.at[0], misc_self.at[4])


def per_device(
    rhs_half,
    rhs_root,
    lower_coupling,
    lower_pattern,
    upper_coupling,
    upper_pattern,
    lower_inverse,
    upper_inverse,
    root_lower_inverse,
    root_upper_inverse,
):
    vmem = pl.BlockSpec(memory_space=pltpu.VMEM)
    hbm = pl.BlockSpec(memory_space=pl.ANY)
    one = (16, 256)
    two = (2, 16, 256)
    half = (16, 128)
    stage_chunks = [two, one, one, None, half, half, one, one, two, (64, 128)]
    exchange = [
        pltpu.VMEM((2, 16) + half if chunk is None else (16,) + chunk, BF16)
        for chunk in stage_chunks
    ]
    part_chunks = [two, one, one, half, half, half, one, one, two]
    parts = [pltpu.VMEM(chunk, BF16) for chunk in part_chunks]
    vectors = [
        pltpu.VMEM((2, 4) + chunk if chunk == half else (4,) + chunk, BF16)
        for chunk in part_chunks
    ]
    scratch = [
        pltpu.VMEM((3, 64, 64), F32),
        pltpu.VMEM((64, 64), F32),
        pltpu.SMEM((5, 2, 8), jnp.int32),
        pltpu.SMEM((5, 2, 8), jnp.int32),
        pltpu.VMEM((5, 256, 1024), BF16),
        pltpu.VMEM((5, 256, 1024), BF16),
        pltpu.VMEM((3, 256, 1024), BF16),
        pltpu.VMEM((3, 256, 1024), BF16),
        pltpu.VMEM((256, 512), BF16),
        pltpu.VMEM((256, 512), BF16),
        pltpu.VMEM((64, 128), BF16),
        pltpu.VMEM((4, 64, 128), BF16),
        pltpu.VMEM((4, 64, 128), BF16),
        pltpu.VMEM((64, 128), F32),
        pltpu.VMEM((4, 16, 128), F32),
        *exchange,
        *exchange,
        *parts,
        *vectors,
        pltpu.VMEM(two, F32),
        pltpu.VMEM(one, F32),
        pltpu.VMEM((64, 1024), F32),
        pltpu.VMEM((2, 64, 1024), F32),
        pltpu.VMEM(half, F32),
        pltpu.VMEM((4,) + half, F32),
        pltpu.VMEM((2,) + half, F32),
        pltpu.VMEM((4,) + half, F32),
        pltpu.SemaphoreType.DMA((10,)),
        pltpu.SemaphoreType.DMA((10,)),
        pltpu.SemaphoreType.DMA((10,)),
        pltpu.SemaphoreType.DMA((9,)),
        pltpu.SemaphoreType.DMA((9,)),
        pltpu.SemaphoreType.DMA((9,)),
        pltpu.SemaphoreType.DMA((4,)),
        pltpu.SemaphoreType.DMA((4,)),
        pltpu.SemaphoreType.DMA((5,)),
        pltpu.SemaphoreType.DMA((2,)),
        pltpu.SemaphoreType.REGULAR,
        pltpu.SemaphoreType.REGULAR,
    ]
    sol_half, sol_root = pl.pallas_call(
        kernel,
        name="tree_solve",
        out_shape=(pltpu.VMEM((3, 64, 64), F32), pltpu.VMEM((64, 64), F32)),
        in_specs=[hbm] * 10,
        out_specs=(vmem, vmem),
        scratch_shapes=scratch,
        compiler_params=pltpu.CompilerParams(collective_id=0, has_side_effects=True),
    )(
        rhs_half[0],
        rhs_root,
        lower_pattern[0],
        upper_pattern[0],
        lower_coupling[0],
        upper_coupling[0],
        lower_inverse[0],
        upper_inverse[0],
        root_lower_inverse,
        root_upper_inverse,
    )

    def leave(half_ref, root_ref, half_out, root_out, sems):
        first = pltpu.make_async_copy(half_ref, half_out, sems.at[0])
        second = pltpu.make_async_copy(root_ref, root_out, sems.at[1])
        first.start()
        second.start()
        first.wait()
        second.wait()

    sol_half, sol_root = pl.pallas_call(
        leave,
        name="leave",
        out_shape=(
            jax.ShapeDtypeStruct((3, 64, 64), F32),
            jax.ShapeDtypeStruct((64, 64), F32),
        ),
        in_specs=[vmem, vmem],
        out_specs=(hbm, hbm),
        scratch_shapes=[pltpu.SemaphoreType.DMA((2,))],
        compiler_params=pltpu.CompilerParams(vmem_limit_bytes=1 << 20),
    )(sol_half, sol_root)
    return (sol_half[None], sol_root)


def solution(mesh):
    in_specs = (
        P("gz", None, None, ("row", "col")),
        P(None, ("row", "col")),
        P("gz", None, "col", "row"),
        P("gz", None, "col", "row"),
        P("gz", None, "col", "row"),
        P("gz", None, "col", "row"),
        P("gz", None, "col", "row"),
        P("gz", None, "col", "row"),
        P("col", "row"),
        P("col", "row"),
    )
    out_specs = (P("gz", None, None, ("row", "col")), P(None, ("row", "col")))
    return jax.shard_map(
        per_device, mesh=mesh, in_specs=in_specs, out_specs=out_specs, check_vma=False
    )
```

```python
import jax
import jax.numpy as jnp
from jax import lax
from jax.experimental import pallas as pl
from jax.experimental.pallas import tpu as pltpu
from jax.sharding import PartitionSpec as P

MESH = pl.DeviceIdType.MESH
F32 = jnp.float32
BF16 = jnp.bfloat16

NEAR = sorted(
    ((dx, dy) for dx in range(4) for dy in range(4) if dx or dy),
    key=lambda d: -(min(d[0], 4 - d[0]) + min(d[1], 4 - d[1])),
)


def dot(vector, tiles):
    return jnp.dot(vector, tiles, preferred_element_type=F32)


def add_up(ref, count):
    total = ref[0].astype(F32)
    for i in range(1, count):
        total = total + ref[i].astype(F32)
    return total


def kernel(
    rhs_half_hbm,
    rhs_root_hbm,
    lower_pattern_hbm,
    upper_pattern_hbm,
    lower_hbm,
    upper_hbm,
    lower_inverse_hbm,
    upper_inverse_hbm,
    root_lower_hbm,
    root_upper_hbm,
    sol_half,
    sol_root,
    rhs_half,
    rhs_root,
    lower_pattern,
    upper_pattern,
    lower,
    upper,
    lower_inverse,
    upper_inverse,
    root_lower,
    root_upper,
    leaf_pack,
    leaf_recv,
    leaf_relay,
    bias_pack,
    bias_recv,
    send1,
    send2,
    send3,
    send4,
    send5,
    send6,
    send7,
    send8,
    send9,
    send10,
    recv1,
    recv2,
    recv3,
    recv4,
    recv5,
    recv6,
    recv7,
    recv8,
    recv9,
    recv10,
    part1,
    part2,
    part3,
    part4,
    part5,
    part6,
    part7,
    part8,
    part9,
    vec1,
    vec2,
    vec3,
    vec4,
    vec5,
    vec6,
    vec7,
    vec8,
    vec9,
    leaf_value,
    top_value,
    root_early,
    second_early,
    root_out,
    root_out_recv,
    first_out,
    first_out_recv,
    weight_sem,
    scatter_send,
    scatter_recv,
    spread_send,
    spread_recv,
    spread_self,
    misc_send,
    misc_recv,
    misc_self,
    relay_sem,
    here,
    ready,
    go,
):
    z = lax.axis_index("row")
    col = lax.axis_index("col")
    core = lax.axis_index("gz")
    x = col // 4
    y = col % 4
    other = 1 - core

    def start_local(src, dst, sem):
        pltpu.make_async_copy(src, dst, sem).start()

    def wait_for(ref, sem):
        pltpu.make_async_copy(ref, ref, sem).wait()

    def send(src, dst, send_sem, recv_sem, device):
        pltpu.make_async_remote_copy(
            src_ref=src,
            dst_ref=dst,
            send_sem=send_sem,
            recv_sem=recv_sem,
            device_id=device,
            device_id_type=MESH,
        ).start()

    def send_or_keep(here, src, dst, send_sem, recv_sem, device):
        @pl.when(jnp.logical_not(here))
        def _():
            send(src, dst, send_sem, recv_sem, device)

        @pl.when(here)
        def _():
            start_local(src, dst, recv_sem)

    def wait_sent_unless(here, ref, sem):
        @pl.when(jnp.logical_not(here))
        def _():
            wait_for(ref, sem)

    barrier = pltpu.get_barrier_semaphore()

    def greet(px, py, pz, pcore):
        pl.semaphore_signal(
            barrier, inc=1, device_id=(pz, 4 * px + py, pcore), device_id_type=MESH
        )

    @pl.when(core == 0)
    def _():
        greet(x, y, z, 1)
        for u in range(4):
            greet(y, u, x, 1)
        for dz in (2, 1, 3):
            greet(z, y, (z + dz) % 4, 0)

        @pl.when(x != z)
        def _():
            for u in range(4):
                greet(y, u, x, 0)
                greet(u, y, x, 0)

        for dx, dy in NEAR:
            greet((x + dx) % 4, (y + dy) % 4, z, 0)

    start_local(rhs_half_hbm, rhs_half, weight_sem.at[6])
    start_local(rhs_root_hbm, rhs_root, weight_sem.at[7])
    wait_for(rhs_half, weight_sem.at[6])
    wait_for(rhs_root, weight_sem.at[7])
    leaf_pack[...] = jnp.concatenate([rhs_half[1], rhs_half[2]], axis=1).astype(BF16)
    bias_pack[...] = jnp.concatenate([rhs_half[0], rhs_root[...]], axis=1)

    @pl.when(core == 0)
    def _():
        @pl.when(x == z)
        def _():
            pl.semaphore_wait(barrier, 15 + 3 + 3)

        @pl.when(x != z)
        def _():
            pl.semaphore_wait(barrier, 15 + 3 + 3 + 4)

    @pl.when(core == 1)
    def _():
        pl.semaphore_wait(barrier, 1 + 4)
        pl.semaphore_signal(here, inc=1, device_id=(z, col, 0), device_id_type=MESH)

    leaf_here = jnp.logical_and(x == z, x == y)

    @pl.when(core == 0)
    def _():
        for dz in (2, 1, 3):
            send(
                leaf_pack,
                leaf_recv.at[y],
                misc_send.at[0],
                misc_recv.at[0],
                ((z + dz) % 4, 4 * z + x, 0),
            )
        send_or_keep(
            leaf_here,
            leaf_pack,
            leaf_recv.at[y],
            misc_self.at[0],
            misc_recv.at[0],
            (z, 4 * z + x, 0),
        )

    @pl.when(core == 1)
    def _():
        for dz in (2, 1, 3, 0):
            send(
                leaf_pack,
                leaf_relay.at[y],
                misc_send.at[0],
                relay_sem.at[y],
                ((z + dz) % 4, 4 * z + x, 0),
            )

    start_local(lower_pattern_hbm, lower_pattern, weight_sem.at[8])
    start_local(upper_pattern_hbm, upper_pattern, weight_sem.at[9])
    start_local(lower_inverse_hbm, lower_inverse, weight_sem.at[0])
    start_local(lower_hbm, lower, weight_sem.at[1])
    for j in range(4):
        columns = pl.ds(pl.multiple_of(256 * j + 128 * core, 128), 128)
        start_local(
            root_lower_hbm.at[:, columns], root_lower.at[:, pl.ds(128 * j, 128)], weight_sem.at[2]
        )
    for j in range(4):
        columns = pl.ds(pl.multiple_of(256 * j + 128 * core, 128), 128)
        start_local(
            root_upper_hbm.at[:, columns], root_upper.at[:, pl.ds(128 * j, 128)], weight_sem.at[3]
        )
    start_local(upper_hbm, upper, weight_sem.at[4])
    start_local(upper_inverse_hbm, upper_inverse, weight_sem.at[5])


    def scatter(src, dst, stage):
        for dx, dy in NEAR:
            peer = 4 * ((x + dx) % 4) + (y + dy) % 4
            send(
                src.at[peer],
                dst.at[col],
                scatter_send.at[stage],
                scatter_recv.at[stage],
                (z, peer, core),
            )
        start_local(src.at[col], dst.at[col], scatter_recv.at[stage])

    def spread(src, dst, stage):
        for dz in (2, 1, 3):
            send(
                src,
                dst.at[x],
                spread_send.at[stage],
                spread_recv.at[stage],
                ((z + dz) % 4, 4 * z + y, core),
            )
        send_or_keep(
            x == z,
            src,
            dst.at[x],
            spread_self.at[stage],
            spread_recv.at[stage],
            (z, 4 * z + y, core),
        )

    def spread_both(src, dst, stage):
        for dz in (2, 1, 3):
            for to in (other, core):
                send(
                    src,
                    dst.at[core, x],
                    spread_send.at[stage],
                    spread_recv.at[stage],
                    ((z + dz) % 4, 4 * z + y, to),
                )
        send(
            src,
            dst.at[core, x],
            spread_send.at[stage],
            spread_recv.at[stage],
            (z, 4 * z + y, other),
        )
        send_or_keep(
            x == z,
            src,
            dst.at[core, x],
            spread_self.at[stage],
            spread_recv.at[stage],
            (z, 4 * z + y, core),
        )

    def mask(tiles, pattern):
        @pl.loop(0, 5)
        def _(p):
            for a in range(2):
                for b in range(8):
                    here = (p, pl.ds(128 * a, 128), pl.ds(128 * b, 128))
                    keep = jnp.full((128, 128), pattern[p, a, b].astype(F32), F32)
                    tiles[here] = tiles[here] * keep.astype(BF16)

    def columns_of(j):
        return pl.ds(pl.multiple_of(256 * j, 256), 256)

    def block(ref, j):
        return ref[:, columns_of(j)]

    def multiply(values_of, src, dst, stage):
        for dy in (2, 1, 3, 0):
            j = (y + dy) % 4
            values = values_of(j)
            for q in range(4):
                rows = [value[16 * q : 16 * q + 16].astype(BF16) for value in values]
                if len(rows) == 1:
                    src[4 * q + j] = rows[0]
                else:
                    for s in range(2):
                        src[4 * q + j, s] = rows[s]
            for dx in (2, 1, 3, 0):
                peer = 4 * ((x + dx) % 4) + j
                if dx or dy:
                    send(
                        src.at[peer],
                        dst.at[col],
                        scatter_send.at[stage],
                        scatter_recv.at[stage],
                        (z, peer, core),
                    )
                else:
                    start_local(src.at[peer], dst.at[col], scatter_recv.at[stage])

    bias_here = x == y

    def send_biases():
        for dq in (2, 1, 3):
            q = (x + dq) % 4
            send(
                bias_pack.at[pl.ds(pl.multiple_of(16 * q, 16), 16)],
                bias_recv.at[y],
                misc_send.at[1],
                misc_recv.at[1],
                (z, 4 * q + x, core),
            )
        own_rows = pl.ds(pl.multiple_of(16 * x, 16), 16)
        send_or_keep(
            bias_here,
            bias_pack.at[own_rows],
            bias_recv.at[y],
            misc_self.at[1],
            misc_recv.at[1],
            (z, 4 * x + x, core),
        )

    def tell(px, py, pz):
        pl.semaphore_signal(ready, inc=1, device_id=(pz, 4 * px + py, 0), device_id_type=MESH)

    @pl.when(core == 0)
    def _():
        send_biases()
        pl.semaphore_wait(here, 1)

        @pl.when(x != z)
        def _():
            for u in range(4):
                tell(u, y, x)

        for dx, dy in NEAR:
            tell((x + dx) % 4, (y + dy) % 4, z)

    wait_for(lower, weight_sem.at[1])
    wait_for(lower_pattern, weight_sem.at[8])
    mask(lower, lower_pattern)

    @pl.when(core == 1)
    def _():
        pl.semaphore_wait(go, 1)
        send_biases()

    wait_for(leaf_recv, misc_recv.at[0])
    wait_for(lower_inverse, weight_sem.at[0])
    pieces = [leaf_recv[u].astype(F32) for u in range(4)]
    leaves = [
        jnp.concatenate([p[:, 64 * s : 64 * s + 64] for p in pieces], axis=1).astype(BF16)
        for s in range(2)
    ]
    multiply(
        lambda j: [dot(leaves[s], block(lower_inverse.at[1 + s], j)) for s in range(2)],
        send1,
        recv1,
        0,
    )

    @pl.when(core == 0)
    def _():
        pl.semaphore_wait(ready, 15 + 3)
        pl.semaphore_signal(go, inc=1, device_id=(z, col, 1), device_id_type=MESH)
        for u in range(4):
            wait_for(leaf_relay.at[u], relay_sem.at[u])
            send(leaf_relay.at[u], leaf_recv.at[u], relay_sem.at[4], misc_recv.at[0], (z, col, 1))

    wait_for(recv1, scatter_recv.at[0])
    leaf_value[...] = add_up(recv1, 16)
    part1[...] = leaf_value[...].astype(BF16)
    spread(part1, vec1, 0)

    wait_for(vec1, spread_recv.at[0])
    leaf1 = vec1[:, 0].reshape(64, 256)
    leaf2 = vec1[:, 1].reshape(64, 256)
    multiply(
        lambda j: [dot(leaf1, block(lower.at[0], j)) + dot(leaf2, block(lower.at[1], j))],
        send2,
        recv2,
        1,
    )
    for j in range(4):
        root_early[:, 256 * j : 256 * j + 256] = dot(leaf1, block(lower.at[3], j)) + dot(
            leaf2, block(lower.at[4], j)
        )
    wait_for(bias_recv, misc_recv.at[1])
    top_bias = jnp.concatenate([bias_recv[u][:, 0:64] for u in range(4)], axis=1)
    wait_for(recv2, scatter_recv.at[1])
    part2[...] = (top_bias - add_up(recv2, 16)).astype(BF16)
    spread(part2, vec2, 1)

    wait_for(vec2, spread_recv.at[1])
    vector = vec2[...].reshape(64, 256)
    vector3 = vector
    multiply(lambda j: [dot(vector3, block(lower_inverse.at[0], j))], send3, recv3, 2)
    wait_for(recv3, scatter_recv.at[2])
    top_value[...] = add_up(recv3, 16)
    part3[...] = top_value[...].astype(BF16)
    spread(part3, vec3, 2)

    wait_for(vec3, spread_recv.at[2])
    vector = vec3[...].reshape(64, 256)
    for dy in (2, 1, 3, 0):
        j = (y + dy) % 4
        value = root_early[:, columns_of(j)] + dot(vector, block(lower.at[2], j))
        for half in range(2):
            for q in range(4):
                send4[half, 4 * q + j] = value[
                    16 * q : 16 * q + 16, 128 * half : 128 * half + 128
                ].astype(BF16)
        for dx in (2, 1, 3, 0):
            peer = 4 * ((x + dx) % 4) + j
            for to in (other, core):
                if dx or dy or to is other:
                    send(
                        send4.at[to, peer],
                        recv4.at[core, col],
                        scatter_send.at[3],
                        scatter_recv.at[3],
                        (z, peer, to),
                    )
                else:
                    start_local(send4.at[to, peer], recv4.at[core, col], scatter_recv.at[3])
    root_bias = jnp.concatenate(
        [bias_recv[2 * core][:, 64:128], bias_recv[2 * core + 1][:, 64:128]], axis=1
    )
    wait_for(upper, weight_sem.at[4])
    wait_for(upper_pattern, weight_sem.at[9])
    mask(upper, upper_pattern)
    wait_for(recv4, scatter_recv.at[3])
    part4[...] = (root_bias - add_up(recv4.at[0], 16) - add_up(recv4.at[1], 16)).astype(BF16)
    spread_both(part4, vec4, 3)

    def whole(ref):
        return jnp.concatenate([ref[0].reshape(64, 128), ref[1].reshape(64, 128)], axis=1)

    def halves(ref, vector, tiles):
        for pair in range(2):
            value = dot(vector, tiles[:, 256 * pair : 256 * pair + 256])
            for k in range(2):
                for q in range(4):
                    ref[4 * q + 2 * pair + k] = value[
                        16 * q : 16 * q + 16, 128 * k : 128 * k + 128
                    ].astype(BF16)

    wait_for(root_lower, weight_sem.at[2])
    wait_for(vec4, spread_recv.at[3])
    halves(send5, whole(vec4), root_lower)
    scatter(send5, recv5, 4)
    wait_for(recv5, scatter_recv.at[4])
    part5[...] = add_up(recv5, 16).astype(BF16)
    spread_both(part5, vec5, 4)
    wait_for(root_upper, weight_sem.at[3])
    wait_for(vec5, spread_recv.at[4])
    halves(send6, whole(vec5), root_upper)
    scatter(send6, recv6, 5)
    wait_for(recv6, scatter_recv.at[5])
    root_out[...] = add_up(recv6, 16)
    part6[...] = root_out[...].astype(BF16)
    spread_both(part6, vec6, 5)

    def out_here(k, to):
        return jnp.logical_and(jnp.logical_and(x == y, 2 * core + k == y), to == core)

    for k in range(2):
        owner = 4 * y + 2 * core + k
        send(root_out, root_out_recv.at[x], misc_send.at[2], misc_recv.at[2], (z, owner, other))
        send_or_keep(
            out_here(k, core),
            root_out,
            root_out_recv.at[x],
            misc_self.at[2 + k],
            misc_recv.at[2],
            (z, owner, core),
        )

    wait_for(vec6, spread_recv.at[5])
    vector = whole(vec6)
    vector7 = vector
    multiply(lambda j: [dot(vector7, block(upper.at[2], j))], send7, recv7, 6)
    for s in range(2):
        for j in range(4):
            second_early[s, :, 256 * j : 256 * j + 256] = dot(vector, block(upper.at[3 + s], j))
    wait_for(recv7, scatter_recv.at[6])
    part7[...] = (top_value[...] - add_up(recv7, 16)).astype(BF16)
    spread(part7, vec7, 6)

    wait_for(upper_inverse, weight_sem.at[5])
    wait_for(vec7, spread_recv.at[6])
    vector = vec7[...].reshape(64, 256)
    vector8 = vector
    multiply(lambda j: [dot(vector8, block(upper_inverse.at[0], j))], send8, recv8, 7)
    wait_for(recv8, scatter_recv.at[7])
    first = add_up(recv8, 16)
    part8[...] = first.astype(BF16)
    spread(part8, vec8, 7)
    first_out[0] = first[:, 0:128]
    first_out[1] = first[:, 128:256]
    first_here = x == y
    for du in (2, 1, 3):
        u = (y + du) % 4
        send(
            first_out.at[u // 2],
            first_out_recv.at[x],
            misc_send.at[3],
            misc_recv.at[3],
            (z, 4 * y + u, core),
        )
    send_or_keep(
        first_here,
        first_out.at[y // 2],
        first_out_recv.at[x],
        misc_self.at[4],
        misc_recv.at[3],
        (z, 4 * y + y, core),
    )

    wait_for(vec8, spread_recv.at[7])
    vector = vec8[...].reshape(64, 256)
    vector9 = vector
    multiply(
        lambda j: [
            second_early[s, :, columns_of(j)] + dot(vector9, block(upper.at[s], j))
            for s in range(2)
        ],
        send9,
        recv9,
        8,
    )

    odd = y % 2 == 1
    wait_for(root_out_recv, misc_recv.at[2])
    value = root_out_recv[...].reshape(64, 128)
    sol_root[...] = jnp.where(odd, value[:, 64:128], value[:, 0:64])
    wait_for(first_out_recv, misc_recv.at[3])
    value = first_out_recv[...].reshape(64, 128)
    sol_half[0] = jnp.where(odd, value[:, 64:128], value[:, 0:64])

    wait_for(recv9, scatter_recv.at[8])
    part9[...] = (leaf_value[...] - add_up(recv9, 16)).astype(BF16)
    spread(part9, vec9, 8)

    wait_for(vec9, spread_recv.at[8])
    second1 = vec9[:, 0].reshape(64, 256)
    second2 = vec9[:, 1].reshape(64, 256)
    for dx in (2, 1, 3, 0):
        j = (x + dx) % 4
        value1 = dot(second1, block(upper_inverse.at[1], j))
        value2 = dot(second2, block(upper_inverse.at[2], j))
        for u in range(4):
            span = slice(64 * u, 64 * u + 64)
            send10[4 * j + u] = jnp.concatenate([value1[:, span], value2[:, span]], axis=1).astype(
                BF16
            )
        for dy in (2, 1, 3, 0):
            peer = 4 * j + (y + dy) % 4
            if dx or dy:
                send(
                    send10.at[peer],
                    recv10.at[col],
                    scatter_send.at[9],
                    scatter_recv.at[9],
                    (z, peer, core),
                )
            else:
                start_local(send10.at[peer], recv10.at[col], scatter_recv.at[9])
    wait_for(recv10, scatter_recv.at[9])
    total = add_up(recv10, 16)
    sol_half[1] = total[:, 0:64]
    sol_half[2] = total[:, 64:128]

    sends = (send1, send2, send3, None, send5, send6, send7, send8, send9, send10)
    for stage, ref in enumerate(sends):
        if ref is not None:
            wait_for(ref.at[pl.ds(0, 15)], scatter_send.at[stage])
    wait_for(recv4.at[0], scatter_send.at[3])
    wait_for(recv4.at[1, pl.ds(0, 15)], scatter_send.at[3])
    for stage, ref in enumerate((vec1, vec2, vec3, None, None, None, vec7, vec8, vec9)):
        if ref is not None:
            wait_for(ref.at[pl.ds(0, 3)], spread_send.at[stage])
            wait_sent_unless(x == z, ref.at[0], spread_self.at[stage])
    for stage, ref in ((3, vec4), (4, vec5), (5, vec6)):
        wait_for(ref.at[0], spread_send.at[stage])
        wait_for(ref.at[1, pl.ds(0, 3)], spread_send.at[stage])
        wait_sent_unless(x == z, ref.at[0, 0], spread_self.at[stage])
    wait_for(leaf_recv.at[pl.ds(0, 3)], misc_send.at[0])

    @pl.when(core == 0)
    def _():
        wait_for(leaf_recv, relay_sem.at[4])
        wait_sent_unless(leaf_here, leaf_recv.at[0], misc_self.at[0])

    @pl.when(core == 1)
    def _():
        wait_for(leaf_recv.at[0], misc_send.at[0])

    wait_for(bias_recv.at[pl.ds(0, 3)], misc_send.at[1])
    wait_sent_unless(bias_here, bias_recv.at[0], misc_self.at[1])
    wait_for(root_out_recv.at[pl.ds(0, 2)], misc_send.at[2])
    for k in range(2):
        wait_sent_unless(out_here(k, core), root_out_recv.at[0], misc_self.at[2 + k])
    wait_for(first_out_recv.at[pl.ds(0, 3)], misc_send.at[3])
    wait_sent_unless(first_here, first_out_recv.at[0], misc_self.at[4])


def per_device(
    rhs_half,
    rhs_root,
    lower_coupling,
    lower_pattern,
    upper_coupling,
    upper_pattern,
    lower_inverse,
    upper_inverse,
    root_lower_inverse,
    root_upper_inverse,
):
    vmem = pl.BlockSpec(memory_space=pltpu.VMEM)
    hbm = pl.BlockSpec(memory_space=pl.ANY)
    one = (16, 256)
    two = (2, 16, 256)
    half = (16, 128)
    stage_chunks = [two, one, one, None, half, half, one, one, two, (64, 128)]
    exchange = [
        pltpu.VMEM((2, 16) + half if chunk is None else (16,) + chunk, BF16)
        for chunk in stage_chunks
    ]
    part_chunks = [two, one, one, half, half, half, one, one, two]
    parts = [pltpu.VMEM(chunk, BF16) for chunk in part_chunks]
    vectors = [
        pltpu.VMEM((2, 4) + chunk if chunk == half else (4,) + chunk, BF16)
        for chunk in part_chunks
    ]
    scratch = [
        pltpu.VMEM((3, 64, 64), F32),
        pltpu.VMEM((64, 64), F32),
        pltpu.SMEM((5, 2, 8), jnp.int32),
        pltpu.SMEM((5, 2, 8), jnp.int32),
        pltpu.VMEM((5, 256, 1024), BF16),
        pltpu.VMEM((5, 256, 1024), BF16),
        pltpu.VMEM((3, 256, 1024), BF16),
        pltpu.VMEM((3, 256, 1024), BF16),
        pltpu.VMEM((256, 512), BF16),
        pltpu.VMEM((256, 512), BF16),
        pltpu.VMEM((64, 128), BF16),
        pltpu.VMEM((4, 64, 128), BF16),
        pltpu.VMEM((4, 64, 128), BF16),
        pltpu.VMEM((64, 128), F32),
        pltpu.VMEM((4, 16, 128), F32),
        *exchange,
        *exchange,
        *parts,
        *vectors,
        pltpu.VMEM(two, F32),
        pltpu.VMEM(one, F32),
        pltpu.VMEM((64, 1024), F32),
        pltpu.VMEM((2, 64, 1024), F32),
        pltpu.VMEM(half, F32),
        pltpu.VMEM((4,) + half, F32),
        pltpu.VMEM((2,) + half, F32),
        pltpu.VMEM((4,) + half, F32),
        pltpu.SemaphoreType.DMA((10,)),
        pltpu.SemaphoreType.DMA((10,)),
        pltpu.SemaphoreType.DMA((10,)),
        pltpu.SemaphoreType.DMA((9,)),
        pltpu.SemaphoreType.DMA((9,)),
        pltpu.SemaphoreType.DMA((9,)),
        pltpu.SemaphoreType.DMA((4,)),
        pltpu.SemaphoreType.DMA((4,)),
        pltpu.SemaphoreType.DMA((5,)),
        pltpu.SemaphoreType.DMA((5,)),
        pltpu.SemaphoreType.REGULAR,
        pltpu.SemaphoreType.REGULAR,
        pltpu.SemaphoreType.REGULAR,
    ]
    sol_half, sol_root = pl.pallas_call(
        kernel,
        name="tree_solve",
        out_shape=(pltpu.VMEM((3, 64, 64), F32), pltpu.VMEM((64, 64), F32)),
        in_specs=[hbm] * 10,
        out_specs=(vmem, vmem),
        scratch_shapes=scratch,
        compiler_params=pltpu.CompilerParams(collective_id=0, has_side_effects=True),
    )(
        rhs_half[0],
        rhs_root,
        lower_pattern[0],
        upper_pattern[0],
        lower_coupling[0],
        upper_coupling[0],
        lower_inverse[0],
        upper_inverse[0],
        root_lower_inverse,
        root_upper_inverse,
    )

    def leave(half_ref, root_ref, half_out, root_out, sems):
        first = pltpu.make_async_copy(half_ref, half_out, sems.at[0])
        second = pltpu.make_async_copy(root_ref, root_out, sems.at[1])
        first.start()
        second.start()
        first.wait()
        second.wait()

    sol_half, sol_root = pl.pallas_call(
        leave,
        name="leave",
        out_shape=(
            jax.ShapeDtypeStruct((3, 64, 64), F32),
            jax.ShapeDtypeStruct((64, 64), F32),
        ),
        in_specs=[vmem, vmem],
        out_specs=(hbm, hbm),
        scratch_shapes=[pltpu.SemaphoreType.DMA((2,))],
        compiler_params=pltpu.CompilerParams(vmem_limit_bytes=1 << 20),
    )(sol_half, sol_root)
    return (sol_half[None], sol_root)


def solution(mesh):
    in_specs = (
        P("gz", None, None, ("row", "col")),
        P(None, ("row", "col")),
        P("gz", None, "col", "row"),
        P("gz", None, "col", "row"),
        P("gz", None, "col", "row"),
        P("gz", None, "col", "row"),
        P("gz", None, "col", "row"),
        P("gz", None, "col", "row"),
        P("col", "row"),
        P("col", "row"),
    )
    out_specs = (P("gz", None, None, ("row", "col")), P(None, ("row", "col")))
    return jax.shard_map(
        per_device, mesh=mesh, in_specs=in_specs, out_specs=out_specs, check_vma=False
    )
```

```python
import jax
import jax.numpy as jnp
from jax import lax
from jax.experimental import pallas as pl
from jax.experimental.pallas import tpu as pltpu
from jax.sharding import PartitionSpec as P

MESH = pl.DeviceIdType.MESH
F32 = jnp.float32
BF16 = jnp.bfloat16

NEAR = sorted(
    ((dx, dy) for dx in range(4) for dy in range(4) if dx or dy),
    key=lambda d: -(min(d[0], 4 - d[0]) + min(d[1], 4 - d[1])),
)


def dot(vector, tiles):
    return jnp.dot(vector, tiles, preferred_element_type=F32)


def add_up(ref, count):
    total = ref[0].astype(F32)
    for i in range(1, count):
        total = total + ref[i].astype(F32)
    return total


def kernel(
    rhs_half_hbm,
    rhs_root_hbm,
    lower_pattern_hbm,
    upper_pattern_hbm,
    lower_hbm,
    upper_hbm,
    lower_inverse_hbm,
    upper_inverse_hbm,
    root_lower_hbm,
    root_upper_hbm,
    sol_half,
    sol_root,
    rhs_half,
    rhs_root,
    lower_pattern,
    upper_pattern,
    lower,
    upper,
    lower_inverse,
    upper_inverse,
    root_lower,
    root_upper,
    leaf_pack,
    leaf_recv,
    leaf_relay,
    bias_pack,
    bias_recv,
    send1,
    send2,
    send3,
    send4,
    send5,
    send6,
    send7,
    send8,
    send9,
    send10,
    recv1,
    recv2,
    recv3,
    recv4,
    recv5,
    recv6,
    recv7,
    recv8,
    recv9,
    recv10,
    part1,
    part2,
    part3,
    part4,
    part5,
    part6,
    part7,
    part8,
    part9,
    vec1,
    vec2,
    vec3,
    vec4,
    vec5,
    vec6,
    vec7,
    vec8,
    vec9,
    leaf_value,
    top_value,
    root_early,
    second_early,
    root_out,
    root_out_recv,
    first_out,
    first_out_recv,
    weight_sem,
    scatter_send,
    scatter_recv,
    spread_send,
    spread_recv,
    spread_self,
    misc_send,
    misc_recv,
    misc_self,
    relay_sem,
    ready,
    go,
):
    z = lax.axis_index("row")
    col = lax.axis_index("col")
    core = lax.axis_index("gz")
    x = col // 4
    y = col % 4
    other = 1 - core

    def start_local(src, dst, sem):
        pltpu.make_async_copy(src, dst, sem).start()

    def wait_for(ref, sem):
        pltpu.make_async_copy(ref, ref, sem).wait()

    def send(src, dst, send_sem, recv_sem, device):
        pltpu.make_async_remote_copy(
            src_ref=src,
            dst_ref=dst,
            send_sem=send_sem,
            recv_sem=recv_sem,
            device_id=device,
            device_id_type=MESH,
        ).start()

    def send_or_keep(here, src, dst, send_sem, recv_sem, device):
        @pl.when(jnp.logical_not(here))
        def _():
            send(src, dst, send_sem, recv_sem, device)

        @pl.when(here)
        def _():
            start_local(src, dst, recv_sem)

    def wait_sent_unless(here, ref, sem):
        @pl.when(jnp.logical_not(here))
        def _():
            wait_for(ref, sem)

    barrier = pltpu.get_barrier_semaphore()

    def greet(px, py, pz, pcore):
        pl.semaphore_signal(
            barrier, inc=1, device_id=(pz, 4 * px + py, pcore), device_id_type=MESH
        )

    @pl.when(core == 0)
    def _():
        for u in range(4):
            greet(y, u, x, 1)
        for dz in (2, 1, 3):
            greet(z, y, (z + dz) % 4, 0)

        @pl.when(x != z)
        def _():
            for u in range(4):
                greet(y, u, x, 0)
                greet(u, y, x, 0)

        for dx, dy in NEAR:
            greet((x + dx) % 4, (y + dy) % 4, z, 0)

    @pl.when(core == 1)
    def _():
        greet(x, y, z, 0)

    start_local(rhs_half_hbm, rhs_half, weight_sem.at[6])
    start_local(rhs_root_hbm, rhs_root, weight_sem.at[7])
    start_local(lower_pattern_hbm, lower_pattern, weight_sem.at[8])
    start_local(upper_pattern_hbm, upper_pattern, weight_sem.at[9])
    start_local(lower_inverse_hbm, lower_inverse, weight_sem.at[0])
    start_local(lower_hbm, lower, weight_sem.at[1])
    for j in range(4):
        columns = pl.ds(pl.multiple_of(256 * j + 128 * core, 128), 128)
        start_local(
            root_lower_hbm.at[:, columns], root_lower.at[:, pl.ds(128 * j, 128)], weight_sem.at[2]
        )
    for j in range(4):
        columns = pl.ds(pl.multiple_of(256 * j + 128 * core, 128), 128)
        start_local(
            root_upper_hbm.at[:, columns], root_upper.at[:, pl.ds(128 * j, 128)], weight_sem.at[3]
        )
    start_local(upper_hbm, upper, weight_sem.at[4])
    start_local(upper_inverse_hbm, upper_inverse, weight_sem.at[5])

    wait_for(rhs_half, weight_sem.at[6])
    wait_for(rhs_root, weight_sem.at[7])
    leaf_pack[...] = jnp.concatenate([rhs_half[1], rhs_half[2]], axis=1).astype(BF16)
    bias_pack[...] = jnp.concatenate([rhs_half[0], rhs_root[...]], axis=1)

    def tell(px, py, pz):
        pl.semaphore_signal(ready, inc=1, device_id=(pz, 4 * px + py, 0), device_id_type=MESH)

    @pl.when(core == 0)
    def _():
        @pl.when(x == z)
        def _():
            pl.semaphore_wait(barrier, 15 + 3 + 3 + 1)

        @pl.when(x != z)
        def _():
            pl.semaphore_wait(barrier, 15 + 3 + 3 + 1 + 4)
            for u in range(4):
                tell(u, y, x)

        for dx, dy in NEAR:
            tell((x + dx) % 4, (y + dy) % 4, z)

    @pl.when(core == 1)
    def _():
        pl.semaphore_wait(barrier, 4)

    leaf_here = jnp.logical_and(x == z, x == y)

    @pl.when(core == 0)
    def _():
        for dz in (2, 1, 3):
            send(
                leaf_pack,
                leaf_recv.at[y],
                misc_send.at[0],
                misc_recv.at[0],
                ((z + dz) % 4, 4 * z + x, 0),
            )
        send_or_keep(
            leaf_here,
            leaf_pack,
            leaf_recv.at[y],
            misc_self.at[0],
            misc_recv.at[0],
            (z, 4 * z + x, 0),
        )

    @pl.when(core == 1)
    def _():
        for dz in (2, 1, 3, 0):
            send(
                leaf_pack,
                leaf_relay.at[y],
                misc_send.at[0],
                relay_sem.at[0],
                ((z + dz) % 4, 4 * z + x, 0),
            )

    def scatter(src, dst, stage):
        for dx, dy in NEAR:
            peer = 4 * ((x + dx) % 4) + (y + dy) % 4
            send(
                src.at[peer],
                dst.at[col],
                scatter_send.at[stage],
                scatter_recv.at[stage],
                (z, peer, core),
            )
        start_local(src.at[col], dst.at[col], scatter_recv.at[stage])

    def spread(src, dst, stage):
        for dz in (2, 1, 3):
            send(
                src,
                dst.at[x],
                spread_send.at[stage],
                spread_recv.at[stage],
                ((z + dz) % 4, 4 * z + y, core),
            )
        send_or_keep(
            x == z,
            src,
            dst.at[x],
            spread_self.at[stage],
            spread_recv.at[stage],
            (z, 4 * z + y, core),
        )

    def spread_both(src, dst, stage):
        for dz in (2, 1, 3):
            for to in (other, core):
                send(
                    src,
                    dst.at[core, x],
                    spread_send.at[stage],
                    spread_recv.at[stage],
                    ((z + dz) % 4, 4 * z + y, to),
                )
        send(
            src,
            dst.at[core, x],
            spread_send.at[stage],
            spread_recv.at[stage],
            (z, 4 * z + y, other),
        )
        send_or_keep(
            x == z,
            src,
            dst.at[core, x],
            spread_self.at[stage],
            spread_recv.at[stage],
            (z, 4 * z + y, core),
        )

    def mask(tiles, pattern):
        @pl.loop(0, 5)
        def _(p):
            for a in range(2):
                for b in range(8):
                    here = (p, pl.ds(128 * a, 128), pl.ds(128 * b, 128))
                    keep = jnp.full((128, 128), pattern[p, a, b].astype(F32), F32)
                    tiles[here] = tiles[here] * keep.astype(BF16)

    def columns_of(j):
        return pl.ds(pl.multiple_of(256 * j, 256), 256)

    def block(ref, j):
        return ref[:, columns_of(j)]

    def multiply(values_of, src, dst, stage):
        for dy in (2, 1, 3, 0):
            j = (y + dy) % 4
            values = values_of(j)
            for q in range(4):
                rows = [value[16 * q : 16 * q + 16].astype(BF16) for value in values]
                if len(rows) == 1:
                    src[4 * q + j] = rows[0]
                else:
                    for s in range(2):
                        src[4 * q + j, s] = rows[s]
            for dx in (2, 1, 3, 0):
                peer = 4 * ((x + dx) % 4) + j
                if dx or dy:
                    send(
                        src.at[peer],
                        dst.at[col],
                        scatter_send.at[stage],
                        scatter_recv.at[stage],
                        (z, peer, core),
                    )
                else:
                    start_local(src.at[peer], dst.at[col], scatter_recv.at[stage])

    wait_for(lower, weight_sem.at[1])
    wait_for(lower_pattern, weight_sem.at[8])
    mask(lower, lower_pattern)

    @pl.when(core == 0)
    def _():
        pl.semaphore_wait(ready, 15 + 3)
        pl.semaphore_signal(go, inc=1, device_id=(z, col, 1), device_id_type=MESH)

    @pl.when(core == 1)
    def _():
        pl.semaphore_wait(go, 1)

    bias_here = x == y
    for dq in (2, 1, 3):
        q = (x + dq) % 4
        send(
            bias_pack.at[pl.ds(pl.multiple_of(16 * q, 16), 16)],
            bias_recv.at[y],
            misc_send.at[1],
            misc_recv.at[1],
            (z, 4 * q + x, core),
        )
    own_rows = pl.ds(pl.multiple_of(16 * x, 16), 16)
    send_or_keep(
        bias_here,
        bias_pack.at[own_rows],
        bias_recv.at[y],
        misc_self.at[1],
        misc_recv.at[1],
        (z, 4 * x + x, core),
    )

    @pl.when(core == 0)
    def _():
        wait_for(leaf_relay, relay_sem.at[0])
        send(leaf_relay, leaf_recv, relay_sem.at[1], misc_recv.at[0], (z, col, 1))

    wait_for(leaf_recv, misc_recv.at[0])
    wait_for(lower_inverse, weight_sem.at[0])
    pieces = [leaf_recv[u].astype(F32) for u in range(4)]
    leaves = [
        jnp.concatenate([p[:, 64 * s : 64 * s + 64] for p in pieces], axis=1).astype(BF16)
        for s in range(2)
    ]
    multiply(
        lambda j: [dot(leaves[s], block(lower_inverse.at[1 + s], j)) for s in range(2)],
        send1,
        recv1,
        0,
    )
    wait_for(recv1, scatter_recv.at[0])
    leaf_value[...] = add_up(recv1, 16)
    part1[...] = leaf_value[...].astype(BF16)
    spread(part1, vec1, 0)

    wait_for(vec1, spread_recv.at[0])
    leaf1 = vec1[:, 0].reshape(64, 256)
    leaf2 = vec1[:, 1].reshape(64, 256)
    multiply(
        lambda j: [dot(leaf1, block(lower.at[0], j)) + dot(leaf2, block(lower.at[1], j))],
        send2,
        recv2,
        1,
    )
    for j in range(4):
        root_early[:, 256 * j : 256 * j + 256] = dot(leaf1, block(lower.at[3], j)) + dot(
            leaf2, block(lower.at[4], j)
        )
    wait_for(bias_recv, misc_recv.at[1])
    top_bias = jnp.concatenate([bias_recv[u][:, 0:64] for u in range(4)], axis=1)
    wait_for(recv2, scatter_recv.at[1])
    part2[...] = (top_bias - add_up(recv2, 16)).astype(BF16)
    spread(part2, vec2, 1)

    wait_for(vec2, spread_recv.at[1])
    vector = vec2[...].reshape(64, 256)
    vector3 = vector
    multiply(lambda j: [dot(vector3, block(lower_inverse.at[0], j))], send3, recv3, 2)
    wait_for(recv3, scatter_recv.at[2])
    top_value[...] = add_up(recv3, 16)
    part3[...] = top_value[...].astype(BF16)
    spread(part3, vec3, 2)

    wait_for(vec3, spread_recv.at[2])
    vector = vec3[...].reshape(64, 256)
    for dy in (2, 1, 3, 0):
        j = (y + dy) % 4
        value = root_early[:, columns_of(j)] + dot(vector, block(lower.at[2], j))
        for half in range(2):
            for q in range(4):
                send4[half, 4 * q + j] = value[
                    16 * q : 16 * q + 16, 128 * half : 128 * half + 128
                ].astype(BF16)
        for dx in (2, 1, 3, 0):
            peer = 4 * ((x + dx) % 4) + j
            for to in (other, core):
                if dx or dy or to is other:
                    send(
                        send4.at[to, peer],
                        recv4.at[core, col],
                        scatter_send.at[3],
                        scatter_recv.at[3],
                        (z, peer, to),
                    )
                else:
                    start_local(send4.at[to, peer], recv4.at[core, col], scatter_recv.at[3])
    root_bias = jnp.concatenate(
        [bias_recv[2 * core][:, 64:128], bias_recv[2 * core + 1][:, 64:128]], axis=1
    )
    wait_for(upper, weight_sem.at[4])
    wait_for(upper_pattern, weight_sem.at[9])
    mask(upper, upper_pattern)
    wait_for(recv4, scatter_recv.at[3])
    part4[...] = (root_bias - add_up(recv4.at[0], 16) - add_up(recv4.at[1], 16)).astype(BF16)
    spread_both(part4, vec4, 3)

    def whole(ref):
        return jnp.concatenate([ref[0].reshape(64, 128), ref[1].reshape(64, 128)], axis=1)

    def halves(ref, vector, tiles):
        for pair in range(2):
            value = dot(vector, tiles[:, 256 * pair : 256 * pair + 256])
            for k in range(2):
                for q in range(4):
                    ref[4 * q + 2 * pair + k] = value[
                        16 * q : 16 * q + 16, 128 * k : 128 * k + 128
                    ].astype(BF16)

    wait_for(root_lower, weight_sem.at[2])
    wait_for(vec4, spread_recv.at[3])
    halves(send5, whole(vec4), root_lower)
    scatter(send5, recv5, 4)
    wait_for(recv5, scatter_recv.at[4])
    part5[...] = add_up(recv5, 16).astype(BF16)
    spread_both(part5, vec5, 4)
    wait_for(root_upper, weight_sem.at[3])
    wait_for(vec5, spread_recv.at[4])
    halves(send6, whole(vec5), root_upper)
    scatter(send6, recv6, 5)
    wait_for(recv6, scatter_recv.at[5])
    root_out[...] = add_up(recv6, 16)
    part6[...] = root_out[...].astype(BF16)
    spread_both(part6, vec6, 5)

    def out_here(k, to):
        return jnp.logical_and(jnp.logical_and(x == y, 2 * core + k == y), to == core)

    for k in range(2):
        owner = 4 * y + 2 * core + k
        send(root_out, root_out_recv.at[x], misc_send.at[2], misc_recv.at[2], (z, owner, other))
        send_or_keep(
            out_here(k, core),
            root_out,
            root_out_recv.at[x],
            misc_self.at[2 + k],
            misc_recv.at[2],
            (z, owner, core),
        )

    wait_for(vec6, spread_recv.at[5])
    vector = whole(vec6)
    vector7 = vector
    multiply(lambda j: [dot(vector7, block(upper.at[2], j))], send7, recv7, 6)
    for s in range(2):
        for j in range(4):
            second_early[s, :, 256 * j : 256 * j + 256] = dot(vector, block(upper.at[3 + s], j))
    wait_for(recv7, scatter_recv.at[6])
    part7[...] = (top_value[...] - add_up(recv7, 16)).astype(BF16)
    spread(part7, vec7, 6)

    wait_for(upper_inverse, weight_sem.at[5])
    wait_for(vec7, spread_recv.at[6])
    vector = vec7[...].reshape(64, 256)
    vector8 = vector
    multiply(lambda j: [dot(vector8, block(upper_inverse.at[0], j))], send8, recv8, 7)
    wait_for(recv8, scatter_recv.at[7])
    first = add_up(recv8, 16)
    part8[...] = first.astype(BF16)
    spread(part8, vec8, 7)
    first_out[0] = first[:, 0:128]
    first_out[1] = first[:, 128:256]
    first_here = x == y
    for du in (2, 1, 3):
        u = (y + du) % 4
        send(
            first_out.at[u // 2],
            first_out_recv.at[x],
            misc_send.at[3],
            misc_recv.at[3],
            (z, 4 * y + u, core),
        )
    send_or_keep(
        first_here,
        first_out.at[y // 2],
        first_out_recv.at[x],
        misc_self.at[4],
        misc_recv.at[3],
        (z, 4 * y + y, core),
    )

    wait_for(vec8, spread_recv.at[7])
    vector = vec8[...].reshape(64, 256)
    vector9 = vector
    for s in range(2):
        multiply(
            lambda j, s=s: [
                second_early[s, :, columns_of(j)] + dot(vector9, block(upper.at[s], j))
            ],
            send9.at[s],
            recv9.at[s],
            8 + 2 * s,
        )

    odd = y % 2 == 1
    wait_for(root_out_recv, misc_recv.at[2])
    value = root_out_recv[...].reshape(64, 128)
    sol_root[...] = jnp.where(odd, value[:, 64:128], value[:, 0:64])
    wait_for(first_out_recv, misc_recv.at[3])
    value = first_out_recv[...].reshape(64, 128)
    sol_half[0] = jnp.where(odd, value[:, 64:128], value[:, 0:64])

    for s in range(2):
        wait_for(recv9.at[s], scatter_recv.at[8 + 2 * s])
        part9[s] = (leaf_value[s] - add_up(recv9.at[s], 16)).astype(BF16)
        spread(part9.at[s], vec9.at[s], 8 + s)

    for s in range(2):
        wait_for(vec9.at[s], spread_recv.at[8 + s])
        vector = vec9[s].reshape(64, 256)
        for dx in (2, 1, 3, 0):
            j = (x + dx) % 4
            value = dot(vector, block(upper_inverse.at[1 + s], j))
            for u in range(4):
                span = slice(64 * u, 64 * u + 64)
                send10[s, 4 * j + u] = jnp.concatenate(
                    [value[0:32, span], value[32:64, span]], axis=1
                ).astype(BF16)
            for dy in (2, 1, 3, 0):
                peer = 4 * j + (y + dy) % 4
                if dx or dy:
                    send(
                        send10.at[s, peer],
                        recv10.at[s, col],
                        scatter_send.at[9 + 2 * s],
                        scatter_recv.at[9 + 2 * s],
                        (z, peer, core),
                    )
                else:
                    start_local(
                        send10.at[s, peer], recv10.at[s, col], scatter_recv.at[9 + 2 * s]
                    )
    for s in range(2):
        wait_for(recv10.at[s], scatter_recv.at[9 + 2 * s])
        total = add_up(recv10.at[s], 16)
        sol_half[1 + s, 0:32] = total[:, 0:64]
        sol_half[1 + s, 32:64] = total[:, 64:128]

    sends = (send1, send2, send3, None, send5, send6, send7, send8)
    for stage, ref in enumerate(sends):
        if ref is not None:
            wait_for(ref.at[pl.ds(0, 15)], scatter_send.at[stage])
    wait_for(recv4.at[0], scatter_send.at[3])
    wait_for(recv4.at[1, pl.ds(0, 15)], scatter_send.at[3])
    for s in range(2):
        wait_for(send9.at[s, pl.ds(0, 15)], scatter_send.at[8 + 2 * s])
        wait_for(send10.at[s, pl.ds(0, 15)], scatter_send.at[9 + 2 * s])
        wait_for(vec9.at[s, pl.ds(0, 3)], spread_send.at[8 + s])
        wait_sent_unless(x == z, vec9.at[s, 0], spread_self.at[8 + s])
    for stage, ref in enumerate((vec1, vec2, vec3, None, None, None, vec7, vec8)):
        if ref is not None:
            wait_for(ref.at[pl.ds(0, 3)], spread_send.at[stage])
            wait_sent_unless(x == z, ref.at[0], spread_self.at[stage])
    for stage, ref in ((3, vec4), (4, vec5), (5, vec6)):
        wait_for(ref.at[0], spread_send.at[stage])
        wait_for(ref.at[1, pl.ds(0, 3)], spread_send.at[stage])
        wait_sent_unless(x == z, ref.at[0, 0], spread_self.at[stage])
    wait_for(leaf_recv.at[pl.ds(0, 3)], misc_send.at[0])

    @pl.when(core == 0)
    def _():
        wait_for(leaf_recv, relay_sem.at[1])
        wait_sent_unless(leaf_here, leaf_recv.at[0], misc_self.at[0])

    @pl.when(core == 1)
    def _():
        wait_for(leaf_recv.at[0], misc_send.at[0])

    wait_for(bias_recv.at[pl.ds(0, 3)], misc_send.at[1])
    wait_sent_unless(bias_here, bias_recv.at[0], misc_self.at[1])
    wait_for(root_out_recv.at[pl.ds(0, 2)], misc_send.at[2])
    for k in range(2):
        wait_sent_unless(out_here(k, core), root_out_recv.at[0], misc_self.at[2 + k])
    wait_for(first_out_recv.at[pl.ds(0, 3)], misc_send.at[3])
    wait_sent_unless(first_here, first_out_recv.at[0], misc_self.at[4])


def per_device(
    rhs_half,
    rhs_root,
    lower_coupling,
    lower_pattern,
    upper_coupling,
    upper_pattern,
    lower_inverse,
    upper_inverse,
    root_lower_inverse,
    root_upper_inverse,
):
    vmem = pl.BlockSpec(memory_space=pltpu.VMEM)
    hbm = pl.BlockSpec(memory_space=pl.ANY)
    one = (16, 256)
    two = (2, 16, 256)
    half = (16, 128)
    stage_chunks = [
        (16,) + two,
        (16,) + one,
        (16,) + one,
        (2, 16) + half,
        (16,) + half,
        (16,) + half,
        (16,) + one,
        (16,) + one,
        (2, 16) + one,
        (2, 16, 32, 128),
    ]
    exchange = [pltpu.VMEM(chunk, BF16) for chunk in stage_chunks]
    part_chunks = [two, one, one, half, half, half, one, one, two]
    parts = [pltpu.VMEM(chunk, BF16) for chunk in part_chunks]
    vectors = [
        pltpu.VMEM((2, 4) + chunk if chunk == half else (4,) + chunk, BF16)
        for chunk in part_chunks[:8]
    ] + [pltpu.VMEM((2, 4) + one, BF16)]
    scratch = [
        pltpu.VMEM((3, 64, 64), F32),
        pltpu.VMEM((64, 64), F32),
        pltpu.SMEM((5, 2, 8), jnp.int32),
        pltpu.SMEM((5, 2, 8), jnp.int32),
        pltpu.VMEM((5, 256, 1024), BF16),
        pltpu.VMEM((5, 256, 1024), BF16),
        pltpu.VMEM((3, 256, 1024), BF16),
        pltpu.VMEM((3, 256, 1024), BF16),
        pltpu.VMEM((256, 512), BF16),
        pltpu.VMEM((256, 512), BF16),
        pltpu.VMEM((64, 128), BF16),
        pltpu.VMEM((4, 64, 128), BF16),
        pltpu.VMEM((4, 64, 128), BF16),
        pltpu.VMEM((64, 128), F32),
        pltpu.VMEM((4, 16, 128), F32),
        *exchange,
        *exchange,
        *parts,
        *vectors,
        pltpu.VMEM(two, F32),
        pltpu.VMEM(one, F32),
        pltpu.VMEM((64, 1024), F32),
        pltpu.VMEM((2, 64, 1024), F32),
        pltpu.VMEM(half, F32),
        pltpu.VMEM((4,) + half, F32),
        pltpu.VMEM((2,) + half, F32),
        pltpu.VMEM((4,) + half, F32),
        pltpu.SemaphoreType.DMA((10,)),
        pltpu.SemaphoreType.DMA((12,)),
        pltpu.SemaphoreType.DMA((12,)),
        pltpu.SemaphoreType.DMA((10,)),
        pltpu.SemaphoreType.DMA((10,)),
        pltpu.SemaphoreType.DMA((10,)),
        pltpu.SemaphoreType.DMA((4,)),
        pltpu.SemaphoreType.DMA((4,)),
        pltpu.SemaphoreType.DMA((5,)),
        pltpu.SemaphoreType.DMA((2,)),
        pltpu.SemaphoreType.REGULAR,
        pltpu.SemaphoreType.REGULAR,
    ]
    sol_half, sol_root = pl.pallas_call(
        kernel,
        name="tree_solve",
        out_shape=(pltpu.VMEM((3, 64, 64), F32), pltpu.VMEM((64, 64), F32)),
        in_specs=[hbm] * 10,
        out_specs=(vmem, vmem),
        scratch_shapes=scratch,
        compiler_params=pltpu.CompilerParams(collective_id=0, has_side_effects=True),
    )(
        rhs_half[0],
        rhs_root,
        lower_pattern[0],
        upper_pattern[0],
        lower_coupling[0],
        upper_coupling[0],
        lower_inverse[0],
        upper_inverse[0],
        root_lower_inverse,
        root_upper_inverse,
    )

    def leave(half_ref, root_ref, half_out, root_out, sems):
        first = pltpu.make_async_copy(half_ref, half_out, sems.at[0])
        second = pltpu.make_async_copy(root_ref, root_out, sems.at[1])
        first.start()
        second.start()
        first.wait()
        second.wait()

    sol_half, sol_root = pl.pallas_call(
        leave,
        name="leave",
        out_shape=(
            jax.ShapeDtypeStruct((3, 64, 64), F32),
            jax.ShapeDtypeStruct((64, 64), F32),
        ),
        in_specs=[vmem, vmem],
        out_specs=(hbm, hbm),
        scratch_shapes=[pltpu.SemaphoreType.DMA((2,))],
        compiler_params=pltpu.CompilerParams(vmem_limit_bytes=1 << 20),
    )(sol_half, sol_root)
    return (sol_half[None], sol_root)


def solution(mesh):
    in_specs = (
        P("gz", None, None, ("row", "col")),
        P(None, ("row", "col")),
        P("gz", None, "col", "row"),
        P("gz", None, "col", "row"),
        P("gz", None, "col", "row"),
        P("gz", None, "col", "row"),
        P("gz", None, "col", "row"),
        P("gz", None, "col", "row"),
        P("col", "row"),
        P("col", "row"),
    )
    out_specs = (P("gz", None, None, ("row", "col")), P(None, ("row", "col")))
    return jax.shard_map(
        per_device, mesh=mesh, in_specs=in_specs, out_specs=out_specs, check_vma=False
    )
```

```python
import jax
import jax.numpy as jnp
from jax import lax
from jax.experimental import pallas as pl
from jax.experimental.pallas import tpu as pltpu
from jax.sharding import PartitionSpec as P

MESH = pl.DeviceIdType.MESH
F32 = jnp.float32
BF16 = jnp.bfloat16

NEAR = sorted(
    ((dx, dy) for dx in range(4) for dy in range(4) if dx or dy),
    key=lambda d: -(min(d[0], 4 - d[0]) + min(d[1], 4 - d[1])),
)


def dot(vector, tiles):
    return jnp.dot(vector, tiles, preferred_element_type=F32)


def add_up(ref, count):
    total = ref[0].astype(F32)
    for i in range(1, count):
        total = total + ref[i].astype(F32)
    return total


def kernel(
    rhs_half_hbm,
    rhs_root_hbm,
    lower_pattern_hbm,
    upper_pattern_hbm,
    lower_hbm,
    upper_hbm,
    lower_inverse_hbm,
    upper_inverse_hbm,
    root_lower_hbm,
    root_upper_hbm,
    sol_half,
    sol_root,
    rhs_half,
    rhs_root,
    lower_pattern,
    upper_pattern,
    lower,
    upper,
    lower_inverse,
    upper_inverse,
    root_lower,
    root_upper,
    leaf_pack,
    leaf_recv,
    leaf_relay,
    bias_pack,
    bias_recv,
    send1,
    send2,
    send3,
    send4,
    send5,
    send6,
    send7,
    send8,
    send9,
    send10,
    recv1,
    recv2,
    recv3,
    recv4,
    recv5,
    recv6,
    recv7,
    recv8,
    recv9,
    recv10,
    part1,
    part2,
    part3,
    part4,
    part5,
    part6,
    part7,
    part8,
    part9,
    vec1,
    vec2,
    vec3,
    vec4,
    vec5,
    vec6,
    vec7,
    vec8,
    vec9,
    leaf_value,
    top_value,
    top_early,
    root_early,
    second_early,
    root_out,
    root_out_recv,
    first_out,
    first_out_recv,
    weight_sem,
    scatter_send,
    scatter_recv,
    spread_send,
    spread_recv,
    spread_self,
    misc_send,
    misc_recv,
    misc_self,
    relay_sem,
    ready,
    go,
):
    z = lax.axis_index("row")
    col = lax.axis_index("col")
    core = lax.axis_index("gz")
    x = col // 4
    y = col % 4
    other = 1 - core

    def start_local(src, dst, sem):
        pltpu.make_async_copy(src, dst, sem).start()

    def wait_for(ref, sem):
        pltpu.make_async_copy(ref, ref, sem).wait()

    def send(src, dst, send_sem, recv_sem, device):
        pltpu.make_async_remote_copy(
            src_ref=src,
            dst_ref=dst,
            send_sem=send_sem,
            recv_sem=recv_sem,
            device_id=device,
            device_id_type=MESH,
        ).start()

    def send_or_keep(here, src, dst, send_sem, recv_sem, device):
        @pl.when(jnp.logical_not(here))
        def _():
            send(src, dst, send_sem, recv_sem, device)

        @pl.when(here)
        def _():
            start_local(src, dst, recv_sem)

    def wait_sent_unless(here, ref, sem):
        @pl.when(jnp.logical_not(here))
        def _():
            wait_for(ref, sem)

    barrier = pltpu.get_barrier_semaphore()

    def greet(px, py, pz, pcore):
        pl.semaphore_signal(
            barrier, inc=1, device_id=(pz, 4 * px + py, pcore), device_id_type=MESH
        )

    @pl.when(core == 0)
    def _():
        for u in range(4):
            greet(y, u, x, 1)
        for dz in (2, 1, 3):
            greet(z, y, (z + dz) % 4, 0)

        @pl.when(x != z)
        def _():
            for u in range(4):
                greet(y, u, x, 0)
                greet(u, y, x, 0)

        for dx, dy in NEAR:
            greet((x + dx) % 4, (y + dy) % 4, z, 0)

    @pl.when(core == 1)
    def _():
        greet(x, y, z, 0)

    start_local(rhs_half_hbm, rhs_half, weight_sem.at[6])
    start_local(rhs_root_hbm, rhs_root, weight_sem.at[7])
    start_local(lower_pattern_hbm, lower_pattern, weight_sem.at[8])
    start_local(upper_pattern_hbm, upper_pattern, weight_sem.at[9])
    start_local(lower_inverse_hbm, lower_inverse, weight_sem.at[0])
    start_local(lower_hbm, lower, weight_sem.at[1])
    for j in range(4):
        columns = pl.ds(pl.multiple_of(256 * j + 128 * core, 128), 128)
        start_local(
            root_lower_hbm.at[:, columns], root_lower.at[:, pl.ds(128 * j, 128)], weight_sem.at[2]
        )
    for j in range(4):
        columns = pl.ds(pl.multiple_of(256 * j + 128 * core, 128), 128)
        start_local(
            root_upper_hbm.at[:, columns], root_upper.at[:, pl.ds(128 * j, 128)], weight_sem.at[3]
        )
    start_local(upper_hbm, upper, weight_sem.at[4])
    start_local(upper_inverse_hbm, upper_inverse, weight_sem.at[5])

    wait_for(rhs_half, weight_sem.at[6])
    wait_for(rhs_root, weight_sem.at[7])
    leaf_pack[...] = jnp.concatenate([rhs_half[1], rhs_half[2]], axis=1).astype(BF16)
    bias_pack[...] = jnp.concatenate([rhs_half[0], rhs_root[...]], axis=1)

    def tell(px, py, pz):
        pl.semaphore_signal(ready, inc=1, device_id=(pz, 4 * px + py, 0), device_id_type=MESH)

    @pl.when(core == 0)
    def _():
        @pl.when(x == z)
        def _():
            pl.semaphore_wait(barrier, 15 + 3 + 3 + 1)

        @pl.when(x != z)
        def _():
            pl.semaphore_wait(barrier, 15 + 3 + 3 + 1 + 4)
            for u in range(4):
                tell(u, y, x)

        for dx, dy in NEAR:
            tell((x + dx) % 4, (y + dy) % 4, z)

    @pl.when(core == 1)
    def _():
        pl.semaphore_wait(barrier, 4)

    leaf_here = jnp.logical_and(x == z, x == y)

    @pl.when(core == 0)
    def _():
        for dz in (2, 1, 3):
            send(
                leaf_pack,
                leaf_recv.at[y],
                misc_send.at[0],
                misc_recv.at[0],
                ((z + dz) % 4, 4 * z + x, 0),
            )
        send_or_keep(
            leaf_here,
            leaf_pack,
            leaf_recv.at[y],
            misc_self.at[0],
            misc_recv.at[0],
            (z, 4 * z + x, 0),
        )

    @pl.when(core == 1)
    def _():
        for dz in (2, 1, 3, 0):
            send(
                leaf_pack,
                leaf_relay.at[y],
                misc_send.at[0],
                relay_sem.at[0],
                ((z + dz) % 4, 4 * z + x, 0),
            )

    def scatter(src, dst, stage):
        for dx, dy in NEAR:
            peer = 4 * ((x + dx) % 4) + (y + dy) % 4
            send(
                src.at[peer],
                dst.at[col],
                scatter_send.at[stage],
                scatter_recv.at[stage],
                (z, peer, core),
            )
        start_local(src.at[col], dst.at[col], scatter_recv.at[stage])

    def spread(src, dst, stage):
        for dz in (2, 1, 3):
            send(
                src,
                dst.at[x],
                spread_send.at[stage],
                spread_recv.at[stage],
                ((z + dz) % 4, 4 * z + y, core),
            )
        send_or_keep(
            x == z,
            src,
            dst.at[x],
            spread_self.at[stage],
            spread_recv.at[stage],
            (z, 4 * z + y, core),
        )

    def spread_both(src, dst, stage):
        for dz in (2, 1, 3):
            for to in (other, core):
                send(
                    src,
                    dst.at[core, x],
                    spread_send.at[stage],
                    spread_recv.at[stage],
                    ((z + dz) % 4, 4 * z + y, to),
                )
        send(
            src,
            dst.at[core, x],
            spread_send.at[stage],
            spread_recv.at[stage],
            (z, 4 * z + y, other),
        )
        send_or_keep(
            x == z,
            src,
            dst.at[core, x],
            spread_self.at[stage],
            spread_recv.at[stage],
            (z, 4 * z + y, core),
        )

    def mask(tiles, pattern):
        @pl.loop(0, 5)
        def _(p):
            for a in range(2):
                for b in range(8):
                    here = (p, pl.ds(128 * a, 128), pl.ds(128 * b, 128))
                    keep = jnp.full((128, 128), pattern[p, a, b].astype(F32), F32)
                    tiles[here] = tiles[here] * keep.astype(BF16)

    def columns_of(j):
        return pl.ds(pl.multiple_of(256 * j, 256), 256)

    def block(ref, j):
        return ref[:, columns_of(j)]

    def multiply(values_of, src, dst, stage):
        for dy in (2, 1, 3, 0):
            j = (y + dy) % 4
            values = values_of(j)
            for q in range(4):
                rows = [value[16 * q : 16 * q + 16].astype(BF16) for value in values]
                if len(rows) == 1:
                    src[4 * q + j] = rows[0]
                else:
                    for s in range(2):
                        src[4 * q + j, s] = rows[s]
            for dx in (2, 1, 3, 0):
                peer = 4 * ((x + dx) % 4) + j
                if dx or dy:
                    send(
                        src.at[peer],
                        dst.at[col],
                        scatter_send.at[stage],
                        scatter_recv.at[stage],
                        (z, peer, core),
                    )
                else:
                    start_local(src.at[peer], dst.at[col], scatter_recv.at[stage])

    wait_for(lower, weight_sem.at[1])
    wait_for(lower_pattern, weight_sem.at[8])
    mask(lower, lower_pattern)

    @pl.when(core == 0)
    def _():
        pl.semaphore_wait(ready, 15 + 3)
        pl.semaphore_signal(go, inc=1, device_id=(z, col, 1), device_id_type=MESH)

    @pl.when(core == 1)
    def _():
        pl.semaphore_wait(go, 1)

    bias_here = x == y
    for dq in (2, 1, 3):
        q = (x + dq) % 4
        send(
            bias_pack.at[pl.ds(pl.multiple_of(16 * q, 16), 16)],
            bias_recv.at[y],
            misc_send.at[1],
            misc_recv.at[1],
            (z, 4 * q + x, core),
        )
    own_rows = pl.ds(pl.multiple_of(16 * x, 16), 16)
    send_or_keep(
        bias_here,
        bias_pack.at[own_rows],
        bias_recv.at[y],
        misc_self.at[1],
        misc_recv.at[1],
        (z, 4 * x + x, core),
    )

    @pl.when(core == 0)
    def _():
        wait_for(leaf_relay, relay_sem.at[0])
        send(leaf_relay, leaf_recv, relay_sem.at[1], misc_recv.at[0], (z, col, 1))

    wait_for(leaf_recv, misc_recv.at[0])
    wait_for(lower_inverse, weight_sem.at[0])
    pieces = [leaf_recv[u].astype(F32) for u in range(4)]
    leaves = [
        jnp.concatenate([p[:, 64 * s : 64 * s + 64] for p in pieces], axis=1).astype(BF16)
        for s in range(2)
    ]
    for s in range(2):
        multiply(
            lambda j, s=s: [dot(leaves[s], block(lower_inverse.at[1 + s], j))],
            send1.at[s],
            recv1.at[s],
            12 * s,
        )
    for s in range(2):
        wait_for(recv1.at[s], scatter_recv.at[12 * s])
        leaf_value[s] = add_up(recv1.at[s], 16)
        part1[s] = leaf_value[s].astype(BF16)
        spread(part1.at[s], vec1.at[s], 10 * s)

    wait_for(vec1.at[0], spread_recv.at[0])
    leaf1 = vec1[0].reshape(64, 256)
    for j in range(4):
        top_early[:, 256 * j : 256 * j + 256] = dot(leaf1, block(lower.at[0], j))
    wait_for(vec1.at[1], spread_recv.at[10])
    leaf2 = vec1[1].reshape(64, 256)
    multiply(
        lambda j: [top_early[:, columns_of(j)] + dot(leaf2, block(lower.at[1], j))],
        send2,
        recv2,
        1,
    )
    for j in range(4):
        root_early[:, 256 * j : 256 * j + 256] = dot(leaf1, block(lower.at[3], j)) + dot(
            leaf2, block(lower.at[4], j)
        )
    wait_for(bias_recv, misc_recv.at[1])
    top_bias = jnp.concatenate([bias_recv[u][:, 0:64] for u in range(4)], axis=1)
    wait_for(recv2, scatter_recv.at[1])
    part2[...] = (top_bias - add_up(recv2, 16)).astype(BF16)
    spread(part2, vec2, 1)

    wait_for(vec2, spread_recv.at[1])
    vector = vec2[...].reshape(64, 256)
    vector3 = vector
    multiply(lambda j: [dot(vector3, block(lower_inverse.at[0], j))], send3, recv3, 2)
    wait_for(recv3, scatter_recv.at[2])
    top_value[...] = add_up(recv3, 16)
    part3[...] = top_value[...].astype(BF16)
    spread(part3, vec3, 2)

    wait_for(vec3, spread_recv.at[2])
    vector = vec3[...].reshape(64, 256)
    for dy in (2, 1, 3, 0):
        j = (y + dy) % 4
        value = root_early[:, columns_of(j)] + dot(vector, block(lower.at[2], j))
        for half in range(2):
            for q in range(4):
                send4[half, 4 * q + j] = value[
                    16 * q : 16 * q + 16, 128 * half : 128 * half + 128
                ].astype(BF16)
        for dx in (2, 1, 3, 0):
            peer = 4 * ((x + dx) % 4) + j
            for to in (other, core):
                if dx or dy or to is other:
                    send(
                        send4.at[to, peer],
                        recv4.at[core, col],
                        scatter_send.at[3],
                        scatter_recv.at[3],
                        (z, peer, to),
                    )
                else:
                    start_local(send4.at[to, peer], recv4.at[core, col], scatter_recv.at[3])
    root_bias = jnp.concatenate(
        [bias_recv[2 * core][:, 64:128], bias_recv[2 * core + 1][:, 64:128]], axis=1
    )
    wait_for(upper, weight_sem.at[4])
    wait_for(upper_pattern, weight_sem.at[9])
    mask(upper, upper_pattern)
    wait_for(recv4, scatter_recv.at[3])
    part4[...] = (root_bias - add_up(recv4.at[0], 16) - add_up(recv4.at[1], 16)).astype(BF16)
    spread_both(part4, vec4, 3)

    def whole(ref):
        return jnp.concatenate([ref[0].reshape(64, 128), ref[1].reshape(64, 128)], axis=1)

    def halves(ref, vector, tiles):
        for pair in range(2):
            value = dot(vector, tiles[:, 256 * pair : 256 * pair + 256])
            for k in range(2):
                for q in range(4):
                    ref[4 * q + 2 * pair + k] = value[
                        16 * q : 16 * q + 16, 128 * k : 128 * k + 128
                    ].astype(BF16)

    wait_for(root_lower, weight_sem.at[2])
    wait_for(vec4, spread_recv.at[3])
    halves(send5, whole(vec4), root_lower)
    scatter(send5, recv5, 4)
    wait_for(recv5, scatter_recv.at[4])
    part5[...] = add_up(recv5, 16).astype(BF16)
    spread_both(part5, vec5, 4)
    wait_for(root_upper, weight_sem.at[3])
    wait_for(vec5, spread_recv.at[4])
    halves(send6, whole(vec5), root_upper)
    scatter(send6, recv6, 5)
    wait_for(recv6, scatter_recv.at[5])
    root_out[...] = add_up(recv6, 16)
    part6[...] = root_out[...].astype(BF16)
    spread_both(part6, vec6, 5)

    def out_here(k, to):
        return jnp.logical_and(jnp.logical_and(x == y, 2 * core + k == y), to == core)

    for k in range(2):
        owner = 4 * y + 2 * core + k
        send(root_out, root_out_recv.at[x], misc_send.at[2], misc_recv.at[2], (z, owner, other))
        send_or_keep(
            out_here(k, core),
            root_out,
            root_out_recv.at[x],
            misc_self.at[2 + k],
            misc_recv.at[2],
            (z, owner, core),
        )

    wait_for(vec6, spread_recv.at[5])
    vector = whole(vec6)
    vector7 = vector
    multiply(lambda j: [dot(vector7, block(upper.at[2], j))], send7, recv7, 6)
    for s in range(2):
        for j in range(4):
            second_early[s, :, 256 * j : 256 * j + 256] = dot(vector, block(upper.at[3 + s], j))
    wait_for(recv7, scatter_recv.at[6])
    part7[...] = (top_value[...] - add_up(recv7, 16)).astype(BF16)
    spread(part7, vec7, 6)

    wait_for(upper_inverse, weight_sem.at[5])
    wait_for(vec7, spread_recv.at[6])
    vector = vec7[...].reshape(64, 256)
    vector8 = vector
    multiply(lambda j: [dot(vector8, block(upper_inverse.at[0], j))], send8, recv8, 7)
    wait_for(recv8, scatter_recv.at[7])
    first = add_up(recv8, 16)
    part8[...] = first.astype(BF16)
    spread(part8, vec8, 7)
    first_out[0] = first[:, 0:128]
    first_out[1] = first[:, 128:256]
    first_here = x == y
    for du in (2, 1, 3):
        u = (y + du) % 4
        send(
            first_out.at[u // 2],
            first_out_recv.at[x],
            misc_send.at[3],
            misc_recv.at[3],
            (z, 4 * y + u, core),
        )
    send_or_keep(
        first_here,
        first_out.at[y // 2],
        first_out_recv.at[x],
        misc_self.at[4],
        misc_recv.at[3],
        (z, 4 * y + y, core),
    )

    wait_for(vec8, spread_recv.at[7])
    vector = vec8[...].reshape(64, 256)
    vector9 = vector
    for s in range(2):
        multiply(
            lambda j, s=s: [
                second_early[s, :, columns_of(j)] + dot(vector9, block(upper.at[s], j))
            ],
            send9.at[s],
            recv9.at[s],
            8 + 2 * s,
        )

    odd = y % 2 == 1
    wait_for(root_out_recv, misc_recv.at[2])
    value = root_out_recv[...].reshape(64, 128)
    sol_root[...] = jnp.where(odd, value[:, 64:128], value[:, 0:64])
    wait_for(first_out_recv, misc_recv.at[3])
    value = first_out_recv[...].reshape(64, 128)
    sol_half[0] = jnp.where(odd, value[:, 64:128], value[:, 0:64])

    for s in range(2):
        wait_for(recv9.at[s], scatter_recv.at[8 + 2 * s])
        part9[s] = (leaf_value[s] - add_up(recv9.at[s], 16)).astype(BF16)
        spread(part9.at[s], vec9.at[s], 8 + s)

    for s in range(2):
        wait_for(vec9.at[s], spread_recv.at[8 + s])
        vector = vec9[s].reshape(64, 256)
        for dx in (2, 1, 3, 0):
            j = (x + dx) % 4
            value = dot(vector, block(upper_inverse.at[1 + s], j))
            for u in range(4):
                span = slice(64 * u, 64 * u + 64)
                send10[s, 4 * j + u] = jnp.concatenate(
                    [value[0:32, span], value[32:64, span]], axis=1
                ).astype(BF16)
            for dy in (2, 1, 3, 0):
                peer = 4 * j + (y + dy) % 4
                if dx or dy:
                    send(
                        send10.at[s, peer],
                        recv10.at[s, col],
                        scatter_send.at[9 + 2 * s],
                        scatter_recv.at[9 + 2 * s],
                        (z, peer, core),
                    )
                else:
                    start_local(
                        send10.at[s, peer], recv10.at[s, col], scatter_recv.at[9 + 2 * s]
                    )
    for s in range(2):
        wait_for(recv10.at[s], scatter_recv.at[9 + 2 * s])
        total = add_up(recv10.at[s], 16)
        sol_half[1 + s, 0:32] = total[:, 0:64]
        sol_half[1 + s, 32:64] = total[:, 64:128]

    sends = (None, send2, send3, None, send5, send6, send7, send8)
    for stage, ref in enumerate(sends):
        if ref is not None:
            wait_for(ref.at[pl.ds(0, 15)], scatter_send.at[stage])
    wait_for(recv4.at[0], scatter_send.at[3])
    wait_for(recv4.at[1, pl.ds(0, 15)], scatter_send.at[3])
    for s in range(2):
        wait_for(send1.at[s, pl.ds(0, 15)], scatter_send.at[12 * s])
        wait_for(vec1.at[s, pl.ds(0, 3)], spread_send.at[10 * s])
        wait_sent_unless(x == z, vec1.at[s, 0], spread_self.at[10 * s])
        wait_for(send9.at[s, pl.ds(0, 15)], scatter_send.at[8 + 2 * s])
        wait_for(send10.at[s, pl.ds(0, 15)], scatter_send.at[9 + 2 * s])
        wait_for(vec9.at[s, pl.ds(0, 3)], spread_send.at[8 + s])
        wait_sent_unless(x == z, vec9.at[s, 0], spread_self.at[8 + s])
    for stage, ref in enumerate((None, vec2, vec3, None, None, None, vec7, vec8)):
        if ref is not None:
            wait_for(ref.at[pl.ds(0, 3)], spread_send.at[stage])
            wait_sent_unless(x == z, ref.at[0], spread_self.at[stage])
    for stage, ref in ((3, vec4), (4, vec5), (5, vec6)):
        wait_for(ref.at[0], spread_send.at[stage])
        wait_for(ref.at[1, pl.ds(0, 3)], spread_send.at[stage])
        wait_sent_unless(x == z, ref.at[0, 0], spread_self.at[stage])
    wait_for(leaf_recv.at[pl.ds(0, 3)], misc_send.at[0])

    @pl.when(core == 0)
    def _():
        wait_for(leaf_recv, relay_sem.at[1])
        wait_sent_unless(leaf_here, leaf_recv.at[0], misc_self.at[0])

    @pl.when(core == 1)
    def _():
        wait_for(leaf_recv.at[0], misc_send.at[0])

    wait_for(bias_recv.at[pl.ds(0, 3)], misc_send.at[1])
    wait_sent_unless(bias_here, bias_recv.at[0], misc_self.at[1])
    wait_for(root_out_recv.at[pl.ds(0, 2)], misc_send.at[2])
    for k in range(2):
        wait_sent_unless(out_here(k, core), root_out_recv.at[0], misc_self.at[2 + k])
    wait_for(first_out_recv.at[pl.ds(0, 3)], misc_send.at[3])
    wait_sent_unless(first_here, first_out_recv.at[0], misc_self.at[4])


def per_device(
    rhs_half,
    rhs_root,
    lower_coupling,
    lower_pattern,
    upper_coupling,
    upper_pattern,
    lower_inverse,
    upper_inverse,
    root_lower_inverse,
    root_upper_inverse,
):
    vmem = pl.BlockSpec(memory_space=pltpu.VMEM)
    hbm = pl.BlockSpec(memory_space=pl.ANY)
    one = (16, 256)
    two = (2, 16, 256)
    half = (16, 128)
    stage_chunks = [
        (2, 16) + one,
        (16,) + one,
        (16,) + one,
        (2, 16) + half,
        (16,) + half,
        (16,) + half,
        (16,) + one,
        (16,) + one,
        (2, 16) + one,
        (2, 16, 32, 128),
    ]
    exchange = [pltpu.VMEM(chunk, BF16) for chunk in stage_chunks]
    part_chunks = [two, one, one, half, half, half, one, one, two]
    parts = [pltpu.VMEM(chunk, BF16) for chunk in part_chunks]
    vectors = [
        pltpu.VMEM((2, 4) + chunk if chunk == half else (4,) + chunk, BF16)
        for chunk in part_chunks[1:8]
    ]
    vectors = [pltpu.VMEM((2, 4) + one, BF16), *vectors, pltpu.VMEM((2, 4) + one, BF16)]
    scratch = [
        pltpu.VMEM((3, 64, 64), F32),
        pltpu.VMEM((64, 64), F32),
        pltpu.SMEM((5, 2, 8), jnp.int32),
        pltpu.SMEM((5, 2, 8), jnp.int32),
        pltpu.VMEM((5, 256, 1024), BF16),
        pltpu.VMEM((5, 256, 1024), BF16),
        pltpu.VMEM((3, 256, 1024), BF16),
        pltpu.VMEM((3, 256, 1024), BF16),
        pltpu.VMEM((256, 512), BF16),
        pltpu.VMEM((256, 512), BF16),
        pltpu.VMEM((64, 128), BF16),
        pltpu.VMEM((4, 64, 128), BF16),
        pltpu.VMEM((4, 64, 128), BF16),
        pltpu.VMEM((64, 128), F32),
        pltpu.VMEM((4, 16, 128), F32),
        *exchange,
        *exchange,
        *parts,
        *vectors,
        pltpu.VMEM(two, F32),
        pltpu.VMEM(one, F32),
        pltpu.VMEM((64, 1024), F32),
        pltpu.VMEM((64, 1024), F32),
        pltpu.VMEM((2, 64, 1024), F32),
        pltpu.VMEM(half, F32),
        pltpu.VMEM((4,) + half, F32),
        pltpu.VMEM((2,) + half, F32),
        pltpu.VMEM((4,) + half, F32),
        pltpu.SemaphoreType.DMA((10,)),
        pltpu.SemaphoreType.DMA((13,)),
        pltpu.SemaphoreType.DMA((13,)),
        pltpu.SemaphoreType.DMA((11,)),
        pltpu.SemaphoreType.DMA((11,)),
        pltpu.SemaphoreType.DMA((11,)),
        pltpu.SemaphoreType.DMA((4,)),
        pltpu.SemaphoreType.DMA((4,)),
        pltpu.SemaphoreType.DMA((5,)),
        pltpu.SemaphoreType.DMA((2,)),
        pltpu.SemaphoreType.REGULAR,
        pltpu.SemaphoreType.REGULAR,
    ]
    sol_half, sol_root = pl.pallas_call(
        kernel,
        name="tree_solve",
        out_shape=(pltpu.VMEM((3, 64, 64), F32), pltpu.VMEM((64, 64), F32)),
        in_specs=[hbm] * 10,
        out_specs=(vmem, vmem),
        scratch_shapes=scratch,
        compiler_params=pltpu.CompilerParams(collective_id=0, has_side_effects=True),
    )(
        rhs_half[0],
        rhs_root,
        lower_pattern[0],
        upper_pattern[0],
        lower_coupling[0],
        upper_coupling[0],
        lower_inverse[0],
        upper_inverse[0],
        root_lower_inverse,
        root_upper_inverse,
    )

    def leave(half_ref, root_ref, half_out, root_out, sems):
        first = pltpu.make_async_copy(half_ref, half_out, sems.at[0])
        second = pltpu.make_async_copy(root_ref, root_out, sems.at[1])
        first.start()
        second.start()
        first.wait()
        second.wait()

    sol_half, sol_root = pl.pallas_call(
        leave,
        name="leave",
        out_shape=(
            jax.ShapeDtypeStruct((3, 64, 64), F32),
            jax.ShapeDtypeStruct((64, 64), F32),
        ),
        in_specs=[vmem, vmem],
        out_specs=(hbm, hbm),
        scratch_shapes=[pltpu.SemaphoreType.DMA((2,))],
        compiler_params=pltpu.CompilerParams(vmem_limit_bytes=1 << 20),
    )(sol_half, sol_root)
    return (sol_half[None], sol_root)


def solution(mesh):
    in_specs = (
        P("gz", None, None, ("row", "col")),
        P(None, ("row", "col")),
        P("gz", None, "col", "row"),
        P("gz", None, "col", "row"),
        P("gz", None, "col", "row"),
        P("gz", None, "col", "row"),
        P("gz", None, "col", "row"),
        P("gz", None, "col", "row"),
        P("col", "row"),
        P("col", "row"),
    )
    out_specs = (P("gz", None, None, ("row", "col")), P(None, ("row", "col")))
    return jax.shard_map(
        per_device, mesh=mesh, in_specs=in_specs, out_specs=out_specs, check_vma=False
    )
```

```python
import jax
import jax.numpy as jnp
from jax import lax
from jax.experimental import pallas as pl
from jax.experimental.pallas import tpu as pltpu
from jax.sharding import PartitionSpec as P

MESH = pl.DeviceIdType.MESH
F32 = jnp.float32
BF16 = jnp.bfloat16

NEAR = sorted(
    ((dx, dy) for dx in range(4) for dy in range(4) if dx or dy),
    key=lambda d: -(min(d[0], 4 - d[0]) + min(d[1], 4 - d[1])),
)


def dot(vector, tiles):
    return jnp.dot(vector, tiles, preferred_element_type=F32)


def add_up(ref, count):
    total = ref[0].astype(F32)
    for i in range(1, count):
        total = total + ref[i].astype(F32)
    return total


def kernel(
    rhs_half_hbm,
    rhs_root_hbm,
    lower_pattern_hbm,
    upper_pattern_hbm,
    lower_hbm,
    upper_hbm,
    lower_inverse_hbm,
    upper_inverse_hbm,
    root_lower_hbm,
    root_upper_hbm,
    sol_half,
    sol_root,
    rhs_half,
    rhs_root,
    lower_pattern,
    upper_pattern,
    lower,
    upper,
    lower_inverse,
    upper_inverse,
    root_lower,
    root_upper,
    leaf_pack,
    leaf_recv,
    leaf_relay,
    bias_pack,
    bias_recv,
    send1,
    send2,
    send3,
    send4,
    send5,
    send6,
    send7,
    send8,
    send9,
    send10,
    recv1,
    recv2,
    recv3,
    recv4,
    recv5,
    recv6,
    recv7,
    recv8,
    recv9,
    recv10,
    part1,
    part2,
    part3,
    part4,
    part5,
    part6,
    part7,
    part8,
    part9,
    vec1,
    vec2,
    vec3,
    vec4,
    vec5,
    vec6,
    vec7,
    vec8,
    vec9,
    leaf_value,
    top_value,
    top_early,
    root_early,
    second_early,
    root_out,
    root_out_recv,
    first_out,
    first_out_recv,
    weight_sem,
    scatter_send,
    scatter_recv,
    spread_send,
    spread_recv,
    spread_self,
    misc_send,
    misc_recv,
    misc_self,
    relay_sem,
    ready,
    go,
):
    z = lax.axis_index("row")
    col = lax.axis_index("col")
    core = lax.axis_index("gz")
    x = col // 4
    y = col % 4
    other = 1 - core

    def start_local(src, dst, sem):
        pltpu.make_async_copy(src, dst, sem).start()

    def wait_for(ref, sem):
        pltpu.make_async_copy(ref, ref, sem).wait()

    def send(src, dst, send_sem, recv_sem, device):
        pltpu.make_async_remote_copy(
            src_ref=src,
            dst_ref=dst,
            send_sem=send_sem,
            recv_sem=recv_sem,
            device_id=device,
            device_id_type=MESH,
        ).start()

    def send_or_keep(here, src, dst, send_sem, recv_sem, device):
        @pl.when(jnp.logical_not(here))
        def _():
            send(src, dst, send_sem, recv_sem, device)

        @pl.when(here)
        def _():
            start_local(src, dst, recv_sem)

    def wait_sent_unless(here, ref, sem):
        @pl.when(jnp.logical_not(here))
        def _():
            wait_for(ref, sem)

    barrier = pltpu.get_barrier_semaphore()

    def greet(px, py, pz, pcore):
        pl.semaphore_signal(
            barrier, inc=1, device_id=(pz, 4 * px + py, pcore), device_id_type=MESH
        )

    @pl.when(core == 0)
    def _():
        for u in range(4):
            greet(y, u, x, 1)
        for dz in (2, 1, 3):
            greet(z, y, (z + dz) % 4, 0)

        @pl.when(x != z)
        def _():
            for u in range(4):
                greet(y, u, x, 0)
                greet(u, y, x, 0)

        for dx, dy in NEAR:
            greet((x + dx) % 4, (y + dy) % 4, z, 0)

    @pl.when(core == 1)
    def _():
        greet(x, y, z, 0)

    start_local(rhs_half_hbm, rhs_half, weight_sem.at[6])
    start_local(rhs_root_hbm, rhs_root, weight_sem.at[7])
    start_local(lower_pattern_hbm, lower_pattern, weight_sem.at[8])
    start_local(upper_pattern_hbm, upper_pattern, weight_sem.at[9])
    start_local(lower_inverse_hbm, lower_inverse, weight_sem.at[0])
    start_local(lower_hbm, lower, weight_sem.at[1])
    for j in range(4):
        columns = pl.ds(pl.multiple_of(256 * j + 128 * core, 128), 128)
        start_local(
            root_lower_hbm.at[:, columns], root_lower.at[:, pl.ds(128 * j, 128)], weight_sem.at[2]
        )
    for j in range(4):
        columns = pl.ds(pl.multiple_of(256 * j + 128 * core, 128), 128)
        start_local(
            root_upper_hbm.at[:, columns], root_upper.at[:, pl.ds(128 * j, 128)], weight_sem.at[3]
        )
    start_local(upper_hbm, upper, weight_sem.at[4])
    start_local(upper_inverse_hbm, upper_inverse, weight_sem.at[5])

    wait_for(rhs_half, weight_sem.at[6])
    wait_for(rhs_root, weight_sem.at[7])
    leaf_pack[...] = jnp.concatenate([rhs_half[1], rhs_half[2]], axis=1).astype(BF16)
    bias_pack[...] = jnp.concatenate([rhs_half[0], rhs_root[...]], axis=1)

    def tell(px, py, pz):
        pl.semaphore_signal(ready, inc=1, device_id=(pz, 4 * px + py, 0), device_id_type=MESH)

    @pl.when(core == 0)
    def _():
        @pl.when(x == z)
        def _():
            pl.semaphore_wait(barrier, 15 + 3 + 3 + 1)

        @pl.when(x != z)
        def _():
            pl.semaphore_wait(barrier, 15 + 3 + 3 + 1 + 4)
            for u in range(4):
                tell(u, y, x)

        for dx, dy in NEAR:
            tell((x + dx) % 4, (y + dy) % 4, z)

    @pl.when(core == 1)
    def _():
        pl.semaphore_wait(barrier, 4)

    leaf_here = jnp.logical_and(x == z, x == y)

    @pl.when(core == 0)
    def _():
        for dz in (2, 1, 3):
            send(
                leaf_pack,
                leaf_recv.at[y],
                misc_send.at[0],
                misc_recv.at[0],
                ((z + dz) % 4, 4 * z + x, 0),
            )
        send_or_keep(
            leaf_here,
            leaf_pack,
            leaf_recv.at[y],
            misc_self.at[0],
            misc_recv.at[0],
            (z, 4 * z + x, 0),
        )

    @pl.when(core == 1)
    def _():
        for dz in (2, 1, 3, 0):
            send(
                leaf_pack,
                leaf_relay.at[y],
                misc_send.at[0],
                relay_sem.at[y],
                ((z + dz) % 4, 4 * z + x, 0),
            )

    def scatter(src, dst, stage):
        for dx, dy in NEAR:
            peer = 4 * ((x + dx) % 4) + (y + dy) % 4
            send(
                src.at[peer],
                dst.at[col],
                scatter_send.at[stage],
                scatter_recv.at[stage],
                (z, peer, core),
            )
        start_local(src.at[col], dst.at[col], scatter_recv.at[stage])

    def spread(src, dst, stage):
        for dz in (2, 1, 3):
            send(
                src,
                dst.at[x],
                spread_send.at[stage],
                spread_recv.at[stage],
                ((z + dz) % 4, 4 * z + y, core),
            )
        send_or_keep(
            x == z,
            src,
            dst.at[x],
            spread_self.at[stage],
            spread_recv.at[stage],
            (z, 4 * z + y, core),
        )

    def spread_both(src, dst, stage):
        for dz in (2, 1, 3):
            for to in (other, core):
                send(
                    src,
                    dst.at[core, x],
                    spread_send.at[stage],
                    spread_recv.at[stage],
                    ((z + dz) % 4, 4 * z + y, to),
                )
        send(
            src,
            dst.at[core, x],
            spread_send.at[stage],
            spread_recv.at[stage],
            (z, 4 * z + y, other),
        )
        send_or_keep(
            x == z,
            src,
            dst.at[core, x],
            spread_self.at[stage],
            spread_recv.at[stage],
            (z, 4 * z + y, core),
        )

    def mask(tiles, pattern):
        @pl.loop(0, 5)
        def _(p):
            for a in range(2):
                for b in range(8):
                    here = (p, pl.ds(128 * a, 128), pl.ds(128 * b, 128))
                    keep = jnp.full((128, 128), pattern[p, a, b].astype(F32), F32)
                    tiles[here] = tiles[here] * keep.astype(BF16)

    def columns_of(j):
        return pl.ds(pl.multiple_of(256 * j, 256), 256)

    def block(ref, j):
        return ref[:, columns_of(j)]

    def multiply(values_of, src, dst, stage):
        for dy in (2, 1, 3, 0):
            j = (y + dy) % 4
            values = values_of(j)
            for q in range(4):
                rows = [value[16 * q : 16 * q + 16].astype(BF16) for value in values]
                if len(rows) == 1:
                    src[4 * q + j] = rows[0]
                else:
                    for s in range(2):
                        src[4 * q + j, s] = rows[s]
            for dx in (2, 1, 3, 0):
                peer = 4 * ((x + dx) % 4) + j
                if dx or dy:
                    send(
                        src.at[peer],
                        dst.at[col],
                        scatter_send.at[stage],
                        scatter_recv.at[stage],
                        (z, peer, core),
                    )
                else:
                    start_local(src.at[peer], dst.at[col], scatter_recv.at[stage])

    wait_for(lower, weight_sem.at[1])
    wait_for(lower_pattern, weight_sem.at[8])
    mask(lower, lower_pattern)

    @pl.when(core == 0)
    def _():
        pl.semaphore_wait(ready, 15 + 3)
        pl.semaphore_signal(go, inc=1, device_id=(z, col, 1), device_id_type=MESH)

    @pl.when(core == 1)
    def _():
        pl.semaphore_wait(go, 1)

    bias_here = x == y
    for dq in (2, 1, 3):
        q = (x + dq) % 4
        send(
            bias_pack.at[pl.ds(pl.multiple_of(16 * q, 16), 16)],
            bias_recv.at[y],
            misc_send.at[1],
            misc_recv.at[1],
            (z, 4 * q + x, core),
        )
    own_rows = pl.ds(pl.multiple_of(16 * x, 16), 16)
    send_or_keep(
        bias_here,
        bias_pack.at[own_rows],
        bias_recv.at[y],
        misc_self.at[1],
        misc_recv.at[1],
        (z, 4 * x + x, core),
    )

    @pl.when(core == 0)
    def _():
        for u in range(4):
            wait_for(leaf_relay.at[u], relay_sem.at[u])
            send(leaf_relay.at[u], leaf_recv.at[u], relay_sem.at[4], misc_recv.at[0], (z, col, 1))

    wait_for(leaf_recv, misc_recv.at[0])
    wait_for(lower_inverse, weight_sem.at[0])
    pieces = [leaf_recv[u].astype(F32) for u in range(4)]
    leaves = [
        jnp.concatenate([p[:, 64 * s : 64 * s + 64] for p in pieces], axis=1).astype(BF16)
        for s in range(2)
    ]
    for s in range(2):
        multiply(
            lambda j, s=s: [dot(leaves[s], block(lower_inverse.at[1 + s], j))],
            send1.at[s],
            recv1.at[s],
            12 * s,
        )
    for s in range(2):
        wait_for(recv1.at[s], scatter_recv.at[12 * s])
        leaf_value[s] = add_up(recv1.at[s], 16)
        part1[s] = leaf_value[s].astype(BF16)
        spread(part1.at[s], vec1.at[s], 10 * s)

    wait_for(vec1.at[0], spread_recv.at[0])
    leaf1 = vec1[0].reshape(64, 256)
    for j in range(4):
        top_early[:, 256 * j : 256 * j + 256] = dot(leaf1, block(lower.at[0], j))
    wait_for(vec1.at[1], spread_recv.at[10])
    leaf2 = vec1[1].reshape(64, 256)
    multiply(
        lambda j: [top_early[:, columns_of(j)] + dot(leaf2, block(lower.at[1], j))],
        send2,
        recv2,
        1,
    )
    for j in range(4):
        root_early[:, 256 * j : 256 * j + 256] = dot(leaf1, block(lower.at[3], j)) + dot(
            leaf2, block(lower.at[4], j)
        )
    wait_for(bias_recv, misc_recv.at[1])
    top_bias = jnp.concatenate([bias_recv[u][:, 0:64] for u in range(4)], axis=1)
    wait_for(recv2, scatter_recv.at[1])
    part2[...] = (top_bias - add_up(recv2, 16)).astype(BF16)
    spread(part2, vec2, 1)

    wait_for(vec2, spread_recv.at[1])
    vector = vec2[...].reshape(64, 256)
    vector3 = vector
    multiply(lambda j: [dot(vector3, block(lower_inverse.at[0], j))], send3, recv3, 2)
    wait_for(recv3, scatter_recv.at[2])
    top_value[...] = add_up(recv3, 16)
    part3[...] = top_value[...].astype(BF16)
    spread(part3, vec3, 2)

    wait_for(vec3, spread_recv.at[2])
    vector = vec3[...].reshape(64, 256)
    for dy in (2, 1, 3, 0):
        j = (y + dy) % 4
        value = root_early[:, columns_of(j)] + dot(vector, block(lower.at[2], j))
        for half in range(2):
            for q in range(4):
                send4[half, 4 * q + j] = value[
                    16 * q : 16 * q + 16, 128 * half : 128 * half + 128
                ].astype(BF16)
        for dx in (2, 1, 3, 0):
            peer = 4 * ((x + dx) % 4) + j
            for to in (other, core):
                if dx or dy or to is other:
                    send(
                        send4.at[to, peer],
                        recv4.at[core, col],
                        scatter_send.at[3],
                        scatter_recv.at[3],
                        (z, peer, to),
                    )
                else:
                    start_local(send4.at[to, peer], recv4.at[core, col], scatter_recv.at[3])
    root_bias = jnp.concatenate(
        [bias_recv[2 * core][:, 64:128], bias_recv[2 * core + 1][:, 64:128]], axis=1
    )
    wait_for(upper, weight_sem.at[4])
    wait_for(upper_pattern, weight_sem.at[9])
    mask(upper, upper_pattern)
    wait_for(recv4, scatter_recv.at[3])
    part4[...] = (root_bias - add_up(recv4.at[0], 16) - add_up(recv4.at[1], 16)).astype(BF16)
    spread_both(part4, vec4, 3)

    def whole(ref):
        return jnp.concatenate([ref[0].reshape(64, 128), ref[1].reshape(64, 128)], axis=1)

    def halves(ref, vector, tiles):
        for pair in range(2):
            value = dot(vector, tiles[:, 256 * pair : 256 * pair + 256])
            for k in range(2):
                for q in range(4):
                    ref[4 * q + 2 * pair + k] = value[
                        16 * q : 16 * q + 16, 128 * k : 128 * k + 128
                    ].astype(BF16)

    wait_for(root_lower, weight_sem.at[2])
    wait_for(vec4, spread_recv.at[3])
    halves(send5, whole(vec4), root_lower)
    scatter(send5, recv5, 4)
    wait_for(recv5, scatter_recv.at[4])
    part5[...] = add_up(recv5, 16).astype(BF16)
    spread_both(part5, vec5, 4)
    wait_for(root_upper, weight_sem.at[3])
    wait_for(vec5, spread_recv.at[4])
    halves(send6, whole(vec5), root_upper)
    scatter(send6, recv6, 5)
    wait_for(recv6, scatter_recv.at[5])
    root_out[...] = add_up(recv6, 16)
    part6[...] = root_out[...].astype(BF16)
    spread_both(part6, vec6, 5)

    def out_here(k, to):
        return jnp.logical_and(jnp.logical_and(x == y, 2 * core + k == y), to == core)

    for k in range(2):
        owner = 4 * y + 2 * core + k
        send(root_out, root_out_recv.at[x], misc_send.at[2], misc_recv.at[2], (z, owner, other))
        send_or_keep(
            out_here(k, core),
            root_out,
            root_out_recv.at[x],
            misc_self.at[2 + k],
            misc_recv.at[2],
            (z, owner, core),
        )

    wait_for(vec6, spread_recv.at[5])
    vector = whole(vec6)
    vector7 = vector
    multiply(lambda j: [dot(vector7, block(upper.at[2], j))], send7, recv7, 6)
    for s in range(2):
        for j in range(4):
            second_early[s, :, 256 * j : 256 * j + 256] = dot(vector, block(upper.at[3 + s], j))
    wait_for(recv7, scatter_recv.at[6])
    part7[...] = (top_value[...] - add_up(recv7, 16)).astype(BF16)
    spread(part7, vec7, 6)

    wait_for(upper_inverse, weight_sem.at[5])
    wait_for(vec7, spread_recv.at[6])
    vector = vec7[...].reshape(64, 256)
    vector8 = vector
    multiply(lambda j: [dot(vector8, block(upper_inverse.at[0], j))], send8, recv8, 7)
    wait_for(recv8, scatter_recv.at[7])
    first = add_up(recv8, 16)
    part8[...] = first.astype(BF16)
    spread(part8, vec8, 7)
    first_out[0] = first[:, 0:128]
    first_out[1] = first[:, 128:256]
    first_here = x == y
    for du in (2, 1, 3):
        u = (y + du) % 4
        send(
            first_out.at[u // 2],
            first_out_recv.at[x],
            misc_send.at[3],
            misc_recv.at[3],
            (z, 4 * y + u, core),
        )
    send_or_keep(
        first_here,
        first_out.at[y // 2],
        first_out_recv.at[x],
        misc_self.at[4],
        misc_recv.at[3],
        (z, 4 * y + y, core),
    )

    wait_for(vec8, spread_recv.at[7])
    vector = vec8[...].reshape(64, 256)
    vector9 = vector
    for s in range(2):
        multiply(
            lambda j, s=s: [
                second_early[s, :, columns_of(j)] + dot(vector9, block(upper.at[s], j))
            ],
            send9.at[s],
            recv9.at[s],
            8 + 2 * s,
        )

    odd = y % 2 == 1
    wait_for(root_out_recv, misc_recv.at[2])
    value = root_out_recv[...].reshape(64, 128)
    sol_root[...] = jnp.where(odd, value[:, 64:128], value[:, 0:64])
    wait_for(first_out_recv, misc_recv.at[3])
    value = first_out_recv[...].reshape(64, 128)
    sol_half[0] = jnp.where(odd, value[:, 64:128], value[:, 0:64])

    for s in range(2):
        wait_for(recv9.at[s], scatter_recv.at[8 + 2 * s])
        part9[s] = (leaf_value[s] - add_up(recv9.at[s], 16)).astype(BF16)
        spread(part9.at[s], vec9.at[s], 8 + s)

    for s in range(2):
        wait_for(vec9.at[s], spread_recv.at[8 + s])
        vector = vec9[s].reshape(64, 256)
        for dx in (2, 1, 3, 0):
            j = (x + dx) % 4
            value = dot(vector, block(upper_inverse.at[1 + s], j))
            for u in range(4):
                span = slice(64 * u, 64 * u + 64)
                send10[s, 4 * j + u] = jnp.concatenate(
                    [value[0:32, span], value[32:64, span]], axis=1
                ).astype(BF16)
            for dy in (2, 1, 3, 0):
                peer = 4 * j + (y + dy) % 4
                if dx or dy:
                    send(
                        send10.at[s, peer],
                        recv10.at[s, col],
                        scatter_send.at[9 + 2 * s],
                        scatter_recv.at[9 + 2 * s],
                        (z, peer, core),
                    )
                else:
                    start_local(
                        send10.at[s, peer], recv10.at[s, col], scatter_recv.at[9 + 2 * s]
                    )
    sends = (None, send2, send3, None, send5, send6, send7, send8)
    for stage, ref in enumerate(sends):
        if ref is not None:
            wait_for(ref.at[pl.ds(0, 15)], scatter_send.at[stage])
    wait_for(recv4.at[0], scatter_send.at[3])
    wait_for(recv4.at[1, pl.ds(0, 15)], scatter_send.at[3])
    for s in range(2):
        wait_for(send1.at[s, pl.ds(0, 15)], scatter_send.at[12 * s])
        wait_for(vec1.at[s, pl.ds(0, 3)], spread_send.at[10 * s])
        wait_sent_unless(x == z, vec1.at[s, 0], spread_self.at[10 * s])
        wait_for(send9.at[s, pl.ds(0, 15)], scatter_send.at[8 + 2 * s])
        wait_for(vec9.at[s, pl.ds(0, 3)], spread_send.at[8 + s])
        wait_sent_unless(x == z, vec9.at[s, 0], spread_self.at[8 + s])
    for stage, ref in enumerate((None, vec2, vec3, None, None, None, vec7, vec8)):
        if ref is not None:
            wait_for(ref.at[pl.ds(0, 3)], spread_send.at[stage])
            wait_sent_unless(x == z, ref.at[0], spread_self.at[stage])
    for stage, ref in ((3, vec4), (4, vec5), (5, vec6)):
        wait_for(ref.at[0], spread_send.at[stage])
        wait_for(ref.at[1, pl.ds(0, 3)], spread_send.at[stage])
        wait_sent_unless(x == z, ref.at[0, 0], spread_self.at[stage])
    wait_for(leaf_recv.at[pl.ds(0, 3)], misc_send.at[0])

    @pl.when(core == 0)
    def _():
        wait_for(leaf_recv, relay_sem.at[4])
        wait_sent_unless(leaf_here, leaf_recv.at[0], misc_self.at[0])

    @pl.when(core == 1)
    def _():
        wait_for(leaf_recv.at[0], misc_send.at[0])

    wait_for(bias_recv.at[pl.ds(0, 3)], misc_send.at[1])
    wait_sent_unless(bias_here, bias_recv.at[0], misc_self.at[1])
    wait_for(root_out_recv.at[pl.ds(0, 2)], misc_send.at[2])
    for k in range(2):
        wait_sent_unless(out_here(k, core), root_out_recv.at[0], misc_self.at[2 + k])
    wait_for(first_out_recv.at[pl.ds(0, 3)], misc_send.at[3])
    wait_sent_unless(first_here, first_out_recv.at[0], misc_self.at[4])

    for s in range(2):
        wait_for(recv10.at[s], scatter_recv.at[9 + 2 * s])
        total = add_up(recv10.at[s], 16)
        sol_half[1 + s, 0:32] = total[:, 0:64]
        sol_half[1 + s, 32:64] = total[:, 64:128]
    for s in range(2):
        wait_for(send10.at[s, pl.ds(0, 15)], scatter_send.at[9 + 2 * s])


def per_device(
    rhs_half,
    rhs_root,
    lower_coupling,
    lower_pattern,
    upper_coupling,
    upper_pattern,
    lower_inverse,
    upper_inverse,
    root_lower_inverse,
    root_upper_inverse,
):
    vmem = pl.BlockSpec(memory_space=pltpu.VMEM)
    hbm = pl.BlockSpec(memory_space=pl.ANY)
    one = (16, 256)
    two = (2, 16, 256)
    half = (16, 128)
    stage_chunks = [
        (2, 16) + one,
        (16,) + one,
        (16,) + one,
        (2, 16) + half,
        (16,) + half,
        (16,) + half,
        (16,) + one,
        (16,) + one,
        (2, 16) + one,
        (2, 16, 32, 128),
    ]
    exchange = [pltpu.VMEM(chunk, BF16) for chunk in stage_chunks]
    part_chunks = [two, one, one, half, half, half, one, one, two]
    parts = [pltpu.VMEM(chunk, BF16) for chunk in part_chunks]
    vectors = [
        pltpu.VMEM((2, 4) + chunk if chunk == half else (4,) + chunk, BF16)
        for chunk in part_chunks[1:8]
    ]
    vectors = [pltpu.VMEM((2, 4) + one, BF16), *vectors, pltpu.VMEM((2, 4) + one, BF16)]
    scratch = [
        pltpu.VMEM((3, 64, 64), F32),
        pltpu.VMEM((64, 64), F32),
        pltpu.SMEM((5, 2, 8), jnp.int32),
        pltpu.SMEM((5, 2, 8), jnp.int32),
        pltpu.VMEM((5, 256, 1024), BF16),
        pltpu.VMEM((5, 256, 1024), BF16),
        pltpu.VMEM((3, 256, 1024), BF16),
        pltpu.VMEM((3, 256, 1024), BF16),
        pltpu.VMEM((256, 512), BF16),
        pltpu.VMEM((256, 512), BF16),
        pltpu.VMEM((64, 128), BF16),
        pltpu.VMEM((4, 64, 128), BF16),
        pltpu.VMEM((4, 64, 128), BF16),
        pltpu.VMEM((64, 128), F32),
        pltpu.VMEM((4, 16, 128), F32),
        *exchange,
        *exchange,
        *parts,
        *vectors,
        pltpu.VMEM(two, F32),
        pltpu.VMEM(one, F32),
        pltpu.VMEM((64, 1024), F32),
        pltpu.VMEM((64, 1024), F32),
        pltpu.VMEM((2, 64, 1024), F32),
        pltpu.VMEM(half, F32),
        pltpu.VMEM((4,) + half, F32),
        pltpu.VMEM((2,) + half, F32),
        pltpu.VMEM((4,) + half, F32),
        pltpu.SemaphoreType.DMA((10,)),
        pltpu.SemaphoreType.DMA((13,)),
        pltpu.SemaphoreType.DMA((13,)),
        pltpu.SemaphoreType.DMA((11,)),
        pltpu.SemaphoreType.DMA((11,)),
        pltpu.SemaphoreType.DMA((11,)),
        pltpu.SemaphoreType.DMA((4,)),
        pltpu.SemaphoreType.DMA((4,)),
        pltpu.SemaphoreType.DMA((5,)),
        pltpu.SemaphoreType.DMA((5,)),
        pltpu.SemaphoreType.REGULAR,
        pltpu.SemaphoreType.REGULAR,
    ]
    sol_half, sol_root = pl.pallas_call(
        kernel,
        name="tree_solve",
        out_shape=(pltpu.VMEM((3, 64, 64), F32), pltpu.VMEM((64, 64), F32)),
        in_specs=[hbm] * 10,
        out_specs=(vmem, vmem),
        scratch_shapes=scratch,
        compiler_params=pltpu.CompilerParams(collective_id=0, has_side_effects=True),
    )(
        rhs_half[0],
        rhs_root,
        lower_pattern[0],
        upper_pattern[0],
        lower_coupling[0],
        upper_coupling[0],
        lower_inverse[0],
        upper_inverse[0],
        root_lower_inverse,
        root_upper_inverse,
    )

    def leave(half_ref, root_ref, half_out, root_out, sems):
        first = pltpu.make_async_copy(half_ref, half_out, sems.at[0])
        second = pltpu.make_async_copy(root_ref, root_out, sems.at[1])
        first.start()
        second.start()
        first.wait()
        second.wait()

    sol_half, sol_root = pl.pallas_call(
        leave,
        name="leave",
        out_shape=(
            jax.ShapeDtypeStruct((3, 64, 64), F32),
            jax.ShapeDtypeStruct((64, 64), F32),
        ),
        in_specs=[vmem, vmem],
        out_specs=(hbm, hbm),
        scratch_shapes=[pltpu.SemaphoreType.DMA((2,))],
        compiler_params=pltpu.CompilerParams(vmem_limit_bytes=1 << 20),
    )(sol_half, sol_root)
    return (sol_half[None], sol_root)


def solution(mesh):
    in_specs = (
        P("gz", None, None, ("row", "col")),
        P(None, ("row", "col")),
        P("gz", None, "col", "row"),
        P("gz", None, "col", "row"),
        P("gz", None, "col", "row"),
        P("gz", None, "col", "row"),
        P("gz", None, "col", "row"),
        P("gz", None, "col", "row"),
        P("col", "row"),
        P("col", "row"),
    )
    out_specs = (P("gz", None, None, ("row", "col")), P(None, ("row", "col")))
    return jax.shard_map(
        per_device, mesh=mesh, in_specs=in_specs, out_specs=out_specs, check_vma=False
    )
```

```python
import jax
import jax.numpy as jnp
from jax import lax
from jax.experimental import pallas as pl
from jax.experimental.pallas import tpu as pltpu
from jax.sharding import PartitionSpec as P

MESH = pl.DeviceIdType.MESH
F32 = jnp.float32
BF16 = jnp.bfloat16

NEAR = sorted(
    ((dx, dy) for dx in range(4) for dy in range(4) if dx or dy),
    key=lambda d: -(min(d[0], 4 - d[0]) + min(d[1], 4 - d[1])),
)


def dot(vector, tiles):
    return jnp.dot(vector, tiles, preferred_element_type=F32)


def add_up(ref, count):
    total = ref[0].astype(F32)
    for i in range(1, count):
        total = total + ref[i].astype(F32)
    return total


def kernel(
    rhs_half_hbm,
    rhs_root_hbm,
    lower_pattern_hbm,
    upper_pattern_hbm,
    lower_hbm,
    upper_hbm,
    lower_inverse_hbm,
    upper_inverse_hbm,
    root_lower_hbm,
    root_upper_hbm,
    sol_half,
    sol_root,
    rhs_half,
    rhs_root,
    lower_pattern,
    upper_pattern,
    lower,
    upper,
    lower_inverse,
    upper_inverse,
    root_lower,
    root_upper,
    leaf_pack,
    leaf_recv,
    leaf_relay,
    bias_pack,
    bias_recv,
    send1,
    send2,
    send3,
    send4,
    send5,
    send6,
    send7,
    send8,
    send9,
    send10,
    recv1,
    recv2,
    recv3,
    recv4,
    recv5,
    recv6,
    recv7,
    recv8,
    recv9,
    recv10,
    part1,
    part2,
    part3,
    part4,
    part5,
    part6,
    part7,
    part8,
    part9,
    vec1,
    vec2,
    vec3,
    vec4,
    vec5,
    vec6,
    vec7,
    vec8,
    vec9,
    leaf_value,
    top_value,
    top_early,
    root_early,
    second_early,
    root_out,
    root_out_recv,
    first_out,
    first_out_recv,
    weight_sem,
    scatter_send,
    scatter_recv,
    spread_send,
    spread_recv,
    spread_self,
    misc_send,
    misc_recv,
    misc_self,
    relay_sem,
    ready,
    go,
):
    z = lax.axis_index("row")
    col = lax.axis_index("col")
    core = lax.axis_index("gz")
    x = col // 4
    y = col % 4
    other = 1 - core

    def start_local(src, dst, sem):
        pltpu.make_async_copy(src, dst, sem).start()

    def wait_for(ref, sem):
        pltpu.make_async_copy(ref, ref, sem).wait()

    def send(src, dst, send_sem, recv_sem, device):
        pltpu.make_async_remote_copy(
            src_ref=src,
            dst_ref=dst,
            send_sem=send_sem,
            recv_sem=recv_sem,
            device_id=device,
            device_id_type=MESH,
        ).start()

    def send_or_keep(here, src, dst, send_sem, recv_sem, device):
        @pl.when(jnp.logical_not(here))
        def _():
            send(src, dst, send_sem, recv_sem, device)

        @pl.when(here)
        def _():
            start_local(src, dst, recv_sem)

    def wait_sent_unless(here, ref, sem):
        @pl.when(jnp.logical_not(here))
        def _():
            wait_for(ref, sem)

    barrier = pltpu.get_barrier_semaphore()

    def greet(px, py, pz, pcore):
        pl.semaphore_signal(
            barrier, inc=1, device_id=(pz, 4 * px + py, pcore), device_id_type=MESH
        )

    @pl.when(core == 0)
    def _():
        for u in range(4):
            greet(y, u, x, 1)
        for dz in (2, 1, 3):
            greet(z, y, (z + dz) % 4, 0)

        @pl.when(x != z)
        def _():
            for u in range(4):
                greet(y, u, x, 0)
                greet(u, y, x, 0)

        for dx, dy in NEAR:
            greet((x + dx) % 4, (y + dy) % 4, z, 0)

    @pl.when(core == 1)
    def _():
        greet(x, y, z, 0)

    start_local(rhs_half_hbm, rhs_half, weight_sem.at[6])
    start_local(rhs_root_hbm, rhs_root, weight_sem.at[7])
    start_local(lower_pattern_hbm, lower_pattern, weight_sem.at[8])
    start_local(upper_pattern_hbm, upper_pattern, weight_sem.at[9])
    wait_for(rhs_half, weight_sem.at[6])
    wait_for(rhs_root, weight_sem.at[7])
    leaf_pack[...] = jnp.concatenate([rhs_half[1], rhs_half[2]], axis=1).astype(BF16)
    bias_pack[...] = jnp.concatenate([rhs_half[0], rhs_root[...]], axis=1)

    def tell(px, py, pz):
        pl.semaphore_signal(ready, inc=1, device_id=(pz, 4 * px + py, 0), device_id_type=MESH)

    @pl.when(core == 0)
    def _():
        @pl.when(x == z)
        def _():
            pl.semaphore_wait(barrier, 15 + 3 + 3 + 1)

        @pl.when(x != z)
        def _():
            pl.semaphore_wait(barrier, 15 + 3 + 3 + 1 + 4)
            for u in range(4):
                tell(u, y, x)

        for dx, dy in NEAR:
            tell((x + dx) % 4, (y + dy) % 4, z)

    @pl.when(core == 1)
    def _():
        pl.semaphore_wait(barrier, 4)

    leaf_here = jnp.logical_and(x == z, x == y)

    @pl.when(core == 0)
    def _():
        for dz in (2, 1, 3):
            send(
                leaf_pack,
                leaf_recv.at[y],
                misc_send.at[0],
                misc_recv.at[0],
                ((z + dz) % 4, 4 * z + x, 0),
            )
        send_or_keep(
            leaf_here,
            leaf_pack,
            leaf_recv.at[y],
            misc_self.at[0],
            misc_recv.at[0],
            (z, 4 * z + x, 0),
        )

    @pl.when(core == 1)
    def _():
        for dz in (2, 1, 3, 0):
            send(
                leaf_pack,
                leaf_relay.at[y],
                misc_send.at[0],
                relay_sem.at[y],
                ((z + dz) % 4, 4 * z + x, 0),
            )

    start_local(lower_inverse_hbm, lower_inverse, weight_sem.at[0])
    start_local(lower_hbm, lower, weight_sem.at[1])
    for j in range(4):
        columns = pl.ds(pl.multiple_of(256 * j + 128 * core, 128), 128)
        start_local(
            root_lower_hbm.at[:, columns], root_lower.at[:, pl.ds(128 * j, 128)], weight_sem.at[2]
        )
    for j in range(4):
        columns = pl.ds(pl.multiple_of(256 * j + 128 * core, 128), 128)
        start_local(
            root_upper_hbm.at[:, columns], root_upper.at[:, pl.ds(128 * j, 128)], weight_sem.at[3]
        )
    start_local(upper_hbm, upper, weight_sem.at[4])
    start_local(upper_inverse_hbm, upper_inverse, weight_sem.at[5])

    def scatter(src, dst, stage):
        for dx, dy in NEAR:
            peer = 4 * ((x + dx) % 4) + (y + dy) % 4
            send(
                src.at[peer],
                dst.at[col],
                scatter_send.at[stage],
                scatter_recv.at[stage],
                (z, peer, core),
            )
        start_local(src.at[col], dst.at[col], scatter_recv.at[stage])

    def spread(src, dst, stage):
        for dz in (2, 1, 3):
            send(
                src,
                dst.at[x],
                spread_send.at[stage],
                spread_recv.at[stage],
                ((z + dz) % 4, 4 * z + y, core),
            )
        send_or_keep(
            x == z,
            src,
            dst.at[x],
            spread_self.at[stage],
            spread_recv.at[stage],
            (z, 4 * z + y, core),
        )

    def spread_both(src, dst, stage):
        for dz in (2, 1, 3):
            for to in (other, core):
                send(
                    src,
                    dst.at[core, x],
                    spread_send.at[stage],
                    spread_recv.at[stage],
                    ((z + dz) % 4, 4 * z + y, to),
                )
        send(
            src,
            dst.at[core, x],
            spread_send.at[stage],
            spread_recv.at[stage],
            (z, 4 * z + y, other),
        )
        send_or_keep(
            x == z,
            src,
            dst.at[core, x],
            spread_self.at[stage],
            spread_recv.at[stage],
            (z, 4 * z + y, core),
        )

    def mask(tiles, pattern):
        @pl.loop(0, 5)
        def _(p):
            for a in range(2):
                for b in range(8):
                    here = (p, pl.ds(128 * a, 128), pl.ds(128 * b, 128))
                    keep = jnp.full((128, 128), pattern[p, a, b].astype(F32), F32)
                    tiles[here] = tiles[here] * keep.astype(BF16)

    def columns_of(j):
        return pl.ds(pl.multiple_of(256 * j, 256), 256)

    def block(ref, j):
        return ref[:, columns_of(j)]

    def multiply(values_of, src, dst, stage):
        for dy in (2, 1, 3, 0):
            j = (y + dy) % 4
            values = values_of(j)
            for q in range(4):
                rows = [value[16 * q : 16 * q + 16].astype(BF16) for value in values]
                if len(rows) == 1:
                    src[4 * q + j] = rows[0]
                else:
                    for s in range(2):
                        src[4 * q + j, s] = rows[s]
            for dx in (2, 1, 3, 0):
                peer = 4 * ((x + dx) % 4) + j
                if dx or dy:
                    send(
                        src.at[peer],
                        dst.at[col],
                        scatter_send.at[stage],
                        scatter_recv.at[stage],
                        (z, peer, core),
                    )
                else:
                    start_local(src.at[peer], dst.at[col], scatter_recv.at[stage])

    wait_for(lower, weight_sem.at[1])
    wait_for(lower_pattern, weight_sem.at[8])
    mask(lower, lower_pattern)

    @pl.when(core == 0)
    def _():
        pl.semaphore_wait(ready, 15 + 3)
        pl.semaphore_signal(go, inc=1, device_id=(z, col, 1), device_id_type=MESH)

    @pl.when(core == 1)
    def _():
        pl.semaphore_wait(go, 1)

    bias_here = x == y
    for dq in (2, 1, 3):
        q = (x + dq) % 4
        send(
            bias_pack.at[pl.ds(pl.multiple_of(16 * q, 16), 16)],
            bias_recv.at[y],
            misc_send.at[1],
            misc_recv.at[1],
            (z, 4 * q + x, core),
        )
    own_rows = pl.ds(pl.multiple_of(16 * x, 16), 16)
    send_or_keep(
        bias_here,
        bias_pack.at[own_rows],
        bias_recv.at[y],
        misc_self.at[1],
        misc_recv.at[1],
        (z, 4 * x + x, core),
    )

    @pl.when(core == 0)
    def _():
        for u in range(4):
            wait_for(leaf_relay.at[u], relay_sem.at[u])
            send(leaf_relay.at[u], leaf_recv.at[u], relay_sem.at[4], misc_recv.at[0], (z, col, 1))

    wait_for(leaf_recv, misc_recv.at[0])
    wait_for(lower_inverse, weight_sem.at[0])
    pieces = [leaf_recv[u].astype(F32) for u in range(4)]
    leaves = [
        jnp.concatenate([p[:, 64 * s : 64 * s + 64] for p in pieces], axis=1).astype(BF16)
        for s in range(2)
    ]
    for s in range(2):
        multiply(
            lambda j, s=s: [dot(leaves[s], block(lower_inverse.at[1 + s], j))],
            send1.at[s],
            recv1.at[s],
            12 * s,
        )
    for s in range(2):
        wait_for(recv1.at[s], scatter_recv.at[12 * s])
        leaf_value[s] = add_up(recv1.at[s], 16)
        part1[s] = leaf_value[s].astype(BF16)
        spread(part1.at[s], vec1.at[s], 10 * s)

    wait_for(vec1.at[0], spread_recv.at[0])
    leaf1 = vec1[0].reshape(64, 256)
    for j in range(4):
        top_early[:, 256 * j : 256 * j + 256] = dot(leaf1, block(lower.at[0], j))
    wait_for(vec1.at[1], spread_recv.at[10])
    leaf2 = vec1[1].reshape(64, 256)
    multiply(
        lambda j: [top_early[:, columns_of(j)] + dot(leaf2, block(lower.at[1], j))],
        send2,
        recv2,
        1,
    )
    for j in range(4):
        root_early[:, 256 * j : 256 * j + 256] = dot(leaf1, block(lower.at[3], j)) + dot(
            leaf2, block(lower.at[4], j)
        )
    wait_for(bias_recv, misc_recv.at[1])
    top_bias = jnp.concatenate([bias_recv[u][:, 0:64] for u in range(4)], axis=1)
    wait_for(recv2, scatter_recv.at[1])
    part2[...] = (top_bias - add_up(recv2, 16)).astype(BF16)
    spread(part2, vec2, 1)

    wait_for(vec2, spread_recv.at[1])
    vector = vec2[...].reshape(64, 256)
    vector3 = vector
    multiply(lambda j: [dot(vector3, block(lower_inverse.at[0], j))], send3, recv3, 2)
    wait_for(recv3, scatter_recv.at[2])
    top_value[...] = add_up(recv3, 16)
    part3[...] = top_value[...].astype(BF16)
    spread(part3, vec3, 2)

    wait_for(vec3, spread_recv.at[2])
    vector = vec3[...].reshape(64, 256)
    for dy in (2, 1, 3, 0):
        j = (y + dy) % 4
        value = root_early[:, columns_of(j)] + dot(vector, block(lower.at[2], j))
        for half in range(2):
            for q in range(4):
                send4[half, 4 * q + j] = value[
                    16 * q : 16 * q + 16, 128 * half : 128 * half + 128
                ].astype(BF16)
        for dx in (2, 1, 3, 0):
            peer = 4 * ((x + dx) % 4) + j
            for to in (other, core):
                if dx or dy or to is other:
                    send(
                        send4.at[to, peer],
                        recv4.at[core, col],
                        scatter_send.at[3],
                        scatter_recv.at[3],
                        (z, peer, to),
                    )
                else:
                    start_local(send4.at[to, peer], recv4.at[core, col], scatter_recv.at[3])
    root_bias = jnp.concatenate(
        [bias_recv[2 * core][:, 64:128], bias_recv[2 * core + 1][:, 64:128]], axis=1
    )
    wait_for(upper, weight_sem.at[4])
    wait_for(upper_pattern, weight_sem.at[9])
    mask(upper, upper_pattern)
    wait_for(recv4, scatter_recv.at[3])
    part4[...] = (root_bias - add_up(recv4.at[0], 16) - add_up(recv4.at[1], 16)).astype(BF16)
    spread_both(part4, vec4, 3)

    def whole(ref):
        return jnp.concatenate([ref[0].reshape(64, 128), ref[1].reshape(64, 128)], axis=1)

    def halves(ref, vector, tiles):
        for pair in range(2):
            value = dot(vector, tiles[:, 256 * pair : 256 * pair + 256])
            for k in range(2):
                for q in range(4):
                    ref[4 * q + 2 * pair + k] = value[
                        16 * q : 16 * q + 16, 128 * k : 128 * k + 128
                    ].astype(BF16)

    wait_for(root_lower, weight_sem.at[2])
    wait_for(vec4, spread_recv.at[3])
    halves(send5, whole(vec4), root_lower)
    scatter(send5, recv5, 4)
    wait_for(recv5, scatter_recv.at[4])
    part5[...] = add_up(recv5, 16).astype(BF16)
    spread_both(part5, vec5, 4)
    wait_for(root_upper, weight_sem.at[3])
    wait_for(vec5, spread_recv.at[4])
    halves(send6, whole(vec5), root_upper)
    scatter(send6, recv6, 5)
    wait_for(recv6, scatter_recv.at[5])
    root_out[...] = add_up(recv6, 16)
    part6[...] = root_out[...].astype(BF16)
    spread_both(part6, vec6, 5)

    def out_here(k, to):
        return jnp.logical_and(jnp.logical_and(x == y, 2 * core + k == y), to == core)

    for k in range(2):
        owner = 4 * y + 2 * core + k
        send(root_out, root_out_recv.at[x], misc_send.at[2], misc_recv.at[2], (z, owner, other))
        send_or_keep(
            out_here(k, core),
            root_out,
            root_out_recv.at[x],
            misc_self.at[2 + k],
            misc_recv.at[2],
            (z, owner, core),
        )

    wait_for(vec6, spread_recv.at[5])
    vector = whole(vec6)
    vector7 = vector
    multiply(lambda j: [dot(vector7, block(upper.at[2], j))], send7, recv7, 6)
    for s in range(2):
        for j in range(4):
            second_early[s, :, 256 * j : 256 * j + 256] = dot(vector, block(upper.at[3 + s], j))
    wait_for(recv7, scatter_recv.at[6])
    part7[...] = (top_value[...] - add_up(recv7, 16)).astype(BF16)
    spread(part7, vec7, 6)

    wait_for(upper_inverse, weight_sem.at[5])
    wait_for(vec7, spread_recv.at[6])
    vector = vec7[...].reshape(64, 256)
    vector8 = vector
    multiply(lambda j: [dot(vector8, block(upper_inverse.at[0], j))], send8, recv8, 7)
    wait_for(recv8, scatter_recv.at[7])
    first = add_up(recv8, 16)
    part8[...] = first.astype(BF16)
    spread(part8, vec8, 7)
    first_out[0] = first[:, 0:128]
    first_out[1] = first[:, 128:256]
    first_here = x == y
    for du in (2, 1, 3):
        u = (y + du) % 4
        send(
            first_out.at[u // 2],
            first_out_recv.at[x],
            misc_send.at[3],
            misc_recv.at[3],
            (z, 4 * y + u, core),
        )
    send_or_keep(
        first_here,
        first_out.at[y // 2],
        first_out_recv.at[x],
        misc_self.at[4],
        misc_recv.at[3],
        (z, 4 * y + y, core),
    )

    wait_for(vec8, spread_recv.at[7])
    vector = vec8[...].reshape(64, 256)
    vector9 = vector
    for s in range(2):
        multiply(
            lambda j, s=s: [
                second_early[s, :, columns_of(j)] + dot(vector9, block(upper.at[s], j))
            ],
            send9.at[s],
            recv9.at[s],
            8 + 2 * s,
        )

    odd = y % 2 == 1
    wait_for(root_out_recv, misc_recv.at[2])
    value = root_out_recv[...].reshape(64, 128)
    sol_root[...] = jnp.where(odd, value[:, 64:128], value[:, 0:64])
    wait_for(first_out_recv, misc_recv.at[3])
    value = first_out_recv[...].reshape(64, 128)
    sol_half[0] = jnp.where(odd, value[:, 64:128], value[:, 0:64])

    for s in range(2):
        wait_for(recv9.at[s], scatter_recv.at[8 + 2 * s])
        part9[s] = (leaf_value[s] - add_up(recv9.at[s], 16)).astype(BF16)
        spread(part9.at[s], vec9.at[s], 8 + s)

    for s in range(2):
        wait_for(vec9.at[s], spread_recv.at[8 + s])
        vector = vec9[s].reshape(64, 256)
        for dx in (2, 1, 3, 0):
            j = (x + dx) % 4
            value = dot(vector, block(upper_inverse.at[1 + s], j))
            for u in range(4):
                span = slice(64 * u, 64 * u + 64)
                send10[s, 4 * j + u] = jnp.concatenate(
                    [value[0:32, span], value[32:64, span]], axis=1
                ).astype(BF16)
            for dy in (2, 1, 3, 0):
                peer = 4 * j + (y + dy) % 4
                if dx or dy:
                    send(
                        send10.at[s, peer],
                        recv10.at[s, col],
                        scatter_send.at[9 + 2 * s],
                        scatter_recv.at[9 + 2 * s],
                        (z, peer, core),
                    )
                else:
                    start_local(
                        send10.at[s, peer], recv10.at[s, col], scatter_recv.at[9 + 2 * s]
                    )
    sends = (None, send2, send3, None, send5, send6, send7, send8)
    for stage, ref in enumerate(sends):
        if ref is not None:
            wait_for(ref.at[pl.ds(0, 15)], scatter_send.at[stage])
    wait_for(recv4.at[0], scatter_send.at[3])
    wait_for(recv4.at[1, pl.ds(0, 15)], scatter_send.at[3])
    for s in range(2):
        wait_for(send1.at[s, pl.ds(0, 15)], scatter_send.at[12 * s])
        wait_for(vec1.at[s, pl.ds(0, 3)], spread_send.at[10 * s])
        wait_sent_unless(x == z, vec1.at[s, 0], spread_self.at[10 * s])
        wait_for(send9.at[s, pl.ds(0, 15)], scatter_send.at[8 + 2 * s])
        wait_for(vec9.at[s, pl.ds(0, 3)], spread_send.at[8 + s])
        wait_sent_unless(x == z, vec9.at[s, 0], spread_self.at[8 + s])
    for stage, ref in enumerate((None, vec2, vec3, None, None, None, vec7, vec8)):
        if ref is not None:
            wait_for(ref.at[pl.ds(0, 3)], spread_send.at[stage])
            wait_sent_unless(x == z, ref.at[0], spread_self.at[stage])
    for stage, ref in ((3, vec4), (4, vec5), (5, vec6)):
        wait_for(ref.at[0], spread_send.at[stage])
        wait_for(ref.at[1, pl.ds(0, 3)], spread_send.at[stage])
        wait_sent_unless(x == z, ref.at[0, 0], spread_self.at[stage])
    wait_for(leaf_recv.at[pl.ds(0, 3)], misc_send.at[0])

    @pl.when(core == 0)
    def _():
        wait_for(leaf_recv, relay_sem.at[4])
        wait_sent_unless(leaf_here, leaf_recv.at[0], misc_self.at[0])

    @pl.when(core == 1)
    def _():
        wait_for(leaf_recv.at[0], misc_send.at[0])

    wait_for(bias_recv.at[pl.ds(0, 3)], misc_send.at[1])
    wait_sent_unless(bias_here, bias_recv.at[0], misc_self.at[1])
    wait_for(root_out_recv.at[pl.ds(0, 2)], misc_send.at[2])
    for k in range(2):
        wait_sent_unless(out_here(k, core), root_out_recv.at[0], misc_self.at[2 + k])
    wait_for(first_out_recv.at[pl.ds(0, 3)], misc_send.at[3])
    wait_sent_unless(first_here, first_out_recv.at[0], misc_self.at[4])

    for s in range(2):
        wait_for(recv10.at[s], scatter_recv.at[9 + 2 * s])
        total = add_up(recv10.at[s], 16)
        sol_half[1 + s, 0:32] = total[:, 0:64]
        sol_half[1 + s, 32:64] = total[:, 64:128]
    for s in range(2):
        wait_for(send10.at[s, pl.ds(0, 15)], scatter_send.at[9 + 2 * s])


def per_device(
    rhs_half,
    rhs_root,
    lower_coupling,
    lower_pattern,
    upper_coupling,
    upper_pattern,
    lower_inverse,
    upper_inverse,
    root_lower_inverse,
    root_upper_inverse,
):
    vmem = pl.BlockSpec(memory_space=pltpu.VMEM)
    hbm = pl.BlockSpec(memory_space=pl.ANY)
    one = (16, 256)
    two = (2, 16, 256)
    half = (16, 128)
    stage_chunks = [
        (2, 16) + one,
        (16,) + one,
        (16,) + one,
        (2, 16) + half,
        (16,) + half,
        (16,) + half,
        (16,) + one,
        (16,) + one,
        (2, 16) + one,
        (2, 16, 32, 128),
    ]
    exchange = [pltpu.VMEM(chunk, BF16) for chunk in stage_chunks]
    part_chunks = [two, one, one, half, half, half, one, one, two]
    parts = [pltpu.VMEM(chunk, BF16) for chunk in part_chunks]
    vectors = [
        pltpu.VMEM((2, 4) + chunk if chunk == half else (4,) + chunk, BF16)
        for chunk in part_chunks[1:8]
    ]
    vectors = [pltpu.VMEM((2, 4) + one, BF16), *vectors, pltpu.VMEM((2, 4) + one, BF16)]
    scratch = [
        pltpu.VMEM((3, 64, 64), F32),
        pltpu.VMEM((64, 64), F32),
        pltpu.SMEM((5, 2, 8), jnp.int32),
        pltpu.SMEM((5, 2, 8), jnp.int32),
        pltpu.VMEM((5, 256, 1024), BF16),
        pltpu.VMEM((5, 256, 1024), BF16),
        pltpu.VMEM((3, 256, 1024), BF16),
        pltpu.VMEM((3, 256, 1024), BF16),
        pltpu.VMEM((256, 512), BF16),
        pltpu.VMEM((256, 512), BF16),
        pltpu.VMEM((64, 128), BF16),
        pltpu.VMEM((4, 64, 128), BF16),
        pltpu.VMEM((4, 64, 128), BF16),
        pltpu.VMEM((64, 128), F32),
        pltpu.VMEM((4, 16, 128), F32),
        *exchange,
        *exchange,
        *parts,
        *vectors,
        pltpu.VMEM(two, F32),
        pltpu.VMEM(one, F32),
        pltpu.VMEM((64, 1024), F32),
        pltpu.VMEM((64, 1024), F32),
        pltpu.VMEM((2, 64, 1024), F32),
        pltpu.VMEM(half, F32),
        pltpu.VMEM((4,) + half, F32),
        pltpu.VMEM((2,) + half, F32),
        pltpu.VMEM((4,) + half, F32),
        pltpu.SemaphoreType.DMA((10,)),
        pltpu.SemaphoreType.DMA((13,)),
        pltpu.SemaphoreType.DMA((13,)),
        pltpu.SemaphoreType.DMA((11,)),
        pltpu.SemaphoreType.DMA((11,)),
        pltpu.SemaphoreType.DMA((11,)),
        pltpu.SemaphoreType.DMA((4,)),
        pltpu.SemaphoreType.DMA((4,)),
        pltpu.SemaphoreType.DMA((5,)),
        pltpu.SemaphoreType.DMA((5,)),
        pltpu.SemaphoreType.REGULAR,
        pltpu.SemaphoreType.REGULAR,
    ]
    sol_half, sol_root = pl.pallas_call(
        kernel,
        name="tree_solve",
        out_shape=(pltpu.VMEM((3, 64, 64), F32), pltpu.VMEM((64, 64), F32)),
        in_specs=[hbm] * 10,
        out_specs=(vmem, vmem),
        scratch_shapes=scratch,
        compiler_params=pltpu.CompilerParams(collective_id=0, has_side_effects=True),
    )(
        rhs_half[0],
        rhs_root,
        lower_pattern[0],
        upper_pattern[0],
        lower_coupling[0],
        upper_coupling[0],
        lower_inverse[0],
        upper_inverse[0],
        root_lower_inverse,
        root_upper_inverse,
    )

    def leave(half_ref, root_ref, half_out, root_out, sems):
        first = pltpu.make_async_copy(half_ref, half_out, sems.at[0])
        second = pltpu.make_async_copy(root_ref, root_out, sems.at[1])
        first.start()
        second.start()
        first.wait()
        second.wait()

    sol_half, sol_root = pl.pallas_call(
        leave,
        name="leave",
        out_shape=(
            jax.ShapeDtypeStruct((3, 64, 64), F32),
            jax.ShapeDtypeStruct((64, 64), F32),
        ),
        in_specs=[vmem, vmem],
        out_specs=(hbm, hbm),
        scratch_shapes=[pltpu.SemaphoreType.DMA((2,))],
        compiler_params=pltpu.CompilerParams(vmem_limit_bytes=1 << 20),
    )(sol_half, sol_root)
    return (sol_half[None], sol_root)


def solution(mesh):
    in_specs = (
        P("gz", None, None, ("row", "col")),
        P(None, ("row", "col")),
        P("gz", None, "col", "row"),
        P("gz", None, "col", "row"),
        P("gz", None, "col", "row"),
        P("gz", None, "col", "row"),
        P("gz", None, "col", "row"),
        P("gz", None, "col", "row"),
        P("col", "row"),
        P("col", "row"),
    )
    out_specs = (P("gz", None, None, ("row", "col")), P(None, ("row", "col")))
    return jax.shard_map(
        per_device, mesh=mesh, in_specs=in_specs, out_specs=out_specs, check_vma=False
    )
```

```python
import jax
import jax.numpy as jnp
from jax import lax
from jax.experimental import pallas as pl
from jax.experimental.pallas import tpu as pltpu
from jax.sharding import PartitionSpec as P

MESH = pl.DeviceIdType.MESH
F32 = jnp.float32
BF16 = jnp.bfloat16

NEAR = sorted(
    ((dx, dy) for dx in range(4) for dy in range(4) if dx or dy),
    key=lambda d: -(min(d[0], 4 - d[0]) + min(d[1], 4 - d[1])),
)


def dot(vector, tiles):
    return jnp.dot(vector, tiles, preferred_element_type=F32)


def add_up(ref, count):
    terms = [ref[i].astype(F32) for i in range(count)]
    while len(terms) > 1:
        terms = [terms[i] + terms[i + 1] for i in range(0, len(terms), 2)]
    return terms[0]


def kernel(
    rhs_half_hbm,
    rhs_root_hbm,
    lower_pattern_hbm,
    upper_pattern_hbm,
    lower_hbm,
    upper_hbm,
    lower_inverse_hbm,
    upper_inverse_hbm,
    root_lower_hbm,
    root_upper_hbm,
    sol_half,
    sol_root,
    rhs_half,
    rhs_root,
    lower_pattern,
    upper_pattern,
    lower,
    upper,
    lower_inverse,
    upper_inverse,
    root_lower,
    root_upper,
    leaf_pack,
    leaf_recv,
    leaf_relay,
    bias_pack,
    bias_recv,
    send1,
    send2,
    send3,
    send4,
    send5,
    send6,
    send7,
    send8,
    send9,
    send10,
    recv1,
    recv2,
    recv3,
    recv4,
    recv5,
    recv6,
    recv7,
    recv8,
    recv9,
    recv10,
    part1,
    part2,
    part3,
    part4,
    part5,
    part6,
    part7,
    part8,
    part9,
    vec1,
    vec2,
    vec3,
    vec4,
    vec5,
    vec6,
    vec7,
    vec8,
    vec9,
    leaf_value,
    top_value,
    top_early,
    root_early,
    second_early,
    root_out,
    root_out_recv,
    first_out,
    first_out_recv,
    weight_sem,
    scatter_send,
    scatter_recv,
    spread_send,
    spread_recv,
    spread_self,
    misc_send,
    misc_recv,
    misc_self,
    relay_sem,
    ready,
    go,
):
    z = lax.axis_index("row")
    col = lax.axis_index("col")
    core = lax.axis_index("gz")
    x = col // 4
    y = col % 4
    other = 1 - core

    def start_local(src, dst, sem):
        pltpu.make_async_copy(src, dst, sem).start()

    def wait_for(ref, sem):
        pltpu.make_async_copy(ref, ref, sem).wait()

    def send(src, dst, send_sem, recv_sem, device):
        pltpu.make_async_remote_copy(
            src_ref=src,
            dst_ref=dst,
            send_sem=send_sem,
            recv_sem=recv_sem,
            device_id=device,
            device_id_type=MESH,
        ).start()

    def send_or_keep(here, src, dst, send_sem, recv_sem, device):
        @pl.when(jnp.logical_not(here))
        def _():
            send(src, dst, send_sem, recv_sem, device)

        @pl.when(here)
        def _():
            start_local(src, dst, recv_sem)

    def wait_sent_unless(here, ref, sem):
        @pl.when(jnp.logical_not(here))
        def _():
            wait_for(ref, sem)

    barrier = pltpu.get_barrier_semaphore()

    def greet(px, py, pz, pcore):
        pl.semaphore_signal(
            barrier, inc=1, device_id=(pz, 4 * px + py, pcore), device_id_type=MESH
        )

    @pl.when(core == 0)
    def _():
        for u in range(4):
            greet(y, u, x, 1)
        for dz in (2, 1, 3):
            greet(z, y, (z + dz) % 4, 0)

        @pl.when(x != z)
        def _():
            for u in range(4):
                greet(y, u, x, 0)
                greet(u, y, x, 0)

        for dx, dy in NEAR:
            greet((x + dx) % 4, (y + dy) % 4, z, 0)

    @pl.when(core == 1)
    def _():
        greet(x, y, z, 0)

    start_local(rhs_half_hbm, rhs_half, weight_sem.at[6])
    start_local(rhs_root_hbm, rhs_root, weight_sem.at[7])
    start_local(lower_pattern_hbm, lower_pattern, weight_sem.at[8])
    start_local(upper_pattern_hbm, upper_pattern, weight_sem.at[9])
    start_local(lower_inverse_hbm, lower_inverse, weight_sem.at[0])
    start_local(lower_hbm, lower, weight_sem.at[1])
    for j in range(4):
        columns = pl.ds(pl.multiple_of(256 * j + 128 * core, 128), 128)
        start_local(
            root_lower_hbm.at[:, columns], root_lower.at[:, pl.ds(128 * j, 128)], weight_sem.at[2]
        )
    for j in range(4):
        columns = pl.ds(pl.multiple_of(256 * j + 128 * core, 128), 128)
        start_local(
            root_upper_hbm.at[:, columns], root_upper.at[:, pl.ds(128 * j, 128)], weight_sem.at[3]
        )
    start_local(upper_hbm, upper, weight_sem.at[4])
    start_local(upper_inverse_hbm, upper_inverse, weight_sem.at[5])

    wait_for(rhs_half, weight_sem.at[6])
    wait_for(rhs_root, weight_sem.at[7])
    leaf_pack[...] = jnp.concatenate([rhs_half[1], rhs_half[2]], axis=1).astype(BF16)
    bias_pack[...] = jnp.concatenate([rhs_half[0], rhs_root[...]], axis=1)

    def tell(px, py, pz):
        pl.semaphore_signal(ready, inc=1, device_id=(pz, 4 * px + py, 0), device_id_type=MESH)

    @pl.when(core == 0)
    def _():
        @pl.when(x == z)
        def _():
            pl.semaphore_wait(barrier, 15 + 3 + 3 + 1)

        @pl.when(x != z)
        def _():
            pl.semaphore_wait(barrier, 15 + 3 + 3 + 1 + 4)
            for u in range(4):
                tell(u, y, x)

        for dx, dy in NEAR:
            tell((x + dx) % 4, (y + dy) % 4, z)

    @pl.when(core == 1)
    def _():
        pl.semaphore_wait(barrier, 4)

    leaf_here = jnp.logical_and(x == z, x == y)

    @pl.when(core == 0)
    def _():
        for dz in (2, 1, 3):
            send(
                leaf_pack,
                leaf_recv.at[y],
                misc_send.at[0],
                misc_recv.at[0],
                ((z + dz) % 4, 4 * z + x, 0),
            )
        send_or_keep(
            leaf_here,
            leaf_pack,
            leaf_recv.at[y],
            misc_self.at[0],
            misc_recv.at[0],
            (z, 4 * z + x, 0),
        )

    @pl.when(core == 1)
    def _():
        for dz in (2, 1, 3, 0):
            send(
                leaf_pack,
                leaf_relay.at[y],
                misc_send.at[0],
                relay_sem.at[y],
                ((z + dz) % 4, 4 * z + x, 0),
            )

    def scatter(src, dst, stage):
        for dx, dy in NEAR:
            peer = 4 * ((x + dx) % 4) + (y + dy) % 4
            send(
                src.at[peer],
                dst.at[col],
                scatter_send.at[stage],
                scatter_recv.at[stage],
                (z, peer, core),
            )
        start_local(src.at[col], dst.at[col], scatter_recv.at[stage])

    def spread(src, dst, stage):
        for dz in (2, 1, 3):
            send(
                src,
                dst.at[x],
                spread_send.at[stage],
                spread_recv.at[stage],
                ((z + dz) % 4, 4 * z + y, core),
            )
        send_or_keep(
            x == z,
            src,
            dst.at[x],
            spread_self.at[stage],
            spread_recv.at[stage],
            (z, 4 * z + y, core),
        )

    def spread_both(src, dst, stage):
        for dz in (2, 1, 3):
            for to in (other, core):
                send(
                    src,
                    dst.at[core, x],
                    spread_send.at[stage],
                    spread_recv.at[stage],
                    ((z + dz) % 4, 4 * z + y, to),
                )
        send(
            src,
            dst.at[core, x],
            spread_send.at[stage],
            spread_recv.at[stage],
            (z, 4 * z + y, other),
        )
        send_or_keep(
            x == z,
            src,
            dst.at[core, x],
            spread_self.at[stage],
            spread_recv.at[stage],
            (z, 4 * z + y, core),
        )

    def mask(tiles, pattern):
        @pl.loop(0, 5)
        def _(p):
            for a in range(2):
                for b in range(8):
                    here = (p, pl.ds(128 * a, 128), pl.ds(128 * b, 128))
                    keep = jnp.full((128, 128), pattern[p, a, b].astype(F32), F32)
                    tiles[here] = tiles[here] * keep.astype(BF16)

    def columns_of(j):
        return pl.ds(pl.multiple_of(256 * j, 256), 256)

    def block(ref, j):
        return ref[:, columns_of(j)]

    def multiply(values_of, src, dst, stage):
        for dy in (2, 1, 3, 0):
            j = (y + dy) % 4
            values = values_of(j)
            for q in range(4):
                rows = [value[16 * q : 16 * q + 16].astype(BF16) for value in values]
                if len(rows) == 1:
                    src[4 * q + j] = rows[0]
                else:
                    for s in range(2):
                        src[4 * q + j, s] = rows[s]
            for dx in (2, 1, 3, 0):
                peer = 4 * ((x + dx) % 4) + j
                if dx or dy:
                    send(
                        src.at[peer],
                        dst.at[col],
                        scatter_send.at[stage],
                        scatter_recv.at[stage],
                        (z, peer, core),
                    )
                else:
                    start_local(src.at[peer], dst.at[col], scatter_recv.at[stage])

    wait_for(lower, weight_sem.at[1])
    wait_for(lower_pattern, weight_sem.at[8])
    mask(lower, lower_pattern)

    @pl.when(core == 0)
    def _():
        pl.semaphore_wait(ready, 15 + 3)
        pl.semaphore_signal(go, inc=1, device_id=(z, col, 1), device_id_type=MESH)

    @pl.when(core == 1)
    def _():
        pl.semaphore_wait(go, 1)

    bias_here = x == y
    for dq in (2, 1, 3):
        q = (x + dq) % 4
        send(
            bias_pack.at[pl.ds(pl.multiple_of(16 * q, 16), 16)],
            bias_recv.at[y],
            misc_send.at[1],
            misc_recv.at[1],
            (z, 4 * q + x, core),
        )
    own_rows = pl.ds(pl.multiple_of(16 * x, 16), 16)
    send_or_keep(
        bias_here,
        bias_pack.at[own_rows],
        bias_recv.at[y],
        misc_self.at[1],
        misc_recv.at[1],
        (z, 4 * x + x, core),
    )

    @pl.when(core == 0)
    def _():
        for u in range(4):
            wait_for(leaf_relay.at[u], relay_sem.at[u])
            send(leaf_relay.at[u], leaf_recv.at[u], relay_sem.at[4], misc_recv.at[0], (z, col, 1))

    wait_for(leaf_recv, misc_recv.at[0])
    wait_for(lower_inverse, weight_sem.at[0])
    pieces = [leaf_recv[u].astype(F32) for u in range(4)]
    leaves = [
        jnp.concatenate([p[:, 64 * s : 64 * s + 64] for p in pieces], axis=1).astype(BF16)
        for s in range(2)
    ]
    for s in range(2):
        multiply(
            lambda j, s=s: [dot(leaves[s], block(lower_inverse.at[1 + s], j))],
            send1.at[s],
            recv1.at[s],
            12 * s,
        )
    for s in range(2):
        wait_for(recv1.at[s], scatter_recv.at[12 * s])
        leaf_value[s] = add_up(recv1.at[s], 16)
        part1[s] = leaf_value[s].astype(BF16)
        spread(part1.at[s], vec1.at[s], 10 * s)

    wait_for(vec1.at[0], spread_recv.at[0])
    leaf1 = vec1[0].reshape(64, 256)
    for j in range(4):
        top_early[:, 256 * j : 256 * j + 256] = dot(leaf1, block(lower.at[0], j))
    wait_for(vec1.at[1], spread_recv.at[10])
    leaf2 = vec1[1].reshape(64, 256)
    multiply(
        lambda j: [top_early[:, columns_of(j)] + dot(leaf2, block(lower.at[1], j))],
        send2,
        recv2,
        1,
    )
    for j in range(4):
        root_early[:, 256 * j : 256 * j + 256] = dot(leaf1, block(lower.at[3], j)) + dot(
            leaf2, block(lower.at[4], j)
        )
    wait_for(bias_recv, misc_recv.at[1])
    top_bias = jnp.concatenate([bias_recv[u][:, 0:64] for u in range(4)], axis=1)
    wait_for(recv2, scatter_recv.at[1])
    part2[...] = (top_bias - add_up(recv2, 16)).astype(BF16)
    spread(part2, vec2, 1)

    wait_for(vec2, spread_recv.at[1])
    vector = vec2[...].reshape(64, 256)
    vector3 = vector
    multiply(lambda j: [dot(vector3, block(lower_inverse.at[0], j))], send3, recv3, 2)
    wait_for(recv3, scatter_recv.at[2])
    top_value[...] = add_up(recv3, 16)
    part3[...] = top_value[...].astype(BF16)
    spread(part3, vec3, 2)

    wait_for(vec3, spread_recv.at[2])
    vector = vec3[...].reshape(64, 256)
    for dy in (2, 1, 3, 0):
        j = (y + dy) % 4
        value = root_early[:, columns_of(j)] + dot(vector, block(lower.at[2], j))
        for half in range(2):
            for q in range(4):
                send4[half, 4 * q + j] = value[
                    16 * q : 16 * q + 16, 128 * half : 128 * half + 128
                ].astype(BF16)
        for dx in (2, 1, 3, 0):
            peer = 4 * ((x + dx) % 4) + j
            for to in (other, core):
                if dx or dy or to is other:
                    send(
                        send4.at[to, peer],
                        recv4.at[core, col],
                        scatter_send.at[3],
                        scatter_recv.at[3],
                        (z, peer, to),
                    )
                else:
                    start_local(send4.at[to, peer], recv4.at[core, col], scatter_recv.at[3])
    root_bias = jnp.concatenate(
        [bias_recv[2 * core][:, 64:128], bias_recv[2 * core + 1][:, 64:128]], axis=1
    )
    wait_for(upper, weight_sem.at[4])
    wait_for(upper_pattern, weight_sem.at[9])
    mask(upper, upper_pattern)
    wait_for(recv4, scatter_recv.at[3])
    part4[...] = (root_bias - add_up(recv4.at[0], 16) - add_up(recv4.at[1], 16)).astype(BF16)
    spread_both(part4, vec4, 3)

    def whole(ref):
        return jnp.concatenate([ref[0].reshape(64, 128), ref[1].reshape(64, 128)], axis=1)

    def halves(ref, vector, tiles):
        for pair in range(2):
            value = dot(vector, tiles[:, 256 * pair : 256 * pair + 256])
            for k in range(2):
                for q in range(4):
                    ref[4 * q + 2 * pair + k] = value[
                        16 * q : 16 * q + 16, 128 * k : 128 * k + 128
                    ].astype(BF16)

    wait_for(root_lower, weight_sem.at[2])
    wait_for(vec4, spread_recv.at[3])
    halves(send5, whole(vec4), root_lower)
    scatter(send5, recv5, 4)
    wait_for(recv5, scatter_recv.at[4])
    part5[...] = add_up(recv5, 16).astype(BF16)
    spread_both(part5, vec5, 4)
    wait_for(root_upper, weight_sem.at[3])
    wait_for(vec5, spread_recv.at[4])
    halves(send6, whole(vec5), root_upper)
    scatter(send6, recv6, 5)
    wait_for(recv6, scatter_recv.at[5])
    root_out[...] = add_up(recv6, 16)
    part6[...] = root_out[...].astype(BF16)
    spread_both(part6, vec6, 5)

    def out_here(k, to):
        return jnp.logical_and(jnp.logical_and(x == y, 2 * core + k == y), to == core)

    for k in range(2):
        owner = 4 * y + 2 * core + k
        send(root_out, root_out_recv.at[x], misc_send.at[2], misc_recv.at[2], (z, owner, other))
        send_or_keep(
            out_here(k, core),
            root_out,
            root_out_recv.at[x],
            misc_self.at[2 + k],
            misc_recv.at[2],
            (z, owner, core),
        )

    wait_for(vec6, spread_recv.at[5])
    vector = whole(vec6)
    vector7 = vector
    multiply(lambda j: [dot(vector7, block(upper.at[2], j))], send7, recv7, 6)
    for s in range(2):
        for j in range(4):
            second_early[s, :, 256 * j : 256 * j + 256] = dot(vector, block(upper.at[3 + s], j))
    wait_for(recv7, scatter_recv.at[6])
    part7[...] = (top_value[...] - add_up(recv7, 16)).astype(BF16)
    spread(part7, vec7, 6)

    wait_for(upper_inverse, weight_sem.at[5])
    wait_for(vec7, spread_recv.at[6])
    vector = vec7[...].reshape(64, 256)
    vector8 = vector
    multiply(lambda j: [dot(vector8, block(upper_inverse.at[0], j))], send8, recv8, 7)
    wait_for(recv8, scatter_recv.at[7])
    first = add_up(recv8, 16)
    part8[...] = first.astype(BF16)
    spread(part8, vec8, 7)
    first_out[0] = first[:, 0:128]
    first_out[1] = first[:, 128:256]
    first_here = x == y
    for du in (2, 1, 3):
        u = (y + du) % 4
        send(
            first_out.at[u // 2],
            first_out_recv.at[x],
            misc_send.at[3],
            misc_recv.at[3],
            (z, 4 * y + u, core),
        )
    send_or_keep(
        first_here,
        first_out.at[y // 2],
        first_out_recv.at[x],
        misc_self.at[4],
        misc_recv.at[3],
        (z, 4 * y + y, core),
    )

    wait_for(vec8, spread_recv.at[7])
    vector = vec8[...].reshape(64, 256)
    vector9 = vector
    for s in range(2):
        multiply(
            lambda j, s=s: [
                second_early[s, :, columns_of(j)] + dot(vector9, block(upper.at[s], j))
            ],
            send9.at[s],
            recv9.at[s],
            8 + 2 * s,
        )

    odd = y % 2 == 1
    wait_for(root_out_recv, misc_recv.at[2])
    value = root_out_recv[...].reshape(64, 128)
    sol_root[...] = jnp.where(odd, value[:, 64:128], value[:, 0:64])
    wait_for(first_out_recv, misc_recv.at[3])
    value = first_out_recv[...].reshape(64, 128)
    sol_half[0] = jnp.where(odd, value[:, 64:128], value[:, 0:64])

    for s in range(2):
        wait_for(recv9.at[s], scatter_recv.at[8 + 2 * s])
        part9[s] = (leaf_value[s] - add_up(recv9.at[s], 16)).astype(BF16)
        spread(part9.at[s], vec9.at[s], 8 + s)

    for s in range(2):
        wait_for(vec9.at[s], spread_recv.at[8 + s])
        vector = vec9[s].reshape(64, 256)
        for dx in (2, 1, 3, 0):
            j = (x + dx) % 4
            value = dot(vector, block(upper_inverse.at[1 + s], j))
            for u in range(4):
                span = slice(64 * u, 64 * u + 64)
                send10[s, 4 * j + u] = jnp.concatenate(
                    [value[0:32, span], value[32:64, span]], axis=1
                ).astype(BF16)
            for dy in (2, 1, 3, 0):
                peer = 4 * j + (y + dy) % 4
                if dx or dy:
                    send(
                        send10.at[s, peer],
                        recv10.at[s, col],
                        scatter_send.at[9 + 2 * s],
                        scatter_recv.at[9 + 2 * s],
                        (z, peer, core),
                    )
                else:
                    start_local(
                        send10.at[s, peer], recv10.at[s, col], scatter_recv.at[9 + 2 * s]
                    )
    sends = (None, send2, send3, None, send5, send6, send7, send8)
    for stage, ref in enumerate(sends):
        if ref is not None:
            wait_for(ref.at[pl.ds(0, 15)], scatter_send.at[stage])
    wait_for(recv4.at[0], scatter_send.at[3])
    wait_for(recv4.at[1, pl.ds(0, 15)], scatter_send.at[3])
    for s in range(2):
        wait_for(send1.at[s, pl.ds(0, 15)], scatter_send.at[12 * s])
        wait_for(vec1.at[s, pl.ds(0, 3)], spread_send.at[10 * s])
        wait_sent_unless(x == z, vec1.at[s, 0], spread_self.at[10 * s])
        wait_for(send9.at[s, pl.ds(0, 15)], scatter_send.at[8 + 2 * s])
        wait_for(vec9.at[s, pl.ds(0, 3)], spread_send.at[8 + s])
        wait_sent_unless(x == z, vec9.at[s, 0], spread_self.at[8 + s])
    for stage, ref in enumerate((None, vec2, vec3, None, None, None, vec7, vec8)):
        if ref is not None:
            wait_for(ref.at[pl.ds(0, 3)], spread_send.at[stage])
            wait_sent_unless(x == z, ref.at[0], spread_self.at[stage])
    for stage, ref in ((3, vec4), (4, vec5), (5, vec6)):
        wait_for(ref.at[0], spread_send.at[stage])
        wait_for(ref.at[1, pl.ds(0, 3)], spread_send.at[stage])
        wait_sent_unless(x == z, ref.at[0, 0], spread_self.at[stage])
    wait_for(leaf_recv.at[pl.ds(0, 3)], misc_send.at[0])

    @pl.when(core == 0)
    def _():
        wait_for(leaf_recv, relay_sem.at[4])
        wait_sent_unless(leaf_here, leaf_recv.at[0], misc_self.at[0])

    @pl.when(core == 1)
    def _():
        wait_for(leaf_recv.at[0], misc_send.at[0])

    wait_for(bias_recv.at[pl.ds(0, 3)], misc_send.at[1])
    wait_sent_unless(bias_here, bias_recv.at[0], misc_self.at[1])
    wait_for(root_out_recv.at[pl.ds(0, 2)], misc_send.at[2])
    for k in range(2):
        wait_sent_unless(out_here(k, core), root_out_recv.at[0], misc_self.at[2 + k])
    wait_for(first_out_recv.at[pl.ds(0, 3)], misc_send.at[3])
    wait_sent_unless(first_here, first_out_recv.at[0], misc_self.at[4])

    for s in range(2):
        wait_for(recv10.at[s], scatter_recv.at[9 + 2 * s])
        total = add_up(recv10.at[s], 16)
        sol_half[1 + s, 0:32] = total[:, 0:64]
        sol_half[1 + s, 32:64] = total[:, 64:128]
    for s in range(2):
        wait_for(send10.at[s, pl.ds(0, 15)], scatter_send.at[9 + 2 * s])


def per_device(
    rhs_half,
    rhs_root,
    lower_coupling,
    lower_pattern,
    upper_coupling,
    upper_pattern,
    lower_inverse,
    upper_inverse,
    root_lower_inverse,
    root_upper_inverse,
):
    vmem = pl.BlockSpec(memory_space=pltpu.VMEM)
    hbm = pl.BlockSpec(memory_space=pl.ANY)
    one = (16, 256)
    two = (2, 16, 256)
    half = (16, 128)
    stage_chunks = [
        (2, 16) + one,
        (16,) + one,
        (16,) + one,
        (2, 16) + half,
        (16,) + half,
        (16,) + half,
        (16,) + one,
        (16,) + one,
        (2, 16) + one,
        (2, 16, 32, 128),
    ]
    exchange = [pltpu.VMEM(chunk, BF16) for chunk in stage_chunks]
    part_chunks = [two, one, one, half, half, half, one, one, two]
    parts = [pltpu.VMEM(chunk, BF16) for chunk in part_chunks]
    vectors = [
        pltpu.VMEM((2, 4) + chunk if chunk == half else (4,) + chunk, BF16)
        for chunk in part_chunks[1:8]
    ]
    vectors = [pltpu.VMEM((2, 4) + one, BF16), *vectors, pltpu.VMEM((2, 4) + one, BF16)]
    scratch = [
        pltpu.VMEM((3, 64, 64), F32),
        pltpu.VMEM((64, 64), F32),
        pltpu.SMEM((5, 2, 8), jnp.int32),
        pltpu.SMEM((5, 2, 8), jnp.int32),
        pltpu.VMEM((5, 256, 1024), BF16),
        pltpu.VMEM((5, 256, 1024), BF16),
        pltpu.VMEM((3, 256, 1024), BF16),
        pltpu.VMEM((3, 256, 1024), BF16),
        pltpu.VMEM((256, 512), BF16),
        pltpu.VMEM((256, 512), BF16),
        pltpu.VMEM((64, 128), BF16),
        pltpu.VMEM((4, 64, 128), BF16),
        pltpu.VMEM((4, 64, 128), BF16),
        pltpu.VMEM((64, 128), F32),
        pltpu.VMEM((4, 16, 128), F32),
        *exchange,
        *exchange,
        *parts,
        *vectors,
        pltpu.VMEM(two, F32),
        pltpu.VMEM(one, F32),
        pltpu.VMEM((64, 1024), F32),
        pltpu.VMEM((64, 1024), F32),
        pltpu.VMEM((2, 64, 1024), F32),
        pltpu.VMEM(half, F32),
        pltpu.VMEM((4,) + half, F32),
        pltpu.VMEM((2,) + half, F32),
        pltpu.VMEM((4,) + half, F32),
        pltpu.SemaphoreType.DMA((10,)),
        pltpu.SemaphoreType.DMA((13,)),
        pltpu.SemaphoreType.DMA((13,)),
        pltpu.SemaphoreType.DMA((11,)),
        pltpu.SemaphoreType.DMA((11,)),
        pltpu.SemaphoreType.DMA((11,)),
        pltpu.SemaphoreType.DMA((4,)),
        pltpu.SemaphoreType.DMA((4,)),
        pltpu.SemaphoreType.DMA((5,)),
        pltpu.SemaphoreType.DMA((5,)),
        pltpu.SemaphoreType.REGULAR,
        pltpu.SemaphoreType.REGULAR,
    ]
    sol_half, sol_root = pl.pallas_call(
        kernel,
        name="tree_solve",
        out_shape=(pltpu.VMEM((3, 64, 64), F32), pltpu.VMEM((64, 64), F32)),
        in_specs=[hbm] * 10,
        out_specs=(vmem, vmem),
        scratch_shapes=scratch,
        compiler_params=pltpu.CompilerParams(collective_id=0, has_side_effects=True),
    )(
        rhs_half[0],
        rhs_root,
        lower_pattern[0],
        upper_pattern[0],
        lower_coupling[0],
        upper_coupling[0],
        lower_inverse[0],
        upper_inverse[0],
        root_lower_inverse,
        root_upper_inverse,
    )

    def leave(half_ref, root_ref, half_out, root_out, sems):
        first = pltpu.make_async_copy(half_ref, half_out, sems.at[0])
        second = pltpu.make_async_copy(root_ref, root_out, sems.at[1])
        first.start()
        second.start()
        first.wait()
        second.wait()

    sol_half, sol_root = pl.pallas_call(
        leave,
        name="leave",
        out_shape=(
            jax.ShapeDtypeStruct((3, 64, 64), F32),
            jax.ShapeDtypeStruct((64, 64), F32),
        ),
        in_specs=[vmem, vmem],
        out_specs=(hbm, hbm),
        scratch_shapes=[pltpu.SemaphoreType.DMA((2,))],
        compiler_params=pltpu.CompilerParams(vmem_limit_bytes=1 << 20),
    )(sol_half, sol_root)
    return (sol_half[None], sol_root)


def solution(mesh):
    in_specs = (
        P("gz", None, None, ("row", "col")),
        P(None, ("row", "col")),
        P("gz", None, "col", "row"),
        P("gz", None, "col", "row"),
        P("gz", None, "col", "row"),
        P("gz", None, "col", "row"),
        P("gz", None, "col", "row"),
        P("gz", None, "col", "row"),
        P("col", "row"),
        P("col", "row"),
    )
    out_specs = (P("gz", None, None, ("row", "col")), P(None, ("row", "col")))
    return jax.shard_map(
        per_device, mesh=mesh, in_specs=in_specs, out_specs=out_specs, check_vma=False
    )
```
